256 devices in a mesh: dom: 32 (over z_lo, y, x), ch: 8 (over z_hi, core).
Axes of the slice: x: 4, y: 4, z: 8 (z_hi: 4, z_lo: 2; z = z_hi * 2 + z_lo), core: 2. Of those that a mesh axis runs over, the one named last changes fastest.
Arguments:
- node_feats: bfloat16 [512, 24576], P('ch', 'dom'), may hold values from -6 to 6
- edge_feats: bfloat16 [512, 32768], P('ch', 'dom'), may hold values from -6 to 6
- send_rows: int32 [32768], P('dom'), may hold values from 0 to 767
- edge_src: int32 [32768], P('dom'), may hold values from 0 to 1791
- edge_dst: int32 [32768], P('dom'), may hold values from 0 to 767
- w_edge_in: bfloat16 [2, 3, 512, 512], P(None, None, None, 'ch'), may hold values from -0.15625 to 0.15625
- w_edge_out: bfloat16 [2, 512, 512], P(None, 'ch'), may hold values from -0.25 to 0.25
- w_node_in: bfloat16 [2, 2, 512, 512], P(None, None, None, 'ch'), may hold values from -0.1875 to 0.1875
- w_node_out: bfloat16 [2, 512, 512], P(None, 'ch'), may hold values from -0.25 to 0.25
Outputs:
- nodes_out: bfloat16 [512, 24576], P('ch', 'dom')
- edges_out: bfloat16 [512, 32768], P('ch', 'dom')
The draws below stay inside these ranges and needn't reach their ends.
All inputs are finite; a program needn't handle non-finite values.
Results may differ from the reference program's by a relative error of at most 0.0085.
Values may be sent and summed in bfloat16 or wider, within the bound.
No kernel may reach another device: no remote copies, remote signals or barrier semaphores. Data moves between devices by JAX's collectives and lax.ppermute only.
A program may use at most 64 MiB of HBM per device.

```python
import jax
import jax.numpy as jnp
from jax import lax

LATENT = 512
NODE_DEV = 768
EDGE_DEV = 1024
SLOTS = 32
LAYERS = 2
NODES = 24576
EDGES = 32768
EXT = 1792
N_DOM = 32


def touch_ends(result, own_key, least, high):
    longest = result.shape.index(max(result.shape))
    spots = []
    for shift in (0, 1):
        where = [jax.random.randint(jax.random.fold_in(own_key, axis), (), 0, length) for axis, length in enumerate(result.shape)]
        where[longest] = (where[longest] + shift) % result.shape[longest]
        spots.append(tuple(where))
    return result.at[spots[0]].set(least).at[spots[1]].set(high)


def steps_of(stream_key, dims, pieces, low, high):
    loudness, own = 1.0, jax.random.fold_in(stream_key, 6)
    for axis_at, blocks in pieces:
        steps = jnp.exp(jax.random.uniform(jax.random.fold_in(own, axis_at), (blocks,), jnp.float32, low / len(pieces), high / len(pieces)))
        loudness = loudness * jnp.repeat(steps, dims[axis_at] // blocks).reshape([-1 if axis == axis_at else 1 for axis in range(len(dims))])
    return loudness


def gaussian(stream_key, shape, width, bound, cuts=(), held_as=jnp.bfloat16):
    factor_of = steps_of(stream_key, shape, cuts, -0.22, 0.18) if cuts else 1.0
    values = jax.random.normal(stream_key, shape, jnp.float32) * width * factor_of
    return jnp.minimum(jnp.maximum(values, -bound), bound).astype(held_as)


def setup_inputs(seed: int = 0) -> dict:
    seeds = jax.random.split(jax.random.key(seed), 10)
    node_feats = gaussian(seeds[0], (LATENT, NODES), 1.0, 6.0, ((0, 8), (1, 32)))
    edge_feats = gaussian(seeds[1], (LATENT, EDGES), 1.0, 6.0, ((0, 8), (1, 32)))
    send_rows = touch_ends(jax.random.randint(seeds[2], (N_DOM * N_DOM * SLOTS,), 0, NODE_DEV), jax.random.fold_in(seeds[2], 1), 0, NODE_DEV - 1).astype(jnp.int32)
    edge_src = touch_ends(jax.random.randint(seeds[3], (EDGES,), 0, EXT), jax.random.fold_in(seeds[3], 1), 0, EXT - 1).astype(jnp.int32)
    edge_dst = touch_ends(jax.random.randint(seeds[4], (EDGES,), 0, NODE_DEV), jax.random.fold_in(seeds[4], 1), 0, NODE_DEV - 1).astype(jnp.int32)
    w_edge_in = gaussian(seeds[5], (LAYERS, 3, LATENT, LATENT), (3 * LATENT) ** -0.5, 0.15625, ((3, 8),))
    w_edge_out = gaussian(seeds[6], (LAYERS, LATENT, LATENT), LATENT ** -0.5, 0.25, ((1, 8),))
    w_node_in = gaussian(seeds[7], (LAYERS, 2, LATENT, LATENT), (2 * LATENT) ** -0.5, 0.1875, ((3, 8),))
    w_node_out = gaussian(seeds[8], (LAYERS, LATENT, LATENT), LATENT ** -0.5, 0.25, ((1, 8),))
    return dict(node_feats=node_feats, edge_feats=edge_feats, send_rows=send_rows, edge_src=edge_src, edge_dst=edge_dst, w_edge_in=w_edge_in, w_edge_out=w_edge_out, w_node_in=w_node_in, w_node_out=w_node_out)


def layer_norm(values):
    mean = lax.optimization_barrier(jnp.mean(values, axis=0))
    var = lax.optimization_barrier(jnp.mean(values * values, axis=0)) - mean * mean
    return (values - mean) * lax.rsqrt(var + 1e-05)

def reference(node_feats, edge_feats, send_rows, edge_src, edge_dst, w_edge_in, w_edge_out, w_node_in, w_node_out):
    domain = (jnp.arange(EDGES) // EDGE_DEV).astype(jnp.int32)
    remote = edge_src >= NODE_DEV
    offset = jnp.maximum(edge_src - NODE_DEV, 0).astype(jnp.int32)
    source_dom = (offset // SLOTS).astype(jnp.int32)
    slot = (offset % SLOTS).astype(jnp.int32)
    table = send_rows.reshape(N_DOM, N_DOM, SLOTS)
    remote_row = table[source_dom, domain, slot]
    sender = jnp.where(remote, source_dom * NODE_DEV + remote_row, domain * NODE_DEV + edge_src).astype(jnp.int32)
    receiver = (domain * NODE_DEV + edge_dst).astype(jnp.int32)
    nodes = node_feats
    edges = edge_feats
    for layer in range(LAYERS):
        stacked = jnp.stack([edges, nodes[:, sender], nodes[:, receiver]]).astype(jnp.float32)
        hidden = jnp.einsum('ace,ach->he', stacked, w_edge_in[layer].astype(jnp.float32))
        hidden = jax.nn.silu(hidden).astype(jnp.bfloat16)
        message = jnp.einsum('ho,he->oe', w_edge_out[layer].astype(jnp.float32), hidden.astype(jnp.float32))
        edges = (edges.astype(jnp.float32) + layer_norm(message)).astype(jnp.bfloat16)
        gathered = jnp.zeros((LATENT, NODES), jnp.float32).at[:, receiver].add(edges.astype(jnp.float32))
        gathered = gathered.astype(jnp.bfloat16)
        both = jnp.stack([nodes, gathered]).astype(jnp.float32)
        hidden_n = jnp.einsum('acn,ach->hn', both, w_node_in[layer].astype(jnp.float32))
        hidden_n = jax.nn.silu(hidden_n).astype(jnp.bfloat16)
        update = jnp.einsum('ho,hn->on', w_node_out[layer].astype(jnp.float32), hidden_n.astype(jnp.float32))
        nodes = (nodes.astype(jnp.float32) + layer_norm(update)).astype(jnp.bfloat16)
    return (nodes, edges)
```

```python
import jax
import jax.numpy as jnp
from jax import lax
from jax.sharding import PartitionSpec as P

LATENT = 512
SLOTS = 32
LAYERS = 2
BF = jnp.bfloat16
F32 = jnp.float32

CORE = [(c, c ^ 1) for c in range(8)]
Z_GROUPS = [[k, 2 + k, 4 + k, 6 + k] for k in (0, 1)]
XY_GROUPS = [[16 * z + i for i in range(16)] for z in (0, 1)]


def z_shift(s):
    return [(c, ((c // 2 + s) % 4) * 2 + c % 2) for c in range(8)]


def swap(x):
    return lax.ppermute(x, "ch", CORE)


def z_gather(x, zi):
    prev = lax.ppermute(x, "ch", z_shift(1))
    nxt = lax.ppermute(x, "ch", z_shift(3))
    far_a = lax.ppermute(prev[:32], "ch", z_shift(1))
    far_b = lax.ppermute(nxt[32:], "ch", z_shift(3))
    far = jnp.concatenate([far_a, far_b])
    rel = jnp.stack([x, nxt, far, prev])
    return lax.dynamic_slice_in_dim(jnp.concatenate([rel, rel]), (4 - zi) % 4, 4, 0)


def interleave(own, other, k):
    even = jnp.where(k == 0, own, other)
    odd = jnp.where(k == 0, other, own)
    return jnp.stack([even, odd], axis=1).reshape(LATENT, own.shape[-1])


def dot(a, b, ca, cb):
    return lax.dot_general(a, b, (((ca,), (cb,)), ((), ())), preferred_element_type=F32)


def norm_add(msg, residual):
    mean = jnp.mean(msg, axis=0, keepdims=True)
    var = jnp.mean(msg * msg, axis=0, keepdims=True) - mean * mean
    return (residual.astype(F32) + (msg - mean) * lax.rsqrt(var + 1e-05)).astype(BF)


def one_hot(idx, n):
    return (lax.broadcasted_iota(jnp.int32, (n, idx.shape[0]), 0) == idx[None, :]).astype(BF)


def weight_rows(w_in, w_out):
    blocks = w_in.shape[0]
    return [w_in[b].T for b in range(blocks)] + [w_out]


def shards(node_feats, edge_feats, send_rows, edge_src, edge_dst, w_edge_in, w_edge_out, w_node_in, w_node_out):
    d = lax.axis_index("dom")
    c = lax.axis_index("ch")
    j = d % 16
    zi = c // 2
    k = c % 2
    n_nodes = node_feats.shape[1]
    n_edges = edge_feats.shape[1]

    v_half = z_gather(node_feats, zi)
    v_own = v_half.reshape(256, n_nodes)
    a_rows = [jnp.concatenate(weight_rows(w_edge_in[layer], w_edge_out[layer])) for layer in range(LAYERS)]
    a_mine = [lax.dynamic_slice_in_dim(r, j * 16, 16, 0) for r in a_rows]
    n_mats = jnp.stack([jnp.stack(weight_rows(w_node_in[layer], w_node_out[layer])) for layer in range(LAYERS)])
    n_mine = lax.dynamic_slice(n_mats, (j // 8, 0, (j % 8) * 8, 0), (1, 3, 8, LATENT)).reshape(24, LATENT)
    mine = jnp.concatenate(a_mine + [n_mine])
    mine = lax.all_to_all(jnp.broadcast_to(mine[None], (4,) + mine.shape), "ch", 0, 0, axis_index_groups=Z_GROUPS, tiled=True)

    def spread(x):
        return lax.all_to_all(
            jnp.broadcast_to(x[None], (16,) + x.shape), "dom", 0, 0, axis_index_groups=XY_GROUPS, tiled=True
        )

    edge_w = []
    for layer in range(LAYERS):
        edge_w.append(spread(mine[:, layer * 16 : layer * 16 + 16]).reshape(4, 256, LATENT))
    node_all = spread(mine[:, 32:56]).reshape(2, 8, 4, 3, 8, LATENT)
    node_w = [[node_all[layer, :, :, m].reshape(256, LATENT) for m in range(3)] for layer in range(LAYERS)]

    oh_send = one_hot(send_rows, n_nodes)
    oh_src = one_hot(edge_src, n_nodes + n_edges)
    oh_dst = one_hot(edge_dst, n_nodes)

    def halo(x):
        rows = dot(oh_send, x, 0, 1).astype(BF)
        return lax.all_to_all(rows, "dom", 0, 0, tiled=True)

    halo_own = halo(v_own)
    v_other = swap(v_half)
    e_half = z_gather(edge_feats, zi)
    e_other = swap(e_half)
    halo_other = swap(halo_own)
    nodes = interleave(v_half, v_other, k)
    edges = interleave(e_half, e_other, k)
    halo_t = interleave(
        halo_own.T.reshape(4, 64, -1), halo_other.T.reshape(4, 64, -1), k
    )

    for layer in range(LAYERS):
        w_e, w_s, w_r, w_o = (edge_w[layer][m] for m in range(4))
        sender = dot(w_s, nodes, 1, 0).astype(BF)
        if layer == 0:
            far = dot(w_s, halo_t, 1, 0).astype(BF)
            far_part = dot(far, oh_src[n_nodes:], 1, 0)
        else:
            far_part = dot(halo(sender), oh_src[n_nodes:], 0, 0)
        receiver = dot(w_r, nodes, 1, 0).astype(BF)
        pre = dot(w_e, edges, 1, 0) + dot(sender, oh_src[:n_nodes], 1, 0) + far_part + dot(receiver, oh_dst, 1, 0)
        hidden = jax.nn.silu(pre).astype(BF)
        msg = dot(w_o, hidden, 0, 0) + dot(swap(w_o), swap(hidden), 0, 0)
        edges = norm_add(msg, edges)
        agg = dot(edges, oh_dst, 1, 1).astype(BF)
        n_v, n_a, n_o = node_w[layer]
        hidden_n = jax.nn.silu(dot(n_v, nodes, 1, 0) + dot(n_a, agg, 1, 0)).astype(BF)
        msg_n = dot(n_o, hidden_n, 0, 0) + dot(swap(n_o), swap(hidden_n), 0, 0)
        nodes = norm_add(msg_n, nodes)
    return (
        lax.dynamic_slice_in_dim(nodes, c * 64, 64, 0),
        lax.dynamic_slice_in_dim(edges, c * 64, 64, 0),
    )


def solution(mesh):
    in_specs = (
        P("ch", "dom"),
        P("ch", "dom"),
        P("dom"),
        P("dom"),
        P("dom"),
        P(None, None, None, "ch"),
        P(None, "ch", None),
        P(None, None, None, "ch"),
        P(None, "ch", None),
    )
    out_specs = (P("ch", "dom"), P("ch", "dom"))
    return jax.shard_map(shards, mesh=mesh, in_specs=in_specs, out_specs=out_specs, check_vma=False)
```

```python
import jax
import jax.numpy as jnp
from jax import lax
from jax.sharding import PartitionSpec as P

LATENT = 512
SLOTS = 32
LAYERS = 2
BF = jnp.bfloat16
F32 = jnp.float32

CORE = [(c, c ^ 1) for c in range(8)]


def z_shift(s):
    return [(c, ((c // 2 + s) % 4) * 2 + c % 2) for c in range(8)]


def ring(stage, s):
    pairs = []
    for d in range(32):
        along_x = (d // 4) * 4 + (d + s) % 4
        along_y = (d // 16) * 16 + (d + 4 * s) % 16
        for c in range(8):
            to = along_y if (c % 2 == 0) == (stage == 1) else along_x
            pairs.append((d * 8 + c, to * 8 + c))
    return pairs


def swap(x):
    return lax.ppermute(x, "ch", CORE)


def settle(parts, me):
    rel = jnp.stack(parts)
    return jnp.concatenate([lax.dynamic_slice_in_dim(rel, (i - me) & 3, 1, 0) for i in range(4)])


def z_gather(x, zi):
    prev = lax.ppermute(x, "ch", z_shift(1))
    nxt = lax.ppermute(x, "ch", z_shift(3))
    far_a = lax.ppermute(prev[:32], "ch", z_shift(1))
    far_b = lax.ppermute(nxt[32:], "ch", z_shift(3))
    far = jnp.concatenate([far_a, far_b])
    return settle([x, nxt, far, prev], zi)


def interleave(own, other, k):
    even = jnp.where(k == 0, own, other)
    odd = jnp.where(k == 0, other, own)
    return jnp.stack([even, odd], axis=1).reshape(LATENT, own.shape[-1])


def dot(a, b, ca, cb):
    return lax.dot_general(a, b, (((ca,), (cb,)), ((), ())), preferred_element_type=F32)


def norm_add(msg, residual):
    mean = jnp.mean(msg, axis=0, keepdims=True)
    var = jnp.mean(msg * msg, axis=0, keepdims=True) - mean * mean
    return (residual.astype(F32) + (msg - mean) * lax.rsqrt(var + 1e-05)).astype(BF)


def one_hot(idx, n):
    return (lax.broadcasted_iota(jnp.int32, (n, idx.shape[0]), 0) == idx[None, :]).astype(BF)


def shards(node_feats, edge_feats, send_rows, edge_src, edge_dst, w_edge_in, w_edge_out, w_node_in, w_node_out):
    d = lax.axis_index("dom")
    c = lax.axis_index("ch")
    j = d % 16
    zi = c // 2
    k = c % 2
    n_nodes = node_feats.shape[1]
    n_edges = edge_feats.shape[1]

    v_half = z_gather(node_feats, zi)
    v_own = v_half.reshape(256, n_nodes)
    y, x = j // 4, j % 4
    first = jnp.where(k == 0, y, x)
    second = jnp.where(k == 0, x, y)
    lay = first // 2
    row = 8 * ((first % 2) * 4 + second)

    def cut(w):
        return lax.dynamic_slice(w, (lay, 0, row, 0), (1, w.shape[1], 8, LATENT))[0]

    piece = jnp.concatenate(
        [cut(jnp.swapaxes(w_edge_in, 2, 3)), cut(w_edge_out[:, None]), cut(jnp.swapaxes(w_node_in, 2, 3)), cut(w_node_out[:, None])]
    )
    wz = jnp.stack([piece] + [lax.ppermute(piece, "ch", z_shift(s)) for s in (1, 3, 2)])
    one = [wz] + [lax.ppermute(wz, ("dom", "ch"), ring(1, s)) for s in (3, 2, 1)]
    one = settle(one, first)
    prev = lax.ppermute(one, ("dom", "ch"), ring(2, 1))
    nxt = lax.ppermute(one, ("dom", "ch"), ring(2, 3))
    far_a = lax.ppermute(prev[:2], ("dom", "ch"), ring(2, 1))
    far_b = lax.ppermute(nxt[2:], ("dom", "ch"), ring(2, 3))
    edge_w, node_w = [], []
    for layer in range(LAYERS):
        part = slice(2 * layer, 2 * layer + 2)
        quarters = settle([one[part], nxt[part], (far_a, far_b)[layer], prev[part]], second)
        mats = [quarters[:, :, :, m].reshape(256, LATENT) for m in range(7)]
        edge_w.append(mats[:4])
        node_w.append(mats[4:])

    oh_send = one_hot(send_rows, n_nodes)
    oh_src = one_hot(edge_src, n_nodes + n_edges)
    oh_dst = one_hot(edge_dst, n_nodes)

    def halo(x):
        rows = dot(oh_send, x, 0, 1).astype(BF)
        return lax.all_to_all(rows, "dom", 0, 0, tiled=True)

    halo_own = halo(v_own)
    v_other = swap(v_half)
    e_half = z_gather(lax.optimization_barrier((edge_feats, wz))[0], zi)
    e_other = swap(e_half)
    halo_other = swap(halo_own)
    nodes = interleave(v_half, v_other, k)
    edges = interleave(e_half, e_other, k)
    halo_t = interleave(
        halo_own.T.reshape(4, 64, -1), halo_other.T.reshape(4, 64, -1), k
    )

    for layer in range(LAYERS):
        w_e, w_s, w_r, w_o = (edge_w[layer][m] for m in range(4))
        sender = dot(w_s, nodes, 1, 0).astype(BF)
        if layer == 0:
            far = dot(w_s, halo_t, 1, 0).astype(BF)
            far_part = dot(far, oh_src[n_nodes:], 1, 0)
        else:
            far_part = dot(halo(sender), oh_src[n_nodes:], 0, 0)
        receiver = dot(w_r, nodes, 1, 0).astype(BF)
        pre = dot(w_e, edges, 1, 0) + dot(sender, oh_src[:n_nodes], 1, 0) + far_part + dot(receiver, oh_dst, 1, 0)
        hidden = jax.nn.silu(pre).astype(BF)
        msg = dot(w_o, hidden, 0, 0) + dot(swap(w_o), swap(hidden), 0, 0)
        edges = norm_add(msg, edges)
        agg = dot(edges, oh_dst, 1, 1).astype(BF)
        n_v, n_a, n_o = node_w[layer]
        hidden_n = jax.nn.silu(dot(n_v, nodes, 1, 0) + dot(n_a, agg, 1, 0)).astype(BF)
        msg_n = dot(n_o, hidden_n, 0, 0) + dot(swap(n_o), swap(hidden_n), 0, 0)
        nodes = norm_add(msg_n, nodes)
    return (
        lax.dynamic_slice_in_dim(nodes, c * 64, 64, 0),
        lax.dynamic_slice_in_dim(edges, c * 64, 64, 0),
    )


def solution(mesh):
    in_specs = (
        P("ch", "dom"),
        P("ch", "dom"),
        P("dom"),
        P("dom"),
        P("dom"),
        P(None, None, None, "ch"),
        P(None, "ch", None),
        P(None, None, None, "ch"),
        P(None, "ch", None),
    )
    out_specs = (P("ch", "dom"), P("ch", "dom"))
    return jax.shard_map(shards, mesh=mesh, in_specs=in_specs, out_specs=out_specs, check_vma=False)
```

```python
import jax
import jax.numpy as jnp
from jax import lax
from jax.experimental import pallas as pl
from jax.experimental.pallas import tpu as pltpu
from jax.sharding import PartitionSpec as P

LATENT = 512
HALF = 256
SLOTS = 32
CHUNK = 256
BF = jnp.bfloat16
F32 = jnp.float32

CORE = [(c, c ^ 1) for c in range(8)]
VMEM = pl.BlockSpec(memory_space=pltpu.VMEM)
SMEM = pl.BlockSpec(memory_space=pltpu.SMEM)


def z_shift(s):
    return [(c, ((c // 2 + s) % 4) * 2 + c % 2) for c in range(8)]


def ring(stage, s):
    pairs = []
    for d in range(32):
        along_x = (d // 4) * 4 + (d + s) % 4
        along_y = (d // 16) * 16 + (d + 4 * s) % 16
        for c in range(8):
            to = along_y if (c % 2 == 0) == (stage == 1) else along_x
            pairs.append((d * 8 + c, to * 8 + c))
    return pairs


def swap(x):
    return lax.ppermute(x, "ch", CORE)


def ring_gather(x, axis, perm):
    half = x.shape[0] // 2
    prev = lax.ppermute(x, axis, perm(1))
    nxt = lax.ppermute(x, axis, perm(3))
    far_a = lax.ppermute(prev[:half], axis, perm(1))
    far_b = lax.ppermute(nxt[half:], axis, perm(3))
    return x, nxt, far_a, far_b, prev


def dot(a, b, ca=1, cb=0):
    return lax.dot_general(a, b, (((ca,), (cb,)), ((), ())), preferred_element_type=F32)


def norm_add(msg, residual):
    mean = jnp.sum(msg, axis=0, keepdims=True) / LATENT
    var = jnp.sum(msg * msg, axis=0, keepdims=True) / LATENT - mean * mean
    return (residual.astype(F32) + (msg - mean) * lax.rsqrt(var + 1e-05)).astype(BF)


def silu(x):
    return (x * jax.nn.sigmoid(x)).astype(BF)


def hot(idx, first, rows):
    where = lax.broadcasted_iota(jnp.int32, (rows, idx.shape[1]), 0) + first == idx
    return jnp.where(where, 1.0, 0.0).astype(BF)


def chunks(n, body):
    def step(i, carry):
        body(pl.ds(pl.multiple_of(i * CHUNK, CHUNK), CHUNK), i * CHUNK)
        return carry

    lax.fori_loop(0, n // CHUNK, step, 0)


def call(kernel, outs, *args, scratch=(), flops=0):
    specs = [SMEM] + [VMEM] * (len(args) - 1)
    moved = sum(a.size * a.dtype.itemsize for a in args)
    return pl.pallas_call(
        kernel,
        out_shape=[jax.ShapeDtypeStruct(s, d) for s, d in outs],
        in_specs=specs,
        out_specs=[VMEM] * len(outs),
        scratch_shapes=list(scratch),
        cost_estimate=pl.CostEstimate(flops=flops, bytes_accessed=moved, transcendentals=0),
    )(*args)


def place_half(meta, parts, out):
    own, nxt, far_a, far_b, prev = parts
    zi = meta[0]
    at = lambda s: pl.multiple_of(((zi + s) & 3) * 64, 64)
    n = out.shape[1]
    out[pl.ds(at(0), 64), :] = own[:, :n]
    out[pl.ds(at(1), 64), :] = nxt[:, :n]
    out[pl.ds(at(2), 32), :] = far_a[:, :n]
    out[pl.ds(at(2) + 32, 32), :] = far_b[:, :n]
    out[pl.ds(at(3), 64), :] = prev[:, :n]


def select_rows(send, x, rows):
    def body(sl, _):
        rows[sl, :] = dot(x, hot(send[:, sl], 0, x.shape[1])).T.astype(BF)

    chunks(rows.shape[0], body)


def send_first(meta, own, nxt, far_a, far_b, prev, send, half, rows):
    place_half(meta, (own, nxt, far_a, far_b, prev), half)
    select_rows(send, half[...], rows)


def gather_edges(meta, own, nxt, far_a, far_b, prev, half):
    place_half(meta, (own, nxt, far_a, far_b, prev), half)


def split_layers(meta, own, nxt, far, prev, one, two):
    for s, part in enumerate((own, nxt, far, prev)):
        a = (meta[1] + s) & 3

        @pl.when(a < 2)
        def _():
            one[a] = part[...]

        @pl.when(a >= 2)
        def _():
            two[a - 2] = part[...]


def unpack(meta, own, nxt, far_a, far_b, prev, mats, outs):
    def rows_of(ref, a, m):
        return ref[a, :, m].astype(F32).reshape(32, LATENT)

    pieces = ((own, own), (nxt, nxt), (far_a, far_b), (prev, prev))
    for m in range(7):
        for s in range(4):
            at = pl.multiple_of(((meta[2] + s) & 3) * 64, 64)
            for a in range(2):
                ref = pieces[s][a]
                rows = rows_of(ref, a if ref.shape[0] == 2 else 0, m)
                mats[m, pl.ds(at + 32 * a, 32), :] = rows.astype(BF)
    outs[0] = mats[3].astype(F32).T.astype(BF)
    outs[1] = mats[6].astype(F32).T.astype(BF)


def interleave(meta, own, other, out):
    for z in range(4):
        out[pl.ds(pl.multiple_of(z * 128 + meta[3] * 64, 64), 64), :] = own[z * 64 : z * 64 + 64]
        out[pl.ds(pl.multiple_of(z * 128 + 64 - meta[3] * 64, 64), 64), :] = other[z * 64 : z * 64 + 64]


def edge_first(meta, v_own, v_other, e_own, e_other, h_own, h_other, mats, src, dst, v_all, e_all, hidden, sender, receiver, halo):
    n = v_all.shape[1]
    interleave(meta, v_own, v_other, v_all)
    interleave(meta, e_own, e_other, e_all)
    swapped = meta[3] == 1
    low = lax.broadcasted_iota(jnp.int32, (halo.shape[0], 128), 1) < 64
    for b in range(2):
        blk = slice(128 * b, 128 * b + 128)
        own, other = h_own[:, blk].astype(F32), h_other[:, blk].astype(F32)
        even = jnp.where(swapped, other, own)
        odd = jnp.where(swapped, own, other)
        halo[:, 256 * b : 256 * b + 128] = jnp.where(low, even, pltpu.roll(odd, 64, 1)).astype(BF)
        halo[:, 256 * b + 128 : 256 * b + 256] = jnp.where(low, pltpu.roll(even, 64, 1), odd).astype(BF)
    sender[:, :n] = dot(mats[1], v_all[...]).astype(BF)
    sender[:, n:] = dot(mats[1], halo[...], 1, 1).astype(BF)
    receiver[...] = dot(mats[2], v_all[...]).astype(BF)

    def body(sl, _):
        pre = dot(mats[0], e_all[:, sl])
        pre += dot(sender[...], hot(src[:, sl], 0, sender.shape[1]))
        pre += dot(receiver[...], hot(dst[:, sl], 0, n))
        hidden[:, sl] = silu(pre)

    chunks(hidden.shape[1], body)


def aggregate(meta, hid, hid_other, turned, turned_other, mats, e_all, v_all, dst, e_new, hidden):
    def edges(sl, _):
        msg = dot(turned[0], hid[:, sl]) + dot(turned_other[0], hid_other[:, sl])
        e_new[:, sl] = norm_add(msg, e_all[:, sl])

    chunks(e_new.shape[1], edges)

    def nodes(sl, first):
        agg = dot(e_new[...], hot(dst[...], first, CHUNK), 1, 1).astype(BF)
        hidden[:, sl] = silu(dot(mats[4], v_all[:, sl]) + dot(mats[5], agg))

    chunks(hidden.shape[1], nodes)


def aggregate_last(meta, hid, hid_other, turned, turned_other, mats, e_all, v_all, dst, e_out, hidden, e_new):
    aggregate(meta, hid, hid_other, turned, turned_other, mats, e_all, v_all, dst, e_new, hidden)
    e_out[...] = e_new[pl.ds(pl.multiple_of(meta[4] * 64, 64), 64), :]


def node_norm(hid, hid_other, turned, turned_other, v_all, v_new):
    def nodes(sl, _):
        msg = dot(turned[1], hid[:, sl]) + dot(turned_other[1], hid_other[:, sl])
        v_new[:, sl] = norm_add(msg, v_all[:, sl])

    chunks(v_new.shape[1], nodes)


def send_next(meta, hid, hid_other, turned, turned_other, v_all, mats, send, v_new, sender, rows):
    node_norm(hid, hid_other, turned, turned_other, v_all, v_new)
    sender[...] = dot(mats[1], v_new[...]).astype(BF)
    select_rows(send, sender[...], rows)


def edge_local(meta, v_all, e_all, sender, mats, src, dst, part, receiver):
    n = v_all.shape[1]
    receiver[...] = dot(mats[2], v_all[...]).astype(BF)

    def body(sl, _):
        pre = dot(mats[0], e_all[:, sl])
        pre += dot(sender[...], hot(src[:, sl], 0, n))
        part[:, sl] = pre + dot(receiver[...], hot(dst[:, sl], 0, n))

    chunks(part.shape[1], body)


def edge_far(n, meta, part, rows, src, hidden, far):
    far[...] = rows[...].astype(F32).T.astype(BF)

    def body(sl, _):
        hidden[:, sl] = silu(part[:, sl] + dot(far[...], hot(src[:, sl], n, far.shape[1])))

    chunks(hidden.shape[1], body)


def finish(meta, hid, hid_other, turned, turned_other, v_all, v_out, v_new):
    node_norm(hid, hid_other, turned, turned_other, v_all, v_new)
    v_out[...] = v_new[pl.ds(pl.multiple_of(meta[4] * 64, 64), 64), :]


def shards(node_feats, edge_feats, send_rows, edge_src, edge_dst, w_edge_in, w_edge_out, w_node_in, w_node_out):
    d = lax.axis_index("dom")
    c = lax.axis_index("ch")
    k = c & 1
    y, x = (d >> 2) & 3, d & 3
    n = node_feats.shape[1]
    m = edge_feats.shape[1]
    first = jnp.where(k == 0, y, x)
    second = jnp.where(k == 0, x, y)
    meta = jnp.stack([c >> 1, first, second, k, c]).astype(jnp.int32)
    send, src, dst = (a.reshape(1, -1) for a in (send_rows, edge_src, edge_dst))

    row = 8 * ((first & 1) * 4 + second)

    def cut(w):
        return lax.dynamic_slice(w, (first >> 1, 0, row, 0), (1, w.shape[1], 8, LATENT)).reshape(-1, LATENT)

    piece = [cut(jnp.swapaxes(w_edge_in, 2, 3)), cut(w_edge_out[:, None]), cut(jnp.swapaxes(w_node_in, 2, 3)), cut(w_node_out[:, None])]
    piece = jnp.concatenate(piece + [piece[-1]])
    v_parts = ring_gather(jnp.concatenate([node_feats, piece], axis=1), "ch", z_shift)
    e_parts = ring_gather(lax.optimization_barrier((edge_feats, v_parts[1], v_parts[4]))[0], "ch", z_shift)

    own, nxt, far_a, far_b, prev = (p[:, n:] for p in v_parts)
    wz = jnp.stack([own, nxt, jnp.concatenate([far_a, far_b]), prev])[:, :56].reshape(4, 7, 8, LATENT)
    w_parts = [wz] + [lax.ppermute(wz, ("dom", "ch"), ring(1, s)) for s in (3, 2, 1)]
    layers = call(split_layers, [((2, 4, 7, 8, LATENT), BF)] * 2, meta, *w_parts)

    v_half, rows = call(
        send_first, [((HALF, n), BF), ((m, HALF), BF)], meta, *v_parts, send, flops=2 * HALF * n * m
    )

    def exchange(rows):
        return lax.all_to_all(rows.reshape(32, SLOTS, HALF), "dom", 0, 0, tiled=True).reshape(-1, HALF)

    halo = exchange(rows)
    v_other = swap(v_half)
    (e_half,) = call(gather_edges, [((HALF, m), BF)], meta, *e_parts)
    e_other = swap(e_half)
    halo_other = swap(halo)

    mats, turned, turned_other = [], [], []
    for layer in range(2):
        parts = ring_gather(layers[layer], ("dom", "ch"), lambda s: ring(2, s))
        w, t = call(unpack_call, [((7, HALF, LATENT), BF), ((2, LATENT, HALF), BF)], meta, *parts)
        mats.append(w)
        turned.append(t)
        turned_other.append(swap(t))

    big = lambda r, q: 2 * r * q * LATENT
    v_all, e_all, hid = call(
        edge_first,
        [((LATENT, n), BF), ((LATENT, m), BF), ((HALF, m), BF)],
        meta, v_half, v_other, e_half, e_other, halo, halo_other, mats[0], src, dst,
        scratch=[pltpu.VMEM((HALF, n + m), BF), pltpu.VMEM((HALF, n), BF), pltpu.VMEM((m, LATENT), BF)],
        flops=4 * big(HALF, n + m),
    )
    e_new, hid_n = call(
        aggregate,
        [((LATENT, m), BF), ((HALF, n), BF)],
        meta, hid, swap(hid), turned[0], turned_other[0], mats[0], e_all, v_all, dst,
        flops=3 * big(LATENT, m),
    )
    v_new, sender, rows = call(
        send_next,
        [((LATENT, n), BF), ((HALF, n), BF), ((m, HALF), BF)],
        meta, hid_n, swap(hid_n), turned[0], turned_other[0], v_all, mats[1], send,
        flops=2 * big(LATENT, n),
    )
    far = exchange(rows)
    (part,) = call(
        edge_local, [((HALF, m), F32)], meta, v_new, e_new, sender, mats[1], src, dst,
        scratch=[pltpu.VMEM((HALF, n), BF)], flops=3 * big(HALF, m),
    )
    (hid,) = call(
        lambda *refs: edge_far(n, *refs), [((HALF, m), BF)], meta, part, far, src,
        scratch=[pltpu.VMEM((HALF, m), BF)], flops=2 * big(HALF, m),
    )
    e_out, hid_n = call(
        aggregate_last,
        [((64, m), BF), ((HALF, n), BF)],
        meta, hid, swap(hid), turned[1], turned_other[1], mats[1], e_new, v_new, dst,
        scratch=[pltpu.VMEM((LATENT, m), BF)], flops=3 * big(LATENT, m),
    )
    (v_out,) = call(
        finish, [((64, n), BF)], meta, hid_n, swap(hid_n), turned[1], turned_other[1], v_new,
        scratch=[pltpu.VMEM((LATENT, n), BF)], flops=big(LATENT, n),
    )
    return v_out, e_out


def unpack_call(meta, own, nxt, far_a, far_b, prev, mats, turned):
    unpack(meta, own, nxt, far_a, far_b, prev, mats, turned)


def solution(mesh):
    in_specs = (
        P("ch", "dom"),
        P("ch", "dom"),
        P("dom"),
        P("dom"),
        P("dom"),
        P(None, None, None, "ch"),
        P(None, "ch", None),
        P(None, None, None, "ch"),
        P(None, "ch", None),
    )
    out_specs = (P("ch", "dom"), P("ch", "dom"))
    return jax.shard_map(shards, mesh=mesh, in_specs=in_specs, out_specs=out_specs, check_vma=False)
```

```python
import functools

import jax
import jax.numpy as jnp
from jax import lax
from jax.experimental import pallas as pl
from jax.experimental.pallas import tpu as pltpu
from jax.sharding import PartitionSpec as P

LATENT = 512
HALF = 256
SLOTS = 32
CHUNK = 256
BF = jnp.bfloat16
F32 = jnp.float32

CORE = [(c, c ^ 1) for c in range(8)]
VMEM = pl.BlockSpec(memory_space=pltpu.VMEM)
SMEM = pl.BlockSpec(memory_space=pltpu.SMEM)


def z_shift(s):
    return [(c, ((c // 2 + s) % 4) * 2 + c % 2) for c in range(8)]


def ring(stage, s):
    pairs = []
    for d in range(32):
        along_x = (d // 4) * 4 + (d + s) % 4
        along_y = (d // 16) * 16 + (d + 4 * s) % 16
        for c in range(8):
            to = along_y if (c % 2 == 0) == (stage == 1) else along_x
            pairs.append((d * 8 + c, to * 8 + c))
    return pairs


def swap(x):
    return lax.ppermute(x, "ch", CORE)


def ring_gather(x, axis, perm):
    half = x.shape[0] // 2
    prev = lax.ppermute(x, axis, perm(1))
    nxt = lax.ppermute(x, axis, perm(3))
    far_a = lax.ppermute(prev[:half], axis, perm(1))
    far_b = lax.ppermute(nxt[half:], axis, perm(3))
    return x, nxt, far_a, far_b, prev


def dot(a, b, ca=1, cb=0):
    return lax.dot_general(a, b, (((ca,), (cb,)), ((), ())), preferred_element_type=F32)


def norm_add(msg, residual):
    mean = jnp.sum(msg, axis=0, keepdims=True) / LATENT
    var = jnp.sum(msg * msg, axis=0, keepdims=True) / LATENT - mean * mean
    return (residual.astype(F32) + (msg - mean) * lax.rsqrt(var + 1e-05)).astype(BF)


def silu(x):
    return (x * jax.nn.sigmoid(x)).astype(BF)


def hot(idx, first, rows):
    where = lax.broadcasted_iota(jnp.int32, (rows, idx.shape[1]), 0) + first == idx
    return jnp.where(where, 1.0, 0.0).astype(BF)


def chunks(n, body):
    def step(i, carry):
        body(pl.ds(pl.multiple_of(i * CHUNK, CHUNK), CHUNK), i * CHUNK)
        return carry

    lax.fori_loop(0, n // CHUNK, step, 0)


def call(kernel, outs, *args, scratch=(), flops=0, space=VMEM):
    specs = [SMEM] + [space] * (len(args) - 1)
    moved = sum(a.size * a.dtype.itemsize for a in args)
    return pl.pallas_call(
        kernel,
        out_shape=[jax.ShapeDtypeStruct(s, d) for s, d in outs],
        in_specs=specs,
        out_specs=[VMEM] * len(outs),
        scratch_shapes=list(scratch),
        compiler_params=pltpu.CompilerParams(vmem_limit_bytes=6 << 20),
        cost_estimate=pl.CostEstimate(flops=flops, bytes_accessed=moved, transcendentals=0),
    )(*args)


def place_half(meta, parts, out, col):
    own, nxt, far_a, far_b, prev = parts
    zi = meta[0]
    at = lambda s: pl.multiple_of(((zi + s) & 3) * 64, 64)
    cols = slice(col, col + out.shape[1])
    out[pl.ds(at(0), 64), :] = own[:, cols]
    out[pl.ds(at(1), 64), :] = nxt[:, cols]
    out[pl.ds(at(2), 32), :] = far_a[:, cols]
    out[pl.ds(at(2) + 32, 32), :] = far_b[:, cols]
    out[pl.ds(at(3), 64), :] = prev[:, cols]


def select_rows(send, x, rows):
    def body(sl, _):
        rows[sl, :] = dot(x, hot(send[:, sl], 0, x.shape[1])).T.astype(BF)

    chunks(rows.shape[0], body)


def send_first(meta, own, nxt, far_a, far_b, prev, send, half, rows):
    place_half(meta, (own, nxt, far_a, far_b, prev), half, 0)
    select_rows(send, half[...], rows)


def gather_edges(meta, own, nxt, far_a, far_b, prev, half):
    place_half(meta, (own, nxt, far_a, far_b, prev), half, own.shape[1] - half.shape[1])


def copy_all(copies, sem):
    copies = [pltpu.make_async_copy(a, b, sem.at[i]) for i, (a, b) in enumerate(copies)]
    for copy in copies:
        copy.start()
    for copy in copies:
        copy.wait()


def cut_weights(meta, w_e, w_eo, w_n, w_no, piece, sem):
    lay = meta[1] >> 1
    rows = pl.ds(pl.multiple_of(8 * ((meta[1] & 1) * 4 + meta[2]), 8), 8)
    copies = [
        (w_e.at[lay, :, rows], piece.at[0:3]),
        (w_eo.at[lay, rows], piece.at[3]),
        (w_n.at[lay, :, rows], piece.at[4:6]),
        (w_no.at[lay, rows], piece.at[6]),
    ]
    copy_all(copies, sem)


def beside(meta, v, e, piece, both, sem):
    n = v.shape[1]
    copy_all([(v, both.at[:, :n]), (e, both.at[:, n:])], sem)


def unpack(layer, meta, own, nxt, far_a, far_b, prev, mats, turned):
    for s in range(4):
        for r in range(4):
            a = (meta[1] + r) & 3
            at = pl.multiple_of((((meta[2] + s) & 3) * 2 + (a & 1)) * 32, 32)
            ref, row = ((own, r), (nxt, r), (far_a, r) if r < 2 else (far_b, r - 2), (prev, r))[s]

            @pl.when((a >> 1) == layer)
            def _():
                for m in range(7):
                    mats[m, pl.ds(at, 32), :] = ref[row, :, m].astype(F32).reshape(32, LATENT).astype(BF)

    turned[0] = mats[3].astype(F32).T.astype(BF)
    turned[1] = mats[6].astype(F32).T.astype(BF)


def interleave(meta, own, other, out):
    for z in range(4):
        out[pl.ds(pl.multiple_of(z * 128 + meta[3] * 64, 64), 64), :] = own[z * 64 : z * 64 + 64]
        out[pl.ds(pl.multiple_of(z * 128 + 64 - meta[3] * 64, 64), 64), :] = other[z * 64 : z * 64 + 64]


def edge_first(meta, v_own, v_other, e_own, e_other, h_own, h_other, mats, src, dst, v_all, e_all, hidden, sender, receiver, halo):
    n = v_all.shape[1]
    interleave(meta, v_own, v_other, v_all)
    interleave(meta, e_own, e_other, e_all)
    swapped = meta[3] == 1
    low = lax.broadcasted_iota(jnp.int32, (halo.shape[0], 128), 1) < 64
    for b in range(2):
        blk = slice(128 * b, 128 * b + 128)
        own, other = h_own[:, blk].astype(F32), h_other[:, blk].astype(F32)
        even = jnp.where(swapped, other, own)
        odd = jnp.where(swapped, own, other)
        halo[:, 256 * b : 256 * b + 128] = jnp.where(low, even, pltpu.roll(odd, 64, 1)).astype(BF)
        halo[:, 256 * b + 128 : 256 * b + 256] = jnp.where(low, pltpu.roll(even, 64, 1), odd).astype(BF)
    sender[:, :n] = dot(mats[1], v_all[...]).astype(BF)
    sender[:, n:] = dot(mats[1], halo[...], 1, 1).astype(BF)
    receiver[...] = dot(mats[2], v_all[...]).astype(BF)

    def body(sl, _):
        pre = dot(mats[0], e_all[:, sl])
        pre += dot(sender[...], hot(src[:, sl], 0, sender.shape[1]))
        pre += dot(receiver[...], hot(dst[:, sl], 0, n))
        hidden[:, sl] = silu(pre)

    chunks(hidden.shape[1], body)


def aggregate(meta, hid, hid_other, turned, turned_other, mats, e_all, v_all, dst, e_new, hidden):
    def edges(sl, _):
        msg = dot(turned[0], hid[:, sl]) + dot(turned_other[0], hid_other[:, sl])
        e_new[:, sl] = norm_add(msg, e_all[:, sl])

    chunks(e_new.shape[1], edges)

    def nodes(sl, first):
        agg = dot(e_new[...], hot(dst[...], first, CHUNK), 1, 1).astype(BF)
        hidden[:, sl] = silu(dot(mats[4], v_all[:, sl]) + dot(mats[5], agg))

    chunks(hidden.shape[1], nodes)


def aggregate_last(meta, hid, hid_other, turned, turned_other, mats, e_all, v_all, dst, e_out, hidden, e_new):
    aggregate(meta, hid, hid_other, turned, turned_other, mats, e_all, v_all, dst, e_new, hidden)
    e_out[...] = e_new[pl.ds(pl.multiple_of(meta[4] * 64, 64), 64), :]


def node_norm(hid, hid_other, turned, turned_other, v_all, v_new):
    def nodes(sl, _):
        msg = dot(turned[1], hid[:, sl]) + dot(turned_other[1], hid_other[:, sl])
        v_new[:, sl] = norm_add(msg, v_all[:, sl])

    chunks(v_new.shape[1], nodes)


def send_next(meta, hid, hid_other, turned, turned_other, v_all, mats, send, v_new, sender, rows):
    node_norm(hid, hid_other, turned, turned_other, v_all, v_new)
    sender[...] = dot(mats[1], v_new[...]).astype(BF)
    select_rows(send, sender[...], rows)


def edge_local(meta, v_all, e_all, sender, mats, src, dst, part, receiver):
    n = v_all.shape[1]
    receiver[...] = dot(mats[2], v_all[...]).astype(BF)

    def body(sl, _):
        pre = dot(mats[0], e_all[:, sl])
        pre += dot(sender[...], hot(src[:, sl], 0, n))
        part[:, sl] = pre + dot(receiver[...], hot(dst[:, sl], 0, n))

    chunks(part.shape[1], body)


def edge_far(n, meta, part, rows, src, hidden, far):
    far[...] = rows[...].astype(F32).T.astype(BF)

    def body(sl, _):
        hidden[:, sl] = silu(part[:, sl] + dot(far[...], hot(src[:, sl], n, far.shape[1])))

    chunks(hidden.shape[1], body)


def finish(meta, hid, hid_other, turned, turned_other, v_all, v_out, v_new):
    node_norm(hid, hid_other, turned, turned_other, v_all, v_new)
    v_out[...] = v_new[pl.ds(pl.multiple_of(meta[4] * 64, 64), 64), :]


def shards(node_feats, edge_feats, send_rows, edge_src, edge_dst, w_edge_in, w_edge_out, w_node_in, w_node_out):
    d = lax.axis_index("dom")
    c = lax.axis_index("ch")
    k = c & 1
    y, x = (d >> 2) & 3, d & 3
    n = node_feats.shape[1]
    m = edge_feats.shape[1]
    first = jnp.where(k == 0, y, x)
    second = jnp.where(k == 0, x, y)
    meta = jnp.stack([c >> 1, first, second, k, c]).astype(jnp.int32)
    send, src, dst = (a.reshape(1, -1) for a in (send_rows, edge_src, edge_dst))

    in_hbm = lambda a: pltpu.with_memory_space_constraint(a, pltpu.HBM)
    weights = (jnp.swapaxes(w_edge_in, 2, 3), w_edge_out, jnp.swapaxes(w_node_in, 2, 3), w_node_out)
    anywhere = pl.BlockSpec(memory_space=pl.ANY)
    (piece,) = call(
        cut_weights, [((7, 8, LATENT), BF)], meta, *map(in_hbm, weights),
        scratch=[pltpu.SemaphoreType.DMA((4,))], space=pl.BlockSpec(memory_space=pltpu.HBM),
    )
    (both,) = call(
        beside, [((64, n + m), BF)], meta, in_hbm(node_feats), in_hbm(edge_feats), piece,
        scratch=[pltpu.SemaphoreType.DMA((2,))], space=anywhere,
    )
    wz = jnp.stack([piece] + [lax.ppermute(piece, "ch", z_shift(s)) for s in (1, 3, 2)])
    parts = ring_gather(both, "ch", z_shift)
    one = jnp.stack([wz] + [lax.ppermute(wz, ("dom", "ch"), ring(1, s)) for s in (3, 2, 1)])
    w_parts = ring_gather(one, ("dom", "ch"), lambda s: ring(2, s))

    v_half, rows = call(
        send_first, [((HALF, n), BF), ((m, HALF), BF)], meta, *parts, send, flops=2 * HALF * n * m
    )

    def exchange(rows):
        return lax.all_to_all(rows.reshape(32, SLOTS, HALF), "dom", 0, 0, tiled=True).reshape(-1, HALF)

    halo = exchange(rows)
    v_other = swap(v_half)
    (e_half,) = call(gather_edges, [((HALF, m), BF)], meta, *parts)
    e_other = swap(e_half)
    halo_other = swap(halo)

    mats, turned, turned_other = [], [], []
    for layer in range(2):
        unpack_layer = functools.partial(unpack, layer)
        w, t = call(unpack_layer, [((7, HALF, LATENT), BF), ((2, LATENT, HALF), BF)], meta, *w_parts)
        mats.append(w)
        turned.append(t)
        turned_other.append(swap(t))

    big = lambda r, q: 2 * r * q * LATENT
    v_all, e_all, hid = call(
        edge_first,
        [((LATENT, n), BF), ((LATENT, m), BF), ((HALF, m), BF)],
        meta, v_half, v_other, e_half, e_other, halo, halo_other, mats[0], src, dst,
        scratch=[pltpu.VMEM((HALF, n + m), BF), pltpu.VMEM((HALF, n), BF), pltpu.VMEM((m, LATENT), BF)],
        flops=4 * big(HALF, n + m),
    )
    e_new, hid_n = call(
        aggregate,
        [((LATENT, m), BF), ((HALF, n), BF)],
        meta, hid, swap(hid), turned[0], turned_other[0], mats[0], e_all, v_all, dst,
        flops=3 * big(LATENT, m),
    )
    v_new, sender, rows = call(
        send_next,
        [((LATENT, n), BF), ((HALF, n), BF), ((m, HALF), BF)],
        meta, hid_n, swap(hid_n), turned[0], turned_other[0], v_all, mats[1], send,
        flops=2 * big(LATENT, n),
    )
    far = exchange(rows)
    (part,) = call(
        edge_local, [((HALF, m), F32)], meta, v_new, e_new, sender, mats[1], src, dst,
        scratch=[pltpu.VMEM((HALF, n), BF)], flops=3 * big(HALF, m),
    )
    (hid,) = call(
        lambda *refs: edge_far(n, *refs), [((HALF, m), BF)], meta, part, far, src,
        scratch=[pltpu.VMEM((HALF, m), BF)], flops=2 * big(HALF, m),
    )
    e_out, hid_n = call(
        aggregate_last,
        [((64, m), BF), ((HALF, n), BF)],
        meta, hid, swap(hid), turned[1], turned_other[1], mats[1], e_new, v_new, dst,
        scratch=[pltpu.VMEM((LATENT, m), BF)], flops=3 * big(LATENT, m),
    )
    (v_out,) = call(
        finish, [((64, n), BF)], meta, hid_n, swap(hid_n), turned[1], turned_other[1], v_new,
        scratch=[pltpu.VMEM((LATENT, n), BF)], flops=big(LATENT, n),
    )
    return v_out, e_out


def solution(mesh):
    in_specs = (
        P("ch", "dom"),
        P("ch", "dom"),
        P("dom"),
        P("dom"),
        P("dom"),
        P(None, None, None, "ch"),
        P(None, "ch", None),
        P(None, None, None, "ch"),
        P(None, "ch", None),
    )
    out_specs = (P("ch", "dom"), P("ch", "dom"))
    return jax.shard_map(shards, mesh=mesh, in_specs=in_specs, out_specs=out_specs, check_vma=False)
```

```python
import functools

import jax
import jax.numpy as jnp
from jax import lax
from jax.experimental import pallas as pl
from jax.experimental.pallas import tpu as pltpu
from jax.sharding import PartitionSpec as P

LATENT = 512
HALF = 256
SLOTS = 32
CHUNK = 256
BF = jnp.bfloat16
F32 = jnp.float32

CORE = [(c, c ^ 1) for c in range(8)]
VMEM = pl.BlockSpec(memory_space=pltpu.VMEM)
SMEM = pl.BlockSpec(memory_space=pltpu.SMEM)


def z_shift(s):
    return [(c, ((c // 2 + s) % 4) * 2 + c % 2) for c in range(8)]


def ring(stage, s):
    pairs = []
    for d in range(32):
        along_x = (d // 4) * 4 + (d + s) % 4
        along_y = (d // 16) * 16 + (d + 4 * s) % 16
        for c in range(8):
            to = along_y if (c % 2 == 0) == (stage == 1) else along_x
            pairs.append((d * 8 + c, to * 8 + c))
    return pairs


def swap(x):
    return lax.ppermute(x, "ch", CORE)


def ring_gather(x, axis, perm):
    half = x.shape[0] // 2
    prev = lax.ppermute(x, axis, perm(1))
    nxt = lax.ppermute(x, axis, perm(3))
    far_a = lax.ppermute(prev[:half], axis, perm(1))
    far_b = lax.ppermute(nxt[half:], axis, perm(3))
    return x, nxt, far_a, far_b, prev


def dot(a, b, ca=1, cb=0):
    return lax.dot_general(a, b, (((ca,), (cb,)), ((), ())), preferred_element_type=F32)


def norm_add(msg, residual):
    mean = jnp.sum(msg, axis=0, keepdims=True) / LATENT
    var = jnp.sum(msg * msg, axis=0, keepdims=True) / LATENT - mean * mean
    return (residual.astype(F32) + (msg - mean) * lax.rsqrt(var + 1e-05)).astype(BF)


def silu(x):
    return (x * jax.nn.sigmoid(x)).astype(BF)


def hot(idx, first, rows):
    where = lax.broadcasted_iota(jnp.int32, (rows, idx.shape[1]), 0) + first == idx
    return jnp.where(where, 1.0, 0.0).astype(BF)


def chunks(n, body):
    def step(i, carry):
        body(pl.ds(pl.multiple_of(i * CHUNK, CHUNK), CHUNK), i * CHUNK)
        return carry

    lax.fori_loop(0, n // CHUNK, step, 0)


def call(kernel, outs, *args, scratch=(), flops=0, space=VMEM, after=()):
    specs = [SMEM] + [space] * (len(args) - 1) + [pl.BlockSpec(memory_space=pl.ANY)] * len(after)
    moved = sum(a.size * a.dtype.itemsize for a in args)
    inputs = len(args)

    def body(*refs):
        kernel(*refs[:inputs], *refs[inputs + len(after) :])

    return pl.pallas_call(
        body,
        out_shape=[jax.ShapeDtypeStruct(s, d) for s, d in outs],
        in_specs=specs,
        out_specs=[VMEM] * len(outs),
        scratch_shapes=list(scratch),
        compiler_params=pltpu.CompilerParams(vmem_limit_bytes=6 << 20),
        cost_estimate=pl.CostEstimate(flops=flops, bytes_accessed=moved, transcendentals=0),
    )(*args, *after)


def place_half(meta, parts, out, col):
    own, nxt, far_a, far_b, prev = parts
    zi = meta[0]
    at = lambda s: pl.multiple_of(((zi + s) & 3) * 64, 64)
    cols = slice(col, col + out.shape[1])
    out[pl.ds(at(0), 64), :] = own[:, cols]
    out[pl.ds(at(1), 64), :] = nxt[:, cols]
    out[pl.ds(at(2), 32), :] = far_a[:, cols]
    out[pl.ds(at(2) + 32, 32), :] = far_b[:, cols]
    out[pl.ds(at(3), 64), :] = prev[:, cols]


def select_rows(send, x, rows):
    def body(sl, _):
        rows[sl, :] = dot(x, hot(send[:, sl], 0, x.shape[1])).T.astype(BF)

    chunks(rows.shape[0], body)


def send_first(meta, own, nxt, far_a, far_b, prev, send, half, rows):
    place_half(meta, (own, nxt, far_a, far_b, prev), half, 0)
    select_rows(send, half[...], rows)


def gather_edges(meta, own, nxt, far_a, far_b, prev, half):
    place_half(meta, (own, nxt, far_a, far_b, prev), half, own.shape[1] - half.shape[1])


def copy_all(copies, sem):
    copies = [pltpu.make_async_copy(a, b, sem.at[i]) for i, (a, b) in enumerate(copies)]
    for copy in copies:
        copy.start()
    for copy in copies:
        copy.wait()


def cut_weights(meta, w_e, w_eo, w_n, w_no, piece, sem):
    lay = meta[1] >> 1
    rows = pl.ds(pl.multiple_of(8 * ((meta[1] & 1) * 4 + meta[2]), 8), 8)
    copies = [
        (w_e.at[lay, :, rows], piece.at[0:3]),
        (w_eo.at[lay, rows], piece.at[3]),
        (w_n.at[lay, :, rows], piece.at[4:6]),
        (w_no.at[lay, rows], piece.at[6]),
    ]
    copy_all(copies, sem)


def beside(meta, v, e, both, sem):
    n = v.shape[1]
    copy_all([(v, both.at[:, :n]), (e, both.at[:, n:])], sem)


def unpack(layer, meta, own, nxt, far_a, far_b, prev, mats, turned):
    for s in range(4):
        for r in range(4):
            a = (meta[1] + r) & 3
            at = pl.multiple_of((((meta[2] + s) & 3) * 2 + (a & 1)) * 32, 32)
            ref, row = ((own, r), (nxt, r), (far_a, r) if r < 2 else (far_b, r - 2), (prev, r))[s]

            @pl.when((a >> 1) == layer)
            def _():
                for m in range(7):
                    mats[m, pl.ds(at, 32), :] = ref[row, :, m].astype(F32).reshape(32, LATENT).astype(BF)

    turned[0] = mats[3].astype(F32).T.astype(BF)
    turned[1] = mats[6].astype(F32).T.astype(BF)


def interleave(meta, own, other, out):
    for z in range(4):
        out[pl.ds(pl.multiple_of(z * 128 + meta[3] * 64, 64), 64), :] = own[z * 64 : z * 64 + 64]
        out[pl.ds(pl.multiple_of(z * 128 + 64 - meta[3] * 64, 64), 64), :] = other[z * 64 : z * 64 + 64]


def edge_first(meta, v_own, v_other, e_own, e_other, h_own, h_other, mats, src, dst, v_all, e_all, hidden, sender, receiver, halo):
    n = v_all.shape[1]
    interleave(meta, v_own, v_other, v_all)
    interleave(meta, e_own, e_other, e_all)
    swapped = meta[3] == 1
    low = lax.broadcasted_iota(jnp.int32, (halo.shape[0], 128), 1) < 64
    for b in range(2):
        blk = slice(128 * b, 128 * b + 128)
        own, other = h_own[:, blk].astype(F32), h_other[:, blk].astype(F32)
        even = jnp.where(swapped, other, own)
        odd = jnp.where(swapped, own, other)
        halo[:, 256 * b : 256 * b + 128] = jnp.where(low, even, pltpu.roll(odd, 64, 1)).astype(BF)
        halo[:, 256 * b + 128 : 256 * b + 256] = jnp.where(low, pltpu.roll(even, 64, 1), odd).astype(BF)
    sender[:, :n] = dot(mats[1], v_all[...]).astype(BF)
    sender[:, n:] = dot(mats[1], halo[...], 1, 1).astype(BF)
    receiver[...] = dot(mats[2], v_all[...]).astype(BF)

    def body(sl, _):
        pre = dot(mats[0], e_all[:, sl])
        pre += dot(sender[...], hot(src[:, sl], 0, sender.shape[1]))
        pre += dot(receiver[...], hot(dst[:, sl], 0, n))
        hidden[:, sl] = silu(pre)

    chunks(hidden.shape[1], body)


def aggregate(meta, hid, hid_other, turned, turned_other, mats, e_all, v_all, dst, e_new, hidden):
    def edges(sl, _):
        msg = dot(turned[0], hid[:, sl]) + dot(turned_other[0], hid_other[:, sl])
        e_new[:, sl] = norm_add(msg, e_all[:, sl])

    chunks(e_new.shape[1], edges)

    def nodes(sl, first):
        agg = dot(e_new[...], hot(dst[...], first, CHUNK), 1, 1).astype(BF)
        hidden[:, sl] = silu(dot(mats[4], v_all[:, sl]) + dot(mats[5], agg))

    chunks(hidden.shape[1], nodes)


def aggregate_last(meta, hid, hid_other, turned, turned_other, mats, e_all, v_all, dst, e_out, hidden, e_new):
    aggregate(meta, hid, hid_other, turned, turned_other, mats, e_all, v_all, dst, e_new, hidden)
    e_out[...] = e_new[pl.ds(pl.multiple_of(meta[4] * 64, 64), 64), :]


def node_norm(hid, hid_other, turned, turned_other, v_all, v_new):
    def nodes(sl, _):
        msg = dot(turned[1], hid[:, sl]) + dot(turned_other[1], hid_other[:, sl])
        v_new[:, sl] = norm_add(msg, v_all[:, sl])

    chunks(v_new.shape[1], nodes)


def send_next(meta, hid, hid_other, turned, turned_other, v_all, mats, send, v_new, sender, rows):
    node_norm(hid, hid_other, turned, turned_other, v_all, v_new)
    sender[...] = dot(mats[1], v_new[...]).astype(BF)
    select_rows(send, sender[...], rows)


def edge_local(meta, v_all, e_all, sender, mats, src, dst, part, receiver):
    n = v_all.shape[1]
    receiver[...] = dot(mats[2], v_all[...]).astype(BF)

    def body(sl, _):
        pre = dot(mats[0], e_all[:, sl])
        pre += dot(sender[...], hot(src[:, sl], 0, n))
        part[:, sl] = pre + dot(receiver[...], hot(dst[:, sl], 0, n))

    chunks(part.shape[1], body)


def edge_far(n, meta, part, rows, src, hidden, far):
    far[...] = rows[...].astype(F32).T.astype(BF)

    def body(sl, _):
        hidden[:, sl] = silu(part[:, sl] + dot(far[...], hot(src[:, sl], n, far.shape[1])))

    chunks(hidden.shape[1], body)


def finish(meta, hid, hid_other, turned, turned_other, v_all, v_out, v_new):
    node_norm(hid, hid_other, turned, turned_other, v_all, v_new)
    v_out[...] = v_new[pl.ds(pl.multiple_of(meta[4] * 64, 64), 64), :]


def shards(node_feats, edge_feats, send_rows, edge_src, edge_dst, w_edge_in, w_edge_out, w_node_in, w_node_out):
    d = lax.axis_index("dom")
    c = lax.axis_index("ch")
    k = c & 1
    y, x = (d >> 2) & 3, d & 3
    n = node_feats.shape[1]
    m = edge_feats.shape[1]
    first = jnp.where(k == 0, y, x)
    second = jnp.where(k == 0, x, y)
    meta = jnp.stack([c >> 1, first, second, k, c]).astype(jnp.int32)
    send, src, dst = (a.reshape(1, -1) for a in (send_rows, edge_src, edge_dst))

    in_hbm = lambda a: pltpu.with_memory_space_constraint(a, pltpu.HBM)
    weights = (jnp.swapaxes(w_edge_in, 2, 3), w_edge_out, jnp.swapaxes(w_node_in, 2, 3), w_node_out)
    hbm = pl.BlockSpec(memory_space=pltpu.HBM)
    (piece,) = call(
        cut_weights, [((7, 8, LATENT), BF)], meta, *map(in_hbm, weights),
        scratch=[pltpu.SemaphoreType.DMA((4,))], space=hbm,
    )
    pieces = [piece] + [lax.ppermute(piece, "ch", z_shift(s)) for s in (1, 3, 2)]
    (both,) = call(
        beside, [((64, n + m), BF)], meta, in_hbm(node_feats), in_hbm(edge_feats),
        scratch=[pltpu.SemaphoreType.DMA((2,))], space=hbm, after=pieces[1:2],
    )
    wz = jnp.stack(pieces)
    parts = ring_gather(both, "ch", z_shift)
    quarters = [wz] + [lax.ppermute(wz, ("dom", "ch"), ring(1, s)) for s in (3, 2, 1)]
    quarters[0] = lax.optimization_barrier((wz, parts[1], parts[4]))[0]
    one = jnp.stack(quarters)
    w_parts = ring_gather(one, ("dom", "ch"), lambda s: ring(2, s))

    v_half, rows = call(
        send_first, [((HALF, n), BF), ((m, HALF), BF)], meta, *parts, send, flops=2 * HALF * n * m, after=(w_parts[1], w_parts[4])
    )

    def exchange(rows):
        return lax.all_to_all(rows.reshape(32, SLOTS, HALF), "dom", 0, 0, tiled=True).reshape(-1, HALF)

    halo = exchange(rows)
    v_other = swap(v_half)
    (e_half,) = call(gather_edges, [((HALF, m), BF)], meta, *parts)
    e_other = swap(e_half)
    halo_other = swap(halo)

    mats, turned, turned_other = [], [], []
    for layer in range(2):
        unpack_layer = functools.partial(unpack, layer)
        w, t = call(unpack_layer, [((7, HALF, LATENT), BF), ((2, LATENT, HALF), BF)], meta, *w_parts)
        mats.append(w)
        turned.append(t)
        turned_other.append(swap(t))

    big = lambda r, q: 2 * r * q * LATENT
    v_all, e_all, hid = call(
        edge_first,
        [((LATENT, n), BF), ((LATENT, m), BF), ((HALF, m), BF)],
        meta, v_half, v_other, e_half, e_other, halo, halo_other, mats[0], src, dst,
        scratch=[pltpu.VMEM((HALF, n + m), BF), pltpu.VMEM((HALF, n), BF), pltpu.VMEM((m, LATENT), BF)],
        flops=4 * big(HALF, n + m),
    )
    e_new, hid_n = call(
        aggregate,
        [((LATENT, m), BF), ((HALF, n), BF)],
        meta, hid, swap(hid), turned[0], turned_other[0], mats[0], e_all, v_all, dst,
        flops=3 * big(LATENT, m),
    )
    v_new, sender, rows = call(
        send_next,
        [((LATENT, n), BF), ((HALF, n), BF), ((m, HALF), BF)],
        meta, hid_n, swap(hid_n), turned[0], turned_other[0], v_all, mats[1], send,
        flops=2 * big(LATENT, n),
    )
    far = exchange(rows)
    (part,) = call(
        edge_local, [((HALF, m), F32)], meta, v_new, e_new, sender, mats[1], src, dst,
        scratch=[pltpu.VMEM((HALF, n), BF)], flops=3 * big(HALF, m),
    )
    (hid,) = call(
        lambda *refs: edge_far(n, *refs), [((HALF, m), BF)], meta, part, far, src,
        scratch=[pltpu.VMEM((HALF, m), BF)], flops=2 * big(HALF, m),
    )
    e_out, hid_n = call(
        aggregate_last,
        [((64, m), BF), ((HALF, n), BF)],
        meta, hid, swap(hid), turned[1], turned_other[1], mats[1], e_new, v_new, dst,
        scratch=[pltpu.VMEM((LATENT, m), BF)], flops=3 * big(LATENT, m),
    )
    (v_out,) = call(
        finish, [((64, n), BF)], meta, hid_n, swap(hid_n), turned[1], turned_other[1], v_new,
        scratch=[pltpu.VMEM((LATENT, n), BF)], flops=big(LATENT, n),
    )
    return v_out, e_out


def solution(mesh):
    in_specs = (
        P("ch", "dom"),
        P("ch", "dom"),
        P("dom"),
        P("dom"),
        P("dom"),
        P(None, None, None, "ch"),
        P(None, "ch", None),
        P(None, None, None, "ch"),
        P(None, "ch", None),
    )
    out_specs = (P("ch", "dom"), P("ch", "dom"))
    return jax.shard_map(shards, mesh=mesh, in_specs=in_specs, out_specs=out_specs, check_vma=False)
```

```python
import functools

import jax
import jax.numpy as jnp
from jax import lax
from jax.experimental import pallas as pl
from jax.experimental.pallas import tpu as pltpu
from jax.sharding import PartitionSpec as P

LATENT = 512
HALF = 256
SLOTS = 32
CHUNK = 256
BF = jnp.bfloat16
F32 = jnp.float32

CORE = [(c, c ^ 1) for c in range(8)]
VMEM = pl.BlockSpec(memory_space=pltpu.VMEM)
SMEM = pl.BlockSpec(memory_space=pltpu.SMEM)


def z_shift(s):
    return [(c, ((c // 2 + s) % 4) * 2 + c % 2) for c in range(8)]


def ring(stage, s):
    pairs = []
    for d in range(32):
        along_x = (d // 4) * 4 + (d + s) % 4
        along_y = (d // 16) * 16 + (d + 4 * s) % 16
        for c in range(8):
            to = along_y if (c % 2 == 0) == (stage == 1) else along_x
            pairs.append((d * 8 + c, to * 8 + c))
    return pairs


def swap(x):
    return lax.ppermute(x, "ch", CORE)


def ring_gather(x, axis, perm):
    half = x.shape[0] // 2
    prev = lax.ppermute(x, axis, perm(1))
    nxt = lax.ppermute(x, axis, perm(3))
    far_a = lax.ppermute(prev[:half], axis, perm(1))
    far_b = lax.ppermute(nxt[half:], axis, perm(3))
    return x, nxt, far_a, far_b, prev


def dot(a, b, ca=1, cb=0):
    return lax.dot_general(a, b, (((ca,), (cb,)), ((), ())), preferred_element_type=F32)


def norm_add(msg, residual):
    mean = jnp.sum(msg, axis=0, keepdims=True) / LATENT
    var = jnp.sum(msg * msg, axis=0, keepdims=True) / LATENT - mean * mean
    return (residual.astype(F32) + (msg - mean) * lax.rsqrt(var + 1e-05)).astype(BF)


def silu(x):
    return (x * jax.nn.sigmoid(x)).astype(BF)


def hot(idx, first, rows):
    where = lax.broadcasted_iota(jnp.int32, (rows, idx.shape[1]), 0) + first == idx
    return jnp.where(where, 1.0, 0.0).astype(BF)


def chunks(n, body):
    def step(i, carry):
        body(pl.ds(pl.multiple_of(i * CHUNK, CHUNK), CHUNK), i * CHUNK)
        return carry

    lax.fori_loop(0, n // CHUNK, step, 0)


def call(kernel, outs, *args, scratch=(), flops=0, space=VMEM, after=()):
    specs = [SMEM] + [space] * (len(args) - 1) + [pl.BlockSpec(memory_space=pl.ANY)] * len(after)
    moved = sum(a.size * a.dtype.itemsize for a in args)
    inputs = len(args)

    def body(*refs):
        kernel(*refs[:inputs], *refs[inputs + len(after) :])

    return pl.pallas_call(
        body,
        out_shape=[jax.ShapeDtypeStruct(s, d) for s, d in outs],
        in_specs=specs,
        out_specs=[VMEM] * len(outs),
        scratch_shapes=list(scratch),
        compiler_params=pltpu.CompilerParams(vmem_limit_bytes=6 << 20),
        cost_estimate=pl.CostEstimate(flops=flops, bytes_accessed=moved, transcendentals=0),
    )(*args, *after)


def place_half(meta, parts, out, col):
    own, nxt, far_a, far_b, prev = parts
    zi = meta[0]
    at = lambda s: pl.multiple_of(((zi + s) & 3) * 64, 64)
    cols = slice(col, col + out.shape[1])
    out[pl.ds(at(0), 64), :] = own[:, cols]
    out[pl.ds(at(1), 64), :] = nxt[:, cols]
    out[pl.ds(at(2), 32), :] = far_a[:, cols]
    out[pl.ds(at(2) + 32, 32), :] = far_b[:, cols]
    out[pl.ds(at(3), 64), :] = prev[:, cols]


def select_rows(send, x, rows):
    def body(sl, _):
        rows[sl, :] = dot(x, hot(send[:, sl], 0, x.shape[1])).T.astype(BF)

    chunks(rows.shape[0], body)


def send_first(meta, own, nxt, far_a, far_b, prev, send, half, rows):
    place_half(meta, (own, nxt, far_a, far_b, prev), half, 0)
    select_rows(send, half[...], rows)


def gather_edges(meta, own, nxt, far_a, far_b, prev, half):
    place_half(meta, (own, nxt, far_a, far_b, prev), half, own.shape[1] - half.shape[1])


def prepare(meta, w_e, w_eo, w_n, w_no, v, e, piece, both, sem):
    lay = meta[1] >> 1
    rows = pl.ds(pl.multiple_of(8 * ((meta[1] & 1) * 4 + meta[2]), 8), 8)
    n = v.shape[1]
    copies = [
        (w_e.at[lay, :, rows], piece.at[0:3]),
        (w_eo.at[lay, rows], piece.at[3]),
        (w_n.at[lay, :, rows], piece.at[4:6]),
        (w_no.at[lay, rows], piece.at[6]),
        (v, both.at[:, :n]),
        (e, both.at[:, n:]),
    ]
    copies = [pltpu.make_async_copy(a, b, sem.at[i]) for i, (a, b) in enumerate(copies)]
    for copy in copies:
        copy.start()
    for copy in copies:
        copy.wait()


def unpack(layer, meta, own, nxt, far_a, far_b, prev, mats, turned):
    for s in range(4):
        for r in range(4):
            a = (meta[1] + r) & 3
            at = pl.multiple_of((((meta[2] + s) & 3) * 2 + (a & 1)) * 32, 32)
            ref, row = ((own, r), (nxt, r), (far_a, r) if r < 2 else (far_b, r - 2), (prev, r))[s]

            @pl.when((a >> 1) == layer)
            def _():
                for m in range(7):
                    mats[m, pl.ds(at, 32), :] = ref[row, :, m].astype(F32).reshape(32, LATENT).astype(BF)

    turned[0] = mats[3].astype(F32).T.astype(BF)
    turned[1] = mats[6].astype(F32).T.astype(BF)


def interleave(meta, own, other, out):
    for z in range(4):
        out[pl.ds(pl.multiple_of(z * 128 + meta[3] * 64, 64), 64), :] = own[z * 64 : z * 64 + 64]
        out[pl.ds(pl.multiple_of(z * 128 + 64 - meta[3] * 64, 64), 64), :] = other[z * 64 : z * 64 + 64]


def edge_first(meta, v_own, v_other, e_own, e_other, h_own, h_other, mats, src, dst, v_all, e_all, hidden, sender, receiver, halo):
    n = v_all.shape[1]
    interleave(meta, v_own, v_other, v_all)
    interleave(meta, e_own, e_other, e_all)
    swapped = meta[3] == 1
    low = lax.broadcasted_iota(jnp.int32, (halo.shape[0], 128), 1) < 64
    for b in range(2):
        blk = slice(128 * b, 128 * b + 128)
        own, other = h_own[:, blk].astype(F32), h_other[:, blk].astype(F32)
        even = jnp.where(swapped, other, own)
        odd = jnp.where(swapped, own, other)
        halo[:, 256 * b : 256 * b + 128] = jnp.where(low, even, pltpu.roll(odd, 64, 1)).astype(BF)
        halo[:, 256 * b + 128 : 256 * b + 256] = jnp.where(low, pltpu.roll(even, 64, 1), odd).astype(BF)
    sender[:, :n] = dot(mats[1], v_all[...]).astype(BF)
    sender[:, n:] = dot(mats[1], halo[...], 1, 1).astype(BF)
    receiver[...] = dot(mats[2], v_all[...]).astype(BF)

    def body(sl, _):
        pre = dot(mats[0], e_all[:, sl])
        pre += dot(sender[...], hot(src[:, sl], 0, sender.shape[1]))
        pre += dot(receiver[...], hot(dst[:, sl], 0, n))
        hidden[:, sl] = silu(pre)

    chunks(hidden.shape[1], body)


def aggregate(meta, hid, hid_other, turned, turned_other, mats, e_all, v_all, dst, e_new, hidden):
    def edges(sl, _):
        msg = dot(turned[0], hid[:, sl]) + dot(turned_other[0], hid_other[:, sl])
        e_new[:, sl] = norm_add(msg, e_all[:, sl])

    chunks(e_new.shape[1], edges)

    def nodes(sl, first):
        agg = dot(e_new[...], hot(dst[...], first, CHUNK), 1, 1).astype(BF)
        hidden[:, sl] = silu(dot(mats[4], v_all[:, sl]) + dot(mats[5], agg))

    chunks(hidden.shape[1], nodes)


def aggregate_last(meta, hid, hid_other, turned, turned_other, mats, e_all, v_all, dst, e_out, hidden, e_new):
    aggregate(meta, hid, hid_other, turned, turned_other, mats, e_all, v_all, dst, e_new, hidden)
    e_out[...] = e_new[pl.ds(pl.multiple_of(meta[4] * 64, 64), 64), :]


def node_norm(hid, hid_other, turned, turned_other, v_all, v_new):
    def nodes(sl, _):
        msg = dot(turned[1], hid[:, sl]) + dot(turned_other[1], hid_other[:, sl])
        v_new[:, sl] = norm_add(msg, v_all[:, sl])

    chunks(v_new.shape[1], nodes)


def send_next(meta, hid, hid_other, turned, turned_other, v_all, mats, send, v_new, sender, rows):
    node_norm(hid, hid_other, turned, turned_other, v_all, v_new)
    sender[...] = dot(mats[1], v_new[...]).astype(BF)
    select_rows(send, sender[...], rows)


def edge_local(meta, v_all, e_all, sender, mats, src, dst, part, receiver):
    n = v_all.shape[1]
    receiver[...] = dot(mats[2], v_all[...]).astype(BF)

    def body(sl, _):
        pre = dot(mats[0], e_all[:, sl])
        pre += dot(sender[...], hot(src[:, sl], 0, n))
        part[:, sl] = pre + dot(receiver[...], hot(dst[:, sl], 0, n))

    chunks(part.shape[1], body)


def edge_far(n, meta, part, rows, src, hidden, far):
    far[...] = rows[...].astype(F32).T.astype(BF)

    def body(sl, _):
        hidden[:, sl] = silu(part[:, sl] + dot(far[...], hot(src[:, sl], n, far.shape[1])))

    chunks(hidden.shape[1], body)


def finish(meta, hid, hid_other, turned, turned_other, v_all, v_out, v_new):
    node_norm(hid, hid_other, turned, turned_other, v_all, v_new)
    v_out[...] = v_new[pl.ds(pl.multiple_of(meta[4] * 64, 64), 64), :]


def shards(node_feats, edge_feats, send_rows, edge_src, edge_dst, w_edge_in, w_edge_out, w_node_in, w_node_out):
    d = lax.axis_index("dom")
    c = lax.axis_index("ch")
    k = c & 1
    y, x = (d >> 2) & 3, d & 3
    n = node_feats.shape[1]
    m = edge_feats.shape[1]
    first = jnp.where(k == 0, y, x)
    second = jnp.where(k == 0, x, y)
    meta = jnp.stack([c >> 1, first, second, k, c]).astype(jnp.int32)
    send, src, dst = (a.reshape(1, -1) for a in (send_rows, edge_src, edge_dst))

    shared = (jnp.swapaxes(w_edge_in, 2, 3), w_edge_out, jnp.swapaxes(w_node_in, 2, 3), w_node_out, node_feats, edge_feats)
    piece, both = call(
        prepare,
        [((7, 8, LATENT), BF), ((64, n + m), BF)],
        meta, *(pltpu.with_memory_space_constraint(a, pltpu.HBM) for a in shared),
        scratch=[pltpu.SemaphoreType.DMA((6,))], space=pl.BlockSpec(memory_space=pltpu.HBM),
    )
    pieces = [piece] + [lax.ppermute(piece, "ch", z_shift(s)) for s in (1, 3, 2)]
    both = lax.optimization_barrier((both, pieces[1]))[0]
    wz = jnp.stack(pieces)
    parts = ring_gather(both, "ch", z_shift)
    quarters = [wz] + [lax.ppermute(wz, ("dom", "ch"), ring(1, s)) for s in (3, 2, 1)]
    quarters[0] = lax.optimization_barrier((wz, parts[1], parts[4]))[0]
    one = jnp.stack(quarters)
    w_parts = ring_gather(one, ("dom", "ch"), lambda s: ring(2, s))

    v_half, rows = call(
        send_first, [((HALF, n), BF), ((m, HALF), BF)], meta, *parts, send, flops=2 * HALF * n * m
    )

    def exchange(rows):
        return lax.all_to_all(rows.reshape(32, SLOTS, HALF), "dom", 0, 0, tiled=True).reshape(-1, HALF)

    halo = exchange(lax.optimization_barrier((rows, w_parts[1], w_parts[4]))[0])
    v_other = swap(v_half)
    (e_half,) = call(gather_edges, [((HALF, m), BF)], meta, *parts, flops=8 * HALF * n * m, after=w_parts[2:4])
    e_other = swap(e_half)
    halo_other = swap(halo)

    mats, turned, turned_other = [], [], []
    for layer in range(2):
        unpack_layer = functools.partial(unpack, layer)
        w, t = call(unpack_layer, [((7, HALF, LATENT), BF), ((2, LATENT, HALF), BF)], meta, *w_parts)
        mats.append(w)
        turned.append(t)
        turned_other.append(swap(t))

    big = lambda r, q: 2 * r * q * LATENT
    v_all, e_all, hid = call(
        edge_first,
        [((LATENT, n), BF), ((LATENT, m), BF), ((HALF, m), BF)],
        meta, v_half, v_other, e_half, e_other, halo, halo_other, mats[0], src, dst,
        scratch=[pltpu.VMEM((HALF, n + m), BF), pltpu.VMEM((HALF, n), BF), pltpu.VMEM((m, LATENT), BF)],
        flops=4 * big(HALF, n + m),
    )
    e_new, hid_n = call(
        aggregate,
        [((LATENT, m), BF), ((HALF, n), BF)],
        meta, hid, swap(hid), turned[0], turned_other[0], mats[0], e_all, v_all, dst,
        flops=3 * big(LATENT, m),
    )
    v_new, sender, rows = call(
        send_next,
        [((LATENT, n), BF), ((HALF, n), BF), ((m, HALF), BF)],
        meta, hid_n, swap(hid_n), turned[0], turned_other[0], v_all, mats[1], send,
        flops=2 * big(LATENT, n),
    )
    far = exchange(rows)
    (part,) = call(
        edge_local, [((HALF, m), F32)], meta, v_new, e_new, sender, mats[1], src, dst,
        scratch=[pltpu.VMEM((HALF, n), BF)], flops=3 * big(HALF, m),
    )
    (hid,) = call(
        lambda *refs: edge_far(n, *refs), [((HALF, m), BF)], meta, part, far, src,
        scratch=[pltpu.VMEM((HALF, m), BF)], flops=2 * big(HALF, m),
    )
    e_out, hid_n = call(
        aggregate_last,
        [((64, m), BF), ((HALF, n), BF)],
        meta, hid, swap(hid), turned[1], turned_other[1], mats[1], e_new, v_new, dst,
        scratch=[pltpu.VMEM((LATENT, m), BF)], flops=3 * big(LATENT, m),
    )
    (v_out,) = call(
        finish, [((64, n), BF)], meta, hid_n, swap(hid_n), turned[1], turned_other[1], v_new,
        scratch=[pltpu.VMEM((LATENT, n), BF)], flops=big(LATENT, n),
    )
    return v_out, e_out


def solution(mesh):
    in_specs = (
        P("ch", "dom"),
        P("ch", "dom"),
        P("dom"),
        P("dom"),
        P("dom"),
        P(None, None, None, "ch"),
        P(None, "ch", None),
        P(None, None, None, "ch"),
        P(None, "ch", None),
    )
    out_specs = (P("ch", "dom"), P("ch", "dom"))
    return jax.shard_map(shards, mesh=mesh, in_specs=in_specs, out_specs=out_specs, check_vma=False)
```

```python
import functools

import jax
import jax.numpy as jnp
from jax import lax
from jax.experimental import pallas as pl
from jax.experimental.pallas import tpu as pltpu
from jax.sharding import PartitionSpec as P

LATENT = 512
HALF = 256
SLOTS = 32
CHUNK = 512
BF = jnp.bfloat16
F32 = jnp.float32

CORE = [(c, c ^ 1) for c in range(8)]
VMEM = pl.BlockSpec(memory_space=pltpu.VMEM)
SMEM = pl.BlockSpec(memory_space=pltpu.SMEM)


def z_shift(s):
    return [(c, ((c // 2 + s) % 4) * 2 + c % 2) for c in range(8)]


def ring(stage, s):
    pairs = []
    for d in range(32):
        along_x = (d // 4) * 4 + (d + s) % 4
        along_y = (d // 16) * 16 + (d + 4 * s) % 16
        for c in range(8):
            to = along_y if (c % 2 == 0) == (stage == 1) else along_x
            pairs.append((d * 8 + c, to * 8 + c))
    return pairs


def swap(x):
    return lax.ppermute(x, "ch", CORE)


def ring_gather(x, axis, perm):
    half = x.shape[0] // 2
    prev = lax.ppermute(x, axis, perm(1))
    nxt = lax.ppermute(x, axis, perm(3))
    far_a = lax.ppermute(prev[:half], axis, perm(1))
    far_b = lax.ppermute(nxt[half:], axis, perm(3))
    return x, nxt, far_a, far_b, prev


def dot(a, b, ca=1, cb=0):
    return lax.dot_general(a, b, (((ca,), (cb,)), ((), ())), preferred_element_type=F32)


def norm_add(msg, residual, part=None):
    mean = jnp.sum(msg, axis=0, keepdims=True) / LATENT
    var = jnp.sum(msg * msg, axis=0, keepdims=True) / LATENT - mean * mean
    part = msg if part is None else part
    return (residual.astype(F32) + (part - mean) * lax.rsqrt(var + 1e-05)).astype(BF)


def silu(x):
    return (x * jax.nn.sigmoid(x)).astype(BF)


def hot(idx, first, rows):
    where = lax.broadcasted_iota(jnp.int32, (rows, idx.shape[1]), 0) + first == idx
    return where.astype(BF)


def chunks(n, body):
    size = CHUNK if n % CHUNK == 0 else n // 2
    for first in range(0, n, size):
        body(slice(first, first + size), first)


def call(kernel, outs, *args, scratch=(), flops=0, space=VMEM, after=()):
    specs = [SMEM] + [space] * (len(args) - 1) + [pl.BlockSpec(memory_space=pl.ANY)] * len(after)
    moved = sum(a.size * a.dtype.itemsize for a in args)
    inputs = len(args)

    def body(*refs):
        kernel(*refs[:inputs], *refs[inputs + len(after) :])

    return pl.pallas_call(
        body,
        out_shape=[jax.ShapeDtypeStruct(s, d) for s, d in outs],
        in_specs=specs,
        out_specs=[VMEM] * len(outs),
        scratch_shapes=list(scratch),
        compiler_params=pltpu.CompilerParams(vmem_limit_bytes=6 << 20),
        cost_estimate=pl.CostEstimate(flops=flops, bytes_accessed=moved, transcendentals=0),
    )(*args, *after)


def place_half(meta, parts, out, col):
    own, nxt, far_a, far_b, prev = parts
    zi = meta[0]
    at = lambda s: pl.multiple_of(((zi + s) & 3) * 64, 64)
    cols = slice(col, col + out.shape[1])
    out[pl.ds(at(0), 64), :] = own[:, cols]
    out[pl.ds(at(1), 64), :] = nxt[:, cols]
    out[pl.ds(at(2), 32), :] = far_a[:, cols]
    out[pl.ds(at(2) + 32, 32), :] = far_b[:, cols]
    out[pl.ds(at(3), 64), :] = prev[:, cols]


def select_rows(send, x, rows):
    def body(sl, _):
        rows[sl, :] = dot(x, hot(send[:, sl], 0, x.shape[1])).T.astype(BF)

    chunks(rows.shape[0], body)


def send_first(meta, own, nxt, far_a, far_b, prev, send, half, rows):
    place_half(meta, (own, nxt, far_a, far_b, prev), half, 0)
    select_rows(send, half[...], rows)


def gather_edges(meta, own, nxt, far_a, far_b, prev, half):
    place_half(meta, (own, nxt, far_a, far_b, prev), half, own.shape[1] - half.shape[1])


def prepare(meta, w_e, w_eo, w_n, w_no, v, e, piece, both, sem):
    lay = meta[1] >> 1
    rows = pl.ds(pl.multiple_of(8 * ((meta[1] & 1) * 4 + meta[2]), 8), 8)
    n = v.shape[1]
    copies = [
        (w_e.at[lay, :, rows], piece.at[0:3]),
        (w_eo.at[lay, rows], piece.at[3]),
        (w_n.at[lay, :, rows], piece.at[4:6]),
        (w_no.at[lay, rows], piece.at[6]),
        (v, both.at[:, :n]),
        (e, both.at[:, n:]),
    ]
    copies = [pltpu.make_async_copy(a, b, sem.at[i]) for i, (a, b) in enumerate(copies)]
    for copy in copies:
        copy.start()
    for copy in copies:
        copy.wait()


def unpack(layer, meta, own, nxt, far_a, far_b, prev, mats, nodes, turned, outs):
    where = [mats.at[0], mats.at[1], mats.at[2], outs.at[0], nodes.at[0], nodes.at[1], outs.at[1]]
    for s in range(4):
        for r in range(4):
            a = (meta[1] + r) & 3
            at = pl.multiple_of((((meta[2] + s) & 3) * 2 + (a & 1)) * 32, 32)
            ref, row = ((own, r), (nxt, r), (far_a, r) if r < 2 else (far_b, r - 2), (prev, r))[s]

            @pl.when((a >> 1) == layer)
            def _():
                for m in range(7):
                    where[m][pl.ds(at, 32), :] = ref[row, :, m].astype(F32).reshape(32, LATENT).astype(BF)

    turned[0] = outs[0].astype(F32).T.astype(BF)
    turned[1] = outs[1].astype(F32).T.astype(BF)


def interleave(meta, own, other, out):
    for z in range(4):
        out[pl.ds(pl.multiple_of(z * 128 + meta[3] * 64, 64), 64), :] = own[z * 64 : z * 64 + 64]
        out[pl.ds(pl.multiple_of(z * 128 + 64 - meta[3] * 64, 64), 64), :] = other[z * 64 : z * 64 + 64]


def edge_first(meta, v_own, v_other, e_own, e_other, h_own, h_other, mats, src, dst, v_all, e_all, hidden, sender, receiver, halo):
    n = v_all.shape[1]
    interleave(meta, v_own, v_other, v_all)
    interleave(meta, e_own, e_other, e_all)
    swapped = meta[3] == 1
    low = lax.broadcasted_iota(jnp.int32, (halo.shape[0], 128), 1) < 64
    for b in range(2):
        blk = slice(128 * b, 128 * b + 128)
        own, other = h_own[:, blk].astype(F32), h_other[:, blk].astype(F32)
        even = jnp.where(swapped, other, own)
        odd = jnp.where(swapped, own, other)
        halo[:, 256 * b : 256 * b + 128] = jnp.where(low, even, pltpu.roll(odd, 64, 1)).astype(BF)
        halo[:, 256 * b + 128 : 256 * b + 256] = jnp.where(low, pltpu.roll(even, 64, 1), odd).astype(BF)
    sender[:, :n] = dot(mats[1], v_all[...]).astype(BF)
    sender[:, n:] = dot(mats[1], halo[...], 1, 1).astype(BF)
    receiver[...] = dot(mats[2], v_all[...]).astype(BF)

    def body(sl, _):
        pre = dot(mats[0], e_all[:, sl])
        pre += dot(sender[...], hot(src[:, sl], 0, sender.shape[1]))
        pre += dot(receiver[...], hot(dst[:, sl], 0, n))
        hidden[:, sl] = silu(pre)

    chunks(hidden.shape[1], body)


def new_edges(hid, hid_other, turned, turned_other, e_all, e_new):
    def edges(sl, _):
        msg = dot(turned[0], hid[:, sl]) + dot(turned_other[0], hid_other[:, sl])
        e_new[:, sl] = norm_add(msg, e_all[:, sl])

    chunks(e_new.shape[1], edges)


def node_message(first, sl, turned, turned_other, nodes, nodes_other, e_new, v_all, dst):
    agg = dot(e_new[...], hot(dst[...], first, sl.stop - sl.start), 1, 1).astype(BF)
    msg = dot(turned[1], silu(dot(nodes[0], v_all[:, sl]) + dot(nodes[1], agg)))
    return msg + dot(turned_other[1], silu(dot(nodes_other[0], v_all[:, sl]) + dot(nodes_other[1], agg)))


def tail_first(
    meta, hid, hid_other, turned, turned_other, nodes, nodes_other, e_all, v_all, dst, mats_next, send,
    e_new, v_new, sender, rows,
):
    new_edges(hid, hid_other, turned, turned_other, e_all, e_new)

    def body(sl, first):
        msg = node_message(first, sl, turned, turned_other, nodes, nodes_other, e_new, v_all, dst)
        v_new[:, sl] = norm_add(msg, v_all[:, sl])

    chunks(v_new.shape[1], body)
    sender[...] = dot(mats_next[1], v_new[...]).astype(BF)
    select_rows(send, sender[...], rows)


def tail_last(
    meta, hid, hid_other, turned, turned_other, nodes, nodes_other, e_all, v_all, dst,
    e_out, v_out, e_new, sums,
):
    new_edges(hid, hid_other, turned, turned_other, e_all, e_new)
    mine = pl.ds(pl.multiple_of(meta[4] * 64, 64), 64)
    e_out[...] = e_new[mine, :]

    def body(sl, first):
        msg = node_message(first, sl, turned, turned_other, nodes, nodes_other, e_new, v_all, dst)
        sums[...] = msg
        v_out[:, sl] = norm_add(msg, v_all[mine, sl], sums[mine, :])

    chunks(v_out.shape[1], body)


def edge_local(meta, v_all, e_all, sender, mats, src, dst, part, receiver):
    n = v_all.shape[1]
    receiver[...] = dot(mats[2], v_all[...]).astype(BF)

    def body(sl, _):
        pre = dot(mats[0], e_all[:, sl])
        pre += dot(sender[...], hot(src[:, sl], 0, n))
        part[:, sl] = pre + dot(receiver[...], hot(dst[:, sl], 0, n))

    chunks(part.shape[1], body)


def edge_far(n, meta, part, rows, src, hidden, far):
    far[...] = rows[...].astype(F32).T.astype(BF)

    def body(sl, _):
        hidden[:, sl] = silu(part[:, sl] + dot(far[...], hot(src[:, sl], n, far.shape[1])))

    chunks(hidden.shape[1], body)


def shards(node_feats, edge_feats, send_rows, edge_src, edge_dst, w_edge_in, w_edge_out, w_node_in, w_node_out):
    d = lax.axis_index("dom")
    c = lax.axis_index("ch")
    k = c & 1
    y, x = (d >> 2) & 3, d & 3
    n = node_feats.shape[1]
    m = edge_feats.shape[1]
    first = jnp.where(k == 0, y, x)
    second = jnp.where(k == 0, x, y)
    meta = jnp.stack([c >> 1, first, second, k, c]).astype(jnp.int32)
    send, src, dst = (a.reshape(1, -1) for a in (send_rows, edge_src, edge_dst))

    shared = (jnp.swapaxes(w_edge_in, 2, 3), w_edge_out, jnp.swapaxes(w_node_in, 2, 3), w_node_out, node_feats, edge_feats)
    piece, both = call(
        prepare,
        [((7, 8, LATENT), BF), ((64, n + m), BF)],
        meta, *(pltpu.with_memory_space_constraint(a, pltpu.HBM) for a in shared),
        scratch=[pltpu.SemaphoreType.DMA((6,))], space=pl.BlockSpec(memory_space=pltpu.HBM),
    )
    pieces = [piece] + [lax.ppermute(piece, "ch", z_shift(s)) for s in (1, 3, 2)]
    both = lax.optimization_barrier((both, pieces[1]))[0]
    wz = jnp.stack(pieces)
    parts = ring_gather(both, "ch", z_shift)
    quarters = [wz] + [lax.ppermute(wz, ("dom", "ch"), ring(1, s)) for s in (3, 2, 1)]
    quarters[0] = lax.optimization_barrier((wz, parts[1], parts[4]))[0]
    one = jnp.stack(quarters)
    w_parts = ring_gather(one, ("dom", "ch"), lambda s: ring(2, s))

    v_half, rows = call(
        send_first, [((HALF, n), BF), ((m, HALF), BF)], meta, *parts, send, flops=2 * HALF * n * m
    )

    def exchange(rows):
        return lax.all_to_all(rows.reshape(32, SLOTS, HALF), "dom", 0, 0, tiled=True).reshape(-1, HALF)

    halo = exchange(lax.optimization_barrier((rows, w_parts[1], w_parts[4]))[0])
    v_other = swap(v_half)
    (e_half,) = call(gather_edges, [((HALF, m), BF)], meta, *parts)
    e_other = swap(e_half)
    halo_other = swap(halo)

    mats, tails = [], []
    for layer in range(2):
        w, nodes, turned = call(
            functools.partial(unpack, layer),
            [((3, HALF, LATENT), BF), ((2, HALF, LATENT), BF), ((2, LATENT, HALF), BF)],
            meta, *w_parts, scratch=[pltpu.VMEM((2, HALF, LATENT), BF)], flops=8 * HALF * n * m * (1 - layer),
        )
        mats.append(w)
        tails.append((turned, swap(turned), nodes, swap(nodes)))

    big = lambda r, q: 2 * r * q * LATENT
    v_all, e_all, hid = call(
        edge_first,
        [((LATENT, n), BF), ((LATENT, m), BF), ((HALF, m), BF)],
        meta, v_half, v_other, e_half, e_other, halo, halo_other, mats[0], src, dst,
        scratch=[pltpu.VMEM((HALF, n + m), BF), pltpu.VMEM((HALF, n), BF), pltpu.VMEM((m, LATENT), BF)],
        flops=4 * big(HALF, n + m),
    )
    e_new, v_new, sender, rows = call(
        tail_first,
        [((LATENT, m), BF), ((LATENT, n), BF), ((HALF, n), BF), ((m, HALF), BF)],
        meta, hid, swap(hid), *tails[0], e_all, v_all, dst, mats[1], send,
        flops=6 * big(LATENT, m),
    )
    far = exchange(rows)
    (part,) = call(
        edge_local, [((HALF, m), F32)], meta, v_new, e_new, sender, mats[1], src, dst,
        scratch=[pltpu.VMEM((HALF, n), BF)], flops=3 * big(HALF, m),
    )
    (hid,) = call(
        lambda *refs: edge_far(n, *refs), [((HALF, m), BF)], meta, part, far, src,
        scratch=[pltpu.VMEM((HALF, m), BF)], flops=2 * big(HALF, m),
    )
    e_out, v_out = call(
        tail_last,
        [((64, m), BF), ((64, n), BF)],
        meta, hid, swap(hid), *tails[1], e_new, v_new, dst,
        scratch=[pltpu.VMEM((LATENT, m), BF), pltpu.VMEM((LATENT, n // 2), F32)], flops=5 * big(LATENT, m),
    )
    return v_out, e_out


def solution(mesh):
    in_specs = (
        P("ch", "dom"),
        P("ch", "dom"),
        P("dom"),
        P("dom"),
        P("dom"),
        P(None, None, None, "ch"),
        P(None, "ch", None),
        P(None, None, None, "ch"),
        P(None, "ch", None),
    )
    out_specs = (P("ch", "dom"), P("ch", "dom"))
    return jax.shard_map(shards, mesh=mesh, in_specs=in_specs, out_specs=out_specs, check_vma=False)
```

```python
import functools

import jax
import jax.numpy as jnp
from jax import lax
from jax.experimental import pallas as pl
from jax.experimental.pallas import tpu as pltpu
from jax.sharding import PartitionSpec as P

LATENT = 512
HALF = 256
SLOTS = 32
CHUNK = 512
BF = jnp.bfloat16
F32 = jnp.float32

CORE = [(c, c ^ 1) for c in range(8)]
VMEM = pl.BlockSpec(memory_space=pltpu.VMEM)
SMEM = pl.BlockSpec(memory_space=pltpu.SMEM)


def z_shift(s):
    return [(c, ((c // 2 + s) % 4) * 2 + c % 2) for c in range(8)]


def ring(stage, s):
    pairs = []
    for d in range(32):
        along_x = (d // 4) * 4 + (d + s) % 4
        along_y = (d // 16) * 16 + (d + 4 * s) % 16
        for c in range(8):
            to = along_y if (c % 2 == 0) == (stage == 1) else along_x
            pairs.append((d * 8 + c, to * 8 + c))
    return pairs


def swap(x):
    return lax.ppermute(x, "ch", CORE)


def ring_gather(x, axis, perm):
    half = x.shape[0] // 2
    prev = lax.ppermute(x, axis, perm(1))
    nxt = lax.ppermute(x, axis, perm(3))
    far_a = lax.ppermute(prev[:half], axis, perm(1))
    far_b = lax.ppermute(nxt[half:], axis, perm(3))
    return x, nxt, far_a, far_b, prev


def dot(a, b, ca=1, cb=0):
    return lax.dot_general(a, b, (((ca,), (cb,)), ((), ())), preferred_element_type=F32)


def norm_add(msg, residual, part=None):
    mean = jnp.sum(msg, axis=0, keepdims=True) / LATENT
    var = jnp.sum(msg * msg, axis=0, keepdims=True) / LATENT - mean * mean
    part = msg if part is None else part
    return (residual.astype(F32) + (part - mean) * lax.rsqrt(var + 1e-05)).astype(BF)


def silu(x):
    return (x * jax.nn.sigmoid(x)).astype(BF)


def hot(idx, first, rows):
    where = lax.broadcasted_iota(jnp.int32, (rows, idx.shape[1]), 0) + first == idx
    return where.astype(BF)


def chunks(n, body):
    size = CHUNK if n % CHUNK == 0 else n // 2
    for first in range(0, n, size):
        body(slice(first, first + size), first)


def call(kernel, outs, *args, scratch=(), flops=0, space=VMEM, after=()):
    specs = [SMEM] + [space] * (len(args) - 1) + [pl.BlockSpec(memory_space=pl.ANY)] * len(after)
    moved = sum(a.size * a.dtype.itemsize for a in args)
    inputs = len(args)

    def body(*refs):
        kernel(*refs[:inputs], *refs[inputs + len(after) :])

    return pl.pallas_call(
        body,
        out_shape=[jax.ShapeDtypeStruct(s, d) for s, d in outs],
        in_specs=specs,
        out_specs=[VMEM] * len(outs),
        scratch_shapes=list(scratch),
        compiler_params=pltpu.CompilerParams(vmem_limit_bytes=6 << 20),
        cost_estimate=pl.CostEstimate(flops=flops, bytes_accessed=moved, transcendentals=0),
    )(*args, *after)


def place_half(meta, parts, out, col):
    own, nxt, far_a, far_b, prev = parts
    zi = meta[0]
    at = lambda s: pl.multiple_of(((zi + s) & 3) * 64, 64)
    cols = slice(col, col + out.shape[1])
    out[pl.ds(at(0), 64), :] = own[:, cols]
    out[pl.ds(at(1), 64), :] = nxt[:, cols]
    out[pl.ds(at(2), 32), :] = far_a[:, cols]
    out[pl.ds(at(2) + 32, 32), :] = far_b[:, cols]
    out[pl.ds(at(3), 64), :] = prev[:, cols]


def select_rows(send, x, rows):
    def body(sl, _):
        rows[sl, :] = dot(x, hot(send[:, sl], 0, x.shape[1])).T.astype(BF)

    chunks(rows.shape[0], body)


def send_first(meta, own, nxt, far_a, far_b, prev, send, half, rows):
    place_half(meta, (own, nxt, far_a, far_b, prev), half, 0)
    select_rows(send, half[...], rows)


def gather_edges(meta, own, nxt, far_a, far_b, prev, half):
    place_half(meta, (own, nxt, far_a, far_b, prev), half, own.shape[1] - half.shape[1])


def prepare(meta, w_e, w_eo, w_n, w_no, v, e, piece, both, sem):
    lay = meta[1] >> 1
    rows = pl.ds(pl.multiple_of(8 * ((meta[1] & 1) * 4 + meta[2]), 8), 8)
    n = v.shape[1]
    copies = [
        (w_e.at[lay, :, rows], piece.at[0:3]),
        (w_eo.at[lay, rows], piece.at[3]),
        (w_n.at[lay, :, rows], piece.at[4:6]),
        (w_no.at[lay, rows], piece.at[6]),
        (v, both.at[:, :n]),
        (e, both.at[:, n:]),
    ]
    copies = [pltpu.make_async_copy(a, b, sem.at[i]) for i, (a, b) in enumerate(copies)]
    for copy in copies:
        copy.start()
    for copy in copies:
        copy.wait()


def unpack(layer, meta, own, nxt, far_a, far_b, prev, mats, nodes, turned, outs):
    where = [mats.at[0], mats.at[1], mats.at[2], outs.at[0], nodes.at[0], nodes.at[1], outs.at[1]]
    for s in range(4):
        for r in range(4):
            a = (meta[1] + r) & 3
            at = pl.multiple_of((((meta[2] + s) & 3) * 2 + (a & 1)) * 32, 32)
            ref, row = ((own, r), (nxt, r), (far_a, r) if r < 2 else (far_b, r - 2), (prev, r))[s]

            @pl.when((a >> 1) == layer)
            def _():
                for m in range(7):
                    where[m][pl.ds(at, 32), :] = ref[row, :, m].astype(F32).reshape(32, LATENT).astype(BF)

    turned[0] = outs[0].astype(F32).T.astype(BF)
    turned[1] = outs[1].astype(F32).T.astype(BF)


def interleave(meta, own, other, out):
    for z in range(4):
        out[pl.ds(pl.multiple_of(z * 128 + meta[3] * 64, 64), 64), :] = own[z * 64 : z * 64 + 64]
        out[pl.ds(pl.multiple_of(z * 128 + 64 - meta[3] * 64, 64), 64), :] = other[z * 64 : z * 64 + 64]


def edge_first(meta, v_own, v_other, e_own, e_other, h_own, h_other, mats, src, dst, v_all, e_all, hidden, sender, receiver, halo):
    n = v_all.shape[1]
    interleave(meta, v_own, v_other, v_all)
    interleave(meta, e_own, e_other, e_all)
    swapped = meta[3] == 1
    low = lax.broadcasted_iota(jnp.int32, (halo.shape[0], 128), 1) < 64
    for b in range(2):
        blk = slice(128 * b, 128 * b + 128)
        own, other = h_own[:, blk].astype(F32), h_other[:, blk].astype(F32)
        even = jnp.where(swapped, other, own)
        odd = jnp.where(swapped, own, other)
        halo[:, 256 * b : 256 * b + 128] = jnp.where(low, even, pltpu.roll(odd, 64, 1)).astype(BF)
        halo[:, 256 * b + 128 : 256 * b + 256] = jnp.where(low, pltpu.roll(even, 64, 1), odd).astype(BF)
    sender[:, :n] = dot(mats[1], v_all[...]).astype(BF)
    sender[:, n:] = dot(mats[1], halo[...], 1, 1).astype(BF)
    receiver[...] = dot(mats[2], v_all[...]).astype(BF)

    def body(sl, _):
        pre = dot(mats[0], e_all[:, sl])
        pre += dot(sender[...], hot(src[:, sl], 0, sender.shape[1]))
        pre += dot(receiver[...], hot(dst[:, sl], 0, n))
        hidden[:, sl] = silu(pre)

    chunks(hidden.shape[1], body)


def new_edges(hid, hid_other, turned, turned_other, e_all, e_new):
    def edges(sl, _):
        msg = dot(turned[0], hid[:, sl]) + dot(turned_other[0], hid_other[:, sl])
        e_new[:, sl] = norm_add(msg, e_all[:, sl])

    chunks(e_new.shape[1], edges)


def node_message(first, sl, turned, turned_other, nodes, nodes_other, e_new, dst, local):
    agg = dot(e_new[...], hot(dst[...], first, sl.stop - sl.start), 1, 1).astype(BF)
    msg = dot(turned[1], silu(local(0) + dot(nodes[1], agg)))
    return msg + dot(turned_other[1], silu(local(1) + dot(nodes_other[1], agg)))


def node_local(meta, nodes, nodes_other, v_all, out):
    out[0] = dot(nodes[0], v_all[...])
    out[1] = dot(nodes_other[0], v_all[...])


def tail_first(
    meta, hid, hid_other, turned, turned_other, nodes, nodes_other, e_all, v_all, dst, mats_next, send,
    e_new, v_new, sender, rows,
):
    new_edges(hid, hid_other, turned, turned_other, e_all, e_new)

    def body(sl, first):
        local = lambda i: dot((nodes, nodes_other)[i][0], v_all[:, sl])
        msg = node_message(first, sl, turned, turned_other, nodes, nodes_other, e_new, dst, local)
        v_new[:, sl] = norm_add(msg, v_all[:, sl])

    chunks(v_new.shape[1], body)
    sender[...] = dot(mats_next[1], v_new[...]).astype(BF)
    select_rows(send, sender[...], rows)


def tail_last(
    meta, hid, hid_other, turned, turned_other, nodes, nodes_other, e_all, v_all, dst, local,
    e_out, v_out, e_new, sums,
):
    new_edges(hid, hid_other, turned, turned_other, e_all, e_new)
    mine = pl.ds(pl.multiple_of(meta[4] * 64, 64), 64)
    e_out[...] = e_new[mine, :]

    def body(sl, first):
        msg = node_message(first, sl, turned, turned_other, nodes, nodes_other, e_new, dst, lambda i: local[i, :, sl])
        sums[...] = msg
        v_out[:, sl] = norm_add(msg, v_all[mine, sl], sums[mine, :])

    chunks(v_out.shape[1], body)


def edge_local(meta, v_all, e_all, sender, mats, src, dst, part, receiver):
    n = v_all.shape[1]
    receiver[...] = dot(mats[2], v_all[...]).astype(BF)

    def body(sl, _):
        pre = dot(mats[0], e_all[:, sl])
        pre += dot(sender[...], hot(src[:, sl], 0, n))
        part[:, sl] = pre + dot(receiver[...], hot(dst[:, sl], 0, n))

    chunks(part.shape[1], body)


def edge_far(n, meta, part, rows, src, hidden, far):
    far[...] = rows[...].astype(F32).T.astype(BF)

    def body(sl, _):
        hidden[:, sl] = silu(part[:, sl] + dot(far[...], hot(src[:, sl], n, far.shape[1])))

    chunks(hidden.shape[1], body)


def shards(node_feats, edge_feats, send_rows, edge_src, edge_dst, w_edge_in, w_edge_out, w_node_in, w_node_out):
    d = lax.axis_index("dom")
    c = lax.axis_index("ch")
    k = c & 1
    y, x = (d >> 2) & 3, d & 3
    n = node_feats.shape[1]
    m = edge_feats.shape[1]
    first = jnp.where(k == 0, y, x)
    second = jnp.where(k == 0, x, y)
    meta = jnp.stack([c >> 1, first, second, k, c]).astype(jnp.int32)
    send, src, dst = (a.reshape(1, -1) for a in (send_rows, edge_src, edge_dst))

    shared = (jnp.swapaxes(w_edge_in, 2, 3), w_edge_out, jnp.swapaxes(w_node_in, 2, 3), w_node_out, node_feats, edge_feats)
    piece, both = call(
        prepare,
        [((7, 8, LATENT), BF), ((64, n + m), BF)],
        meta, *(pltpu.with_memory_space_constraint(a, pltpu.HBM) for a in shared),
        scratch=[pltpu.SemaphoreType.DMA((6,))], space=pl.BlockSpec(memory_space=pltpu.HBM),
    )
    pieces = [piece] + [lax.ppermute(piece, "ch", z_shift(s)) for s in (2, 1, 3)]
    both = lax.optimization_barrier((both, pieces[1]))[0]
    wz = jnp.stack(pieces)
    parts = ring_gather(both, "ch", z_shift)
    far, nxt, prev = (lax.ppermute(wz, ("dom", "ch"), ring(1, s)) for s in (2, 3, 1))
    quarters = [wz, nxt, far, prev]
    quarters[0] = lax.optimization_barrier((wz, parts[1], parts[4]))[0]
    one = jnp.stack(quarters)
    w_parts = ring_gather(one, ("dom", "ch"), lambda s: ring(2, s))

    v_half, rows = call(
        send_first, [((HALF, n), BF), ((m, HALF), BF)], meta, *parts, send, flops=2 * HALF * n * m
    )

    def exchange(rows):
        return lax.all_to_all(rows.reshape(32, SLOTS, HALF), "dom", 0, 0, tiled=True).reshape(-1, HALF)

    halo = exchange(lax.optimization_barrier((rows, w_parts[1], w_parts[4]))[0])
    v_other = swap(v_half)
    (e_half,) = call(gather_edges, [((HALF, m), BF)], meta, *parts)
    e_other = swap(e_half)
    halo_other = swap(halo)

    mats, tails = [], []
    for layer in range(2):
        w, nodes, turned = call(
            functools.partial(unpack, layer),
            [((3, HALF, LATENT), BF), ((2, HALF, LATENT), BF), ((2, LATENT, HALF), BF)],
            meta, *w_parts, scratch=[pltpu.VMEM((2, HALF, LATENT), BF)], flops=8 * HALF * n * m * (1 - layer),
        )
        mats.append(w)
        tails.append((turned, swap(turned), nodes, swap(nodes)))

    big = lambda r, q: 2 * r * q * LATENT
    v_all, e_all, hid = call(
        edge_first,
        [((LATENT, n), BF), ((LATENT, m), BF), ((HALF, m), BF)],
        meta, v_half, v_other, e_half, e_other, halo, halo_other, mats[0], src, dst,
        scratch=[pltpu.VMEM((HALF, n + m), BF), pltpu.VMEM((HALF, n), BF), pltpu.VMEM((m, LATENT), BF)],
        flops=4 * big(HALF, n + m),
    )
    e_new, v_new, sender, rows = call(
        tail_first,
        [((LATENT, m), BF), ((LATENT, n), BF), ((HALF, n), BF), ((m, HALF), BF)],
        meta, hid, swap(hid), *tails[0], e_all, v_all, dst, mats[1], send,
        flops=6 * big(LATENT, m),
    )
    far = exchange(rows)
    (part,) = call(
        edge_local, [((HALF, m), F32)], meta, v_new, e_new, sender, mats[1], src, dst,
        scratch=[pltpu.VMEM((HALF, n), BF)], flops=3 * big(HALF, m),
    )
    (local,) = call(node_local, [((2, HALF, n), F32)], meta, tails[1][2], tails[1][3], v_new, flops=2 * big(HALF, n))
    (hid,) = call(
        lambda *refs: edge_far(n, *refs), [((HALF, m), BF)], meta, part, far, src,
        scratch=[pltpu.VMEM((HALF, m), BF)], flops=2 * big(HALF, m),
    )
    e_out, v_out = call(
        tail_last,
        [((64, m), BF), ((64, n), BF)],
        meta, hid, swap(hid), *tails[1], e_new, v_new, dst, local,
        scratch=[pltpu.VMEM((LATENT, m), BF), pltpu.VMEM((LATENT, n // 2), F32)], flops=5 * big(LATENT, m),
    )
    return v_out, e_out


def solution(mesh):
    in_specs = (
        P("ch", "dom"),
        P("ch", "dom"),
        P("dom"),
        P("dom"),
        P("dom"),
        P(None, None, None, "ch"),
        P(None, "ch", None),
        P(None, None, None, "ch"),
        P(None, "ch", None),
    )
    out_specs = (P("ch", "dom"), P("ch", "dom"))
    return jax.shard_map(shards, mesh=mesh, in_specs=in_specs, out_specs=out_specs, check_vma=False)
```

```python
import functools

import jax
import jax.numpy as jnp
from jax import lax
from jax.experimental import pallas as pl
from jax.experimental.pallas import tpu as pltpu
from jax.sharding import PartitionSpec as P

LATENT = 512
HALF = 256
SLOTS = 32
CHUNK = 512
BF = jnp.bfloat16
F32 = jnp.float32

CORE = [(c, c ^ 1) for c in range(8)]
VMEM = pl.BlockSpec(memory_space=pltpu.VMEM)
SMEM = pl.BlockSpec(memory_space=pltpu.SMEM)
HBM = pl.BlockSpec(memory_space=pltpu.HBM)


def z_shift(s):
    return [(c, ((c // 2 + s) % 4) * 2 + c % 2) for c in range(8)]


def ring(stage, s):
    pairs = []
    for d in range(32):
        along_x = (d // 4) * 4 + (d + s) % 4
        along_y = (d // 16) * 16 + (d + 4 * s) % 16
        for c in range(8):
            to = along_y if (c % 2 == 0) == (stage == 1) else along_x
            pairs.append((d * 8 + c, to * 8 + c))
    return pairs


def swap(x):
    return lax.ppermute(x, "ch", CORE)


def ring_gather(x, axis, perm):
    half = x.shape[0] // 2
    prev = lax.ppermute(x, axis, perm(1))
    nxt = lax.ppermute(x, axis, perm(3))
    far_a = lax.ppermute(prev[:half], axis, perm(1))
    far_b = lax.ppermute(nxt[half:], axis, perm(3))
    return x, nxt, far_a, far_b, prev


def dot(a, b, ca=1, cb=0):
    return lax.dot_general(a, b, (((ca,), (cb,)), ((), ())), preferred_element_type=F32)


def norm_add(msg, residual, part=None):
    mean = jnp.sum(msg, axis=0, keepdims=True) / LATENT
    var = jnp.sum(msg * msg, axis=0, keepdims=True) / LATENT - mean * mean
    part = msg if part is None else part
    return (residual.astype(F32) + (part - mean) * lax.rsqrt(var + 1e-05)).astype(BF)


def silu(x):
    return (x * jax.nn.sigmoid(x)).astype(BF)


def hot(idx, first, rows):
    where = lax.broadcasted_iota(jnp.int32, (rows, idx.shape[1]), 0) + first == idx
    return where.astype(BF)


def chunks(n, body):
    size = CHUNK if n % CHUNK == 0 else n // 2
    for first in range(0, n, size):
        body(slice(first, first + size), first)


def call(kernel, outs, *args, scratch=(), flops=0, space=VMEM, after=()):
    specs = [SMEM] + [space] * (len(args) - 1) + [pl.BlockSpec(memory_space=pl.ANY)] * len(after)
    moved = sum(a.size * a.dtype.itemsize for a in args)
    inputs = len(args)

    def body(*refs):
        kernel(*refs[:inputs], *refs[inputs + len(after) :])

    return pl.pallas_call(
        body,
        out_shape=[o if isinstance(o, pl.MemoryRef) else jax.ShapeDtypeStruct(*o) for o in outs],
        in_specs=specs,
        out_specs=[HBM if isinstance(o, pl.MemoryRef) else VMEM for o in outs],
        scratch_shapes=list(scratch),
        compiler_params=pltpu.CompilerParams(vmem_limit_bytes=6 << 20),
        cost_estimate=pl.CostEstimate(flops=flops, bytes_accessed=moved, transcendentals=0),
    )(*args, *after)


def place_half(meta, parts, out, col):
    own, nxt, far_a, far_b, prev = parts
    zi = meta[0]
    at = lambda s: pl.multiple_of(((zi + s) & 3) * 64, 64)
    cols = slice(col, col + out.shape[1])
    out[pl.ds(at(0), 64), :] = own[:, cols]
    out[pl.ds(at(1), 64), :] = nxt[:, cols]
    out[pl.ds(at(2), 32), :] = far_a[:, cols]
    out[pl.ds(at(2) + 32, 32), :] = far_b[:, cols]
    out[pl.ds(at(3), 64), :] = prev[:, cols]


def select_rows(send, x, rows, held, sem):
    size = rows.shape[0] // 4
    copies = []
    for i in range(4):
        sl = slice(i * size, i * size + size)
        held[sl, :] = dot(x, hot(send[:, sl], 0, x.shape[1])).T.astype(BF)
        copies.append(pltpu.make_async_copy(held.at[sl], rows.at[sl], sem.at[i]))
        copies[-1].start()
    for copy in copies:
        copy.wait()


def send_first(meta, own, nxt, far_a, far_b, prev, send, half, rows, held, sem):
    place_half(meta, (own, nxt, far_a, far_b, prev), half, 0)
    select_rows(send, half[...], rows, held, sem)


def gather_edges(meta, own, nxt, far_a, far_b, prev, half):
    place_half(meta, (own, nxt, far_a, far_b, prev), half, own.shape[1] - half.shape[1])


def prepare(meta, w_e, w_eo, w_n, w_no, v, e, piece, both, sem):
    lay = meta[1] >> 1
    rows = pl.ds(pl.multiple_of(8 * ((meta[1] & 1) * 4 + meta[2]), 8), 8)
    n = v.shape[1]
    copies = [
        (w_e.at[lay, :, rows], piece.at[0:3]),
        (w_eo.at[lay, rows], piece.at[3]),
        (w_n.at[lay, :, rows], piece.at[4:6]),
        (w_no.at[lay, rows], piece.at[6]),
        (v, both.at[:, :n]),
        (e, both.at[:, n:]),
    ]
    copies = [pltpu.make_async_copy(a, b, sem.at[i]) for i, (a, b) in enumerate(copies)]
    for copy in copies:
        copy.start()
    for copy in copies:
        copy.wait()


def unpack(layer, meta, own, nxt, far_a, far_b, prev, mats, nodes, turned, outs):
    where = [mats.at[0], mats.at[1], mats.at[2], outs.at[0], nodes.at[0], nodes.at[1], outs.at[1]]
    for s in range(4):
        for r in range(4):
            a = (meta[1] + r) & 3
            at = pl.multiple_of((((meta[2] + s) & 3) * 2 + (a & 1)) * 32, 32)
            ref, row = ((own, r), (nxt, r), (far_a, r) if r < 2 else (far_b, r - 2), (prev, r))[s]

            @pl.when((a >> 1) == layer)
            def _():
                for m in range(7):
                    where[m][pl.ds(at, 32), :] = ref[row, :, m].astype(F32).reshape(32, LATENT).astype(BF)

    turned[0] = outs[0].astype(F32).T.astype(BF)
    turned[1] = outs[1].astype(F32).T.astype(BF)


def interleave(meta, own, other, out):
    for z in range(4):
        out[pl.ds(pl.multiple_of(z * 128 + meta[3] * 64, 64), 64), :] = own[z * 64 : z * 64 + 64]
        out[pl.ds(pl.multiple_of(z * 128 + 64 - meta[3] * 64, 64), 64), :] = other[z * 64 : z * 64 + 64]


def edge_first(meta, v_own, v_other, e_own, e_other, h_own, h_other, mats, src, dst, v_all, e_all, hidden, sender, receiver, halo):
    n = v_all.shape[1]
    interleave(meta, v_own, v_other, v_all)
    interleave(meta, e_own, e_other, e_all)
    swapped = meta[3] == 1
    low = lax.broadcasted_iota(jnp.int32, (halo.shape[0], 128), 1) < 64
    for b in range(2):
        blk = slice(128 * b, 128 * b + 128)
        own, other = h_own[:, blk].astype(F32), h_other[:, blk].astype(F32)
        even = jnp.where(swapped, other, own)
        odd = jnp.where(swapped, own, other)
        halo[:, 256 * b : 256 * b + 128] = jnp.where(low, even, pltpu.roll(odd, 64, 1)).astype(BF)
        halo[:, 256 * b + 128 : 256 * b + 256] = jnp.where(low, pltpu.roll(even, 64, 1), odd).astype(BF)
    sender[:, :n] = dot(mats[1], v_all[...]).astype(BF)
    sender[:, n:] = dot(mats[1], halo[...], 1, 1).astype(BF)
    receiver[...] = dot(mats[2], v_all[...]).astype(BF)

    def body(sl, _):
        pre = dot(mats[0], e_all[:, sl])
        pre += dot(sender[...], hot(src[:, sl], 0, sender.shape[1]))
        pre += dot(receiver[...], hot(dst[:, sl], 0, n))
        hidden[:, sl] = silu(pre)

    chunks(hidden.shape[1], body)


def new_edges(hid, hid_other, turned, turned_other, e_all, e_new):
    def edges(sl, _):
        msg = dot(turned[0], hid[:, sl]) + dot(turned_other[0], hid_other[:, sl])
        e_new[:, sl] = norm_add(msg, e_all[:, sl])

    chunks(e_new.shape[1], edges)


def node_message(first, sl, turned, turned_other, nodes, nodes_other, e_new, dst, local):
    agg = dot(e_new[...], hot(dst[...], first, sl.stop - sl.start), 1, 1).astype(BF)
    msg = dot(turned[1], silu(local(0) + dot(nodes[1], agg)))
    return msg + dot(turned_other[1], silu(local(1) + dot(nodes_other[1], agg)))


def node_local(meta, nodes, nodes_other, v_all, out):
    out[0] = dot(nodes[0], v_all[...])
    out[1] = dot(nodes_other[0], v_all[...])


def tail_first(
    meta, hid, hid_other, turned, turned_other, nodes, nodes_other, e_all, v_all, dst, mats_next, send,
    e_new, v_new, rows, sender, held, sem,
):
    new_edges(hid, hid_other, turned, turned_other, e_all, e_new)

    def body(sl, first):
        local = lambda i: dot((nodes, nodes_other)[i][0], v_all[:, sl])
        msg = node_message(first, sl, turned, turned_other, nodes, nodes_other, e_new, dst, local)
        v_new[:, sl] = norm_add(msg, v_all[:, sl])

    chunks(v_new.shape[1], body)
    sender[...] = dot(mats_next[1], v_new[...]).astype(BF)
    select_rows(send, sender[...], rows, held, sem)


def tail_last(
    meta, hid, hid_other, turned, turned_other, nodes, nodes_other, e_all, v_all, dst, local,
    e_out, v_out, e_new, sums,
):
    new_edges(hid, hid_other, turned, turned_other, e_all, e_new)
    mine = pl.ds(pl.multiple_of(meta[4] * 64, 64), 64)
    e_out[...] = e_new[mine, :]

    def body(sl, first):
        msg = node_message(first, sl, turned, turned_other, nodes, nodes_other, e_new, dst, lambda i: local[i, :, sl])
        sums[...] = msg
        v_out[:, sl] = norm_add(msg, v_all[mine, sl], sums[mine, :])

    chunks(v_out.shape[1], body)


def edge_local(meta, v_all, e_all, mats, src, dst, part, sender, receiver):
    n = v_all.shape[1]
    sender[...] = dot(mats[1], v_all[...]).astype(BF)
    receiver[...] = dot(mats[2], v_all[...]).astype(BF)

    def body(sl, _):
        pre = dot(mats[0], e_all[:, sl])
        pre += dot(sender[...], hot(src[:, sl], 0, n))
        part[:, sl] = pre + dot(receiver[...], hot(dst[:, sl], 0, n))

    chunks(part.shape[1], body)


def edge_far(n, meta, part, rows, src, hidden, far):
    far[...] = rows[...].astype(F32).T.astype(BF)

    def body(sl, _):
        hidden[:, sl] = silu(part[:, sl] + dot(far[...], hot(src[:, sl], n, far.shape[1])))

    chunks(hidden.shape[1], body)


def shards(node_feats, edge_feats, send_rows, edge_src, edge_dst, w_edge_in, w_edge_out, w_node_in, w_node_out):
    d = lax.axis_index("dom")
    c = lax.axis_index("ch")
    k = c & 1
    y, x = (d >> 2) & 3, d & 3
    n = node_feats.shape[1]
    m = edge_feats.shape[1]
    first = jnp.where(k == 0, y, x)
    second = jnp.where(k == 0, x, y)
    meta = jnp.stack([c >> 1, first, second, k, c]).astype(jnp.int32)
    send, src, dst = (a.reshape(1, -1) for a in (send_rows, edge_src, edge_dst))

    shared = (jnp.swapaxes(w_edge_in, 2, 3), w_edge_out, jnp.swapaxes(w_node_in, 2, 3), w_node_out, node_feats, edge_feats)
    piece, both = call(
        prepare,
        [((7, 8, LATENT), BF), ((64, n + m), BF)],
        meta, *(pltpu.with_memory_space_constraint(a, pltpu.HBM) for a in shared),
        scratch=[pltpu.SemaphoreType.DMA((6,))], space=HBM,
    )
    pieces = [piece] + [lax.ppermute(piece, "ch", z_shift(s)) for s in (2, 1, 3)]
    both = lax.optimization_barrier((both, pieces[1]))[0]
    wz = jnp.stack(pieces)
    parts = ring_gather(both, "ch", z_shift)
    far, nxt, prev = (lax.ppermute(wz, ("dom", "ch"), ring(1, s)) for s in (2, 3, 1))
    quarters = [wz, nxt, far, prev]
    quarters[0] = lax.optimization_barrier((wz, parts[1], parts[4]))[0]
    one = jnp.stack(quarters)
    w_parts = ring_gather(one, ("dom", "ch"), lambda s: ring(2, s))

    v_half, rows = call(
        send_first, [((HALF, n), BF), pltpu.HBM((m, HALF), BF)], meta, *parts, send,
        scratch=[pltpu.VMEM((m, HALF), BF), pltpu.SemaphoreType.DMA((4,))], flops=2 * HALF * n * m,
    )

    def exchange(rows):
        return lax.all_to_all(rows.reshape(32, SLOTS, HALF), "dom", 0, 0, tiled=True).reshape(-1, HALF)

    halo = exchange(lax.optimization_barrier((rows, w_parts[1], w_parts[4]))[0])
    v_other = swap(v_half)
    (e_half,) = call(gather_edges, [((HALF, m), BF)], meta, *parts)
    e_other = swap(e_half)
    halo_other = swap(halo)

    mats, tails = [], []
    for layer in range(2):
        w, nodes, turned = call(
            functools.partial(unpack, layer),
            [((3, HALF, LATENT), BF), ((2, HALF, LATENT), BF), ((2, LATENT, HALF), BF)],
            meta, *w_parts, scratch=[pltpu.VMEM((2, HALF, LATENT), BF)], flops=8 * HALF * n * m * (1 - layer),
        )
        mats.append(w)
        tails.append((turned, swap(turned), nodes, swap(nodes)))

    big = lambda r, q: 2 * r * q * LATENT
    v_all, e_all, hid = call(
        edge_first,
        [((LATENT, n), BF), ((LATENT, m), BF), ((HALF, m), BF)],
        meta, v_half, v_other, e_half, e_other, halo, halo_other, mats[0], src, dst,
        scratch=[pltpu.VMEM((HALF, n + m), BF), pltpu.VMEM((HALF, n), BF), pltpu.VMEM((m, LATENT), BF)],
        flops=4 * big(HALF, n + m),
    )
    e_new, v_new, rows = call(
        tail_first,
        [((LATENT, m), BF), ((LATENT, n), BF), pltpu.HBM((m, HALF), BF)],
        meta, hid, swap(hid), *tails[0], e_all, v_all, dst, mats[1], send,
        scratch=[pltpu.VMEM((HALF, n), BF), pltpu.VMEM((m, HALF), BF), pltpu.SemaphoreType.DMA((4,))], flops=6 * big(LATENT, m),
    )
    far = exchange(rows)
    (part,) = call(
        edge_local, [((HALF, m), F32)], meta, v_new, e_new, mats[1], src, dst,
        scratch=[pltpu.VMEM((HALF, n), BF)] * 2, flops=3 * big(HALF, m),
    )
    (local,) = call(node_local, [((2, HALF, n), F32)], meta, tails[1][2], tails[1][3], v_new, flops=2 * big(HALF, n))
    (hid,) = call(
        lambda *refs: edge_far(n, *refs), [((HALF, m), BF)], meta, part, far, src,
        scratch=[pltpu.VMEM((HALF, m), BF)], flops=2 * big(HALF, m),
    )
    e_out, v_out = call(
        tail_last,
        [((64, m), BF), ((64, n), BF)],
        meta, hid, swap(hid), *tails[1], e_new, v_new, dst, local,
        scratch=[pltpu.VMEM((LATENT, m), BF), pltpu.VMEM((LATENT, n // 2), F32)], flops=5 * big(LATENT, m),
    )
    return v_out, e_out


def solution(mesh):
    in_specs = (
        P("ch", "dom"),
        P("ch", "dom"),
        P("dom"),
        P("dom"),
        P("dom"),
        P(None, None, None, "ch"),
        P(None, "ch", None),
        P(None, None, None, "ch"),
        P(None, "ch", None),
    )
    out_specs = (P("ch", "dom"), P("ch", "dom"))
    return jax.shard_map(shards, mesh=mesh, in_specs=in_specs, out_specs=out_specs, check_vma=False)
```

```python
import functools

import jax
import jax.numpy as jnp
from jax import lax
from jax.experimental import pallas as pl
from jax.experimental.pallas import tpu as pltpu
from jax.sharding import PartitionSpec as P

LATENT = 512
HALF = 256
SLOTS = 32
CHUNK = 512
BF = jnp.bfloat16
F32 = jnp.float32

CORE = [(c, c ^ 1) for c in range(8)]
VMEM = pl.BlockSpec(memory_space=pltpu.VMEM)
SMEM = pl.BlockSpec(memory_space=pltpu.SMEM)
HBM = pl.BlockSpec(memory_space=pltpu.HBM)


def z_shift(s):
    return [(c, ((c // 2 + s) % 4) * 2 + c % 2) for c in range(8)]


def ring(stage, s):
    pairs = []
    for d in range(32):
        along_x = (d // 4) * 4 + (d + s) % 4
        along_y = (d // 16) * 16 + (d + 4 * s) % 16
        for c in range(8):
            to = along_y if (c % 2 == 0) == (stage == 1) else along_x
            pairs.append((d * 8 + c, to * 8 + c))
    return pairs


def swap(x):
    return lax.ppermute(x, "ch", CORE)


def ring_gather(x, axis, perm):
    half = x.shape[0] // 2
    prev = lax.ppermute(x, axis, perm(1))
    nxt = lax.ppermute(x, axis, perm(3))
    far_a = lax.ppermute(prev[:half], axis, perm(1))
    far_b = lax.ppermute(nxt[half:], axis, perm(3))
    return x, nxt, far_a, far_b, prev


def dot(a, b, ca=1, cb=0):
    return lax.dot_general(a, b, (((ca,), (cb,)), ((), ())), preferred_element_type=F32)


def norm_add(msg, residual, part=None):
    mean = jnp.sum(msg, axis=0, keepdims=True) / LATENT
    var = jnp.sum(msg * msg, axis=0, keepdims=True) / LATENT - mean * mean
    part = msg if part is None else part
    return (residual.astype(F32) + (part - mean) * lax.rsqrt(var + 1e-05)).astype(BF)


def silu(x):
    return (x * jax.nn.sigmoid(x)).astype(BF)


def hot(idx, first, rows):
    where = lax.broadcasted_iota(jnp.int32, (rows, idx.shape[1]), 0) + first == idx
    return where.astype(BF)


def chunks(n, body):
    size = CHUNK if n % CHUNK == 0 else n // 2
    for first in range(0, n, size):
        body(slice(first, first + size), first)


def call(kernel, outs, *args, scratch=(), flops=0, space=VMEM, after=()):
    specs = [SMEM] + [space] * (len(args) - 1) + [pl.BlockSpec(memory_space=pl.ANY)] * len(after)
    moved = sum(a.size * a.dtype.itemsize for a in args)
    inputs = len(args)

    def body(*refs):
        kernel(*refs[:inputs], *refs[inputs + len(after) :])

    return pl.pallas_call(
        body,
        out_shape=[o if isinstance(o, pl.MemoryRef) else jax.ShapeDtypeStruct(*o) for o in outs],
        in_specs=specs,
        out_specs=[HBM if isinstance(o, pl.MemoryRef) else VMEM for o in outs],
        scratch_shapes=list(scratch),
        compiler_params=pltpu.CompilerParams(vmem_limit_bytes=6 << 20),
        cost_estimate=pl.CostEstimate(flops=flops, bytes_accessed=moved, transcendentals=0),
    )(*args, *after)


def place_half(meta, parts, out, col):
    own, nxt, far_a, far_b, prev = parts
    zi = meta[0]
    at = lambda s: pl.multiple_of(((zi + s) & 3) * 64, 64)
    cols = slice(col, col + out.shape[1])
    out[pl.ds(at(0), 64), :] = own[:, cols]
    out[pl.ds(at(1), 64), :] = nxt[:, cols]
    out[pl.ds(at(2), 32), :] = far_a[:, cols]
    out[pl.ds(at(2) + 32, 32), :] = far_b[:, cols]
    out[pl.ds(at(3), 64), :] = prev[:, cols]


def select_rows(send, x, rows, held, sem):
    size = rows.shape[0] // 4
    copies = []
    for i in range(4):
        sl = slice(i * size, i * size + size)
        held[sl, :] = dot(x, hot(send[:, sl], 0, x.shape[1])).T.astype(BF)
        copies.append(pltpu.make_async_copy(held.at[sl], rows.at[sl], sem.at[i]))
        copies[-1].start()
    for copy in copies:
        copy.wait()


def send_first(meta, own, nxt, far_a, far_b, prev, send, half, rows, held, sem):
    place_half(meta, (own, nxt, far_a, far_b, prev), half, 0)
    select_rows(send, half[...], rows, held, sem)


def gather_edges(meta, own, nxt, far_a, far_b, prev, half):
    place_half(meta, (own, nxt, far_a, far_b, prev), half, own.shape[1] - half.shape[1])


def prepare(meta, w_e, w_eo, w_n, w_no, v, e, piece, both, sem):
    lay = meta[1] >> 1
    rows = pl.ds(pl.multiple_of(8 * ((meta[1] & 1) * 4 + meta[2]), 8), 8)
    n = v.shape[1]
    copies = [
        (w_e.at[lay, :, rows], piece.at[0:3]),
        (w_eo.at[lay, rows], piece.at[3]),
        (w_n.at[lay, :, rows], piece.at[4:6]),
        (w_no.at[lay, rows], piece.at[6]),
        (v, both.at[:, :n]),
        (e, both.at[:, n:]),
    ]
    copies = [pltpu.make_async_copy(a, b, sem.at[i]) for i, (a, b) in enumerate(copies)]
    for copy in copies:
        copy.start()
    for copy in copies:
        copy.wait()


def place_rows(layer, meta, parts, where):
    own, nxt, far_a, far_b, prev = parts
    for s in range(4):
        for r in range(4):
            a = (meta[1] + r) & 3
            at = pl.multiple_of((((meta[2] + s) & 3) * 2 + (a & 1)) * 32, 32)
            ref, row = ((own, r), (nxt, r), (far_a, r) if r < 2 else (far_b, r - 2), (prev, r))[s]

            @pl.when((a >> 1) == layer)
            def _():
                for m, out in where:
                    out[pl.ds(at, 32), :] = ref[row, :, m].astype(F32).reshape(32, LATENT).astype(BF)


def unpack(layer, meta, own, nxt, far_a, far_b, prev, mats, nodes, turned, outs):
    tail = [(3, outs.at[0]), (4, nodes.at[0]), (5, nodes.at[1]), (6, outs.at[1])]
    place_rows(layer, meta, (own, nxt, far_a, far_b, prev), [(i, mats.at[i]) for i in range(3)] + tail)
    turned[0] = outs[0].astype(F32).T.astype(BF)
    turned[1] = outs[1].astype(F32).T.astype(BF)


def unpack_edges(layer, meta, own, nxt, far_a, far_b, prev, mats):
    place_rows(layer, meta, (own, nxt, far_a, far_b, prev), [(i, mats.at[i]) for i in range(3)])


def unpack_tail(layer, meta, own, nxt, far_a, far_b, prev, nodes, turned, outs):
    tail = [(3, outs.at[0]), (4, nodes.at[0]), (5, nodes.at[1]), (6, outs.at[1])]
    place_rows(layer, meta, (own, nxt, far_a, far_b, prev), tail)
    turned[0] = outs[0].astype(F32).T.astype(BF)
    turned[1] = outs[1].astype(F32).T.astype(BF)


def interleave(meta, own, other, out):
    for z in range(4):
        out[pl.ds(pl.multiple_of(z * 128 + meta[3] * 64, 64), 64), :] = own[z * 64 : z * 64 + 64]
        out[pl.ds(pl.multiple_of(z * 128 + 64 - meta[3] * 64, 64), 64), :] = other[z * 64 : z * 64 + 64]


def edge_first(meta, v_own, v_other, e_own, e_other, h_own, h_other, mats, src, dst, v_all, e_all, hidden, sender, receiver, halo):
    n = v_all.shape[1]
    interleave(meta, v_own, v_other, v_all)
    interleave(meta, e_own, e_other, e_all)
    swapped = meta[3] == 1
    low = lax.broadcasted_iota(jnp.int32, (halo.shape[0], 128), 1) < 64
    for b in range(2):
        blk = slice(128 * b, 128 * b + 128)
        own, other = h_own[:, blk].astype(F32), h_other[:, blk].astype(F32)
        even = jnp.where(swapped, other, own)
        odd = jnp.where(swapped, own, other)
        halo[:, 256 * b : 256 * b + 128] = jnp.where(low, even, pltpu.roll(odd, 64, 1)).astype(BF)
        halo[:, 256 * b + 128 : 256 * b + 256] = jnp.where(low, pltpu.roll(even, 64, 1), odd).astype(BF)
    sender[:, :n] = dot(mats[1], v_all[...]).astype(BF)
    sender[:, n:] = dot(mats[1], halo[...], 1, 1).astype(BF)
    receiver[...] = dot(mats[2], v_all[...]).astype(BF)

    def body(sl, _):
        pre = dot(mats[0], e_all[:, sl])
        pre += dot(sender[...], hot(src[:, sl], 0, sender.shape[1]))
        pre += dot(receiver[...], hot(dst[:, sl], 0, n))
        hidden[:, sl] = silu(pre)

    chunks(hidden.shape[1], body)


def new_edges(hid, hid_other, turned, turned_other, e_all, e_new):
    def edges(sl, _):
        msg = dot(turned[0], hid[:, sl]) + dot(turned_other[0], hid_other[:, sl])
        e_new[:, sl] = norm_add(msg, e_all[:, sl])

    chunks(e_new.shape[1], edges)


def node_message(first, sl, turned, turned_other, nodes, nodes_other, e_new, dst, local):
    agg = dot(e_new[...], hot(dst[...], first, sl.stop - sl.start), 1, 1).astype(BF)
    msg = dot(turned[1], silu(local(0) + dot(nodes[1], agg)))
    return msg + dot(turned_other[1], silu(local(1) + dot(nodes_other[1], agg)))


def node_local(meta, nodes, nodes_other, v_all, out):
    out[0] = dot(nodes[0], v_all[...])
    out[1] = dot(nodes_other[0], v_all[...])


def tail_first(
    meta, hid, hid_other, turned, turned_other, nodes, nodes_other, e_all, v_all, dst, mats_next, send,
    e_out, v_out, rows, e_new, v_new, sender, held, sem,
):
    new_edges(hid, hid_other, turned, turned_other, e_all, e_new)
    copies = [pltpu.make_async_copy(e_new, e_out, sem.at[4])]
    copies[0].start()

    def body(sl, first):
        local = lambda i: dot((nodes, nodes_other)[i][0], v_all[:, sl])
        msg = node_message(first, sl, turned, turned_other, nodes, nodes_other, e_new, dst, local)
        v_new[:, sl] = norm_add(msg, v_all[:, sl])

    chunks(v_new.shape[1], body)
    copies.append(pltpu.make_async_copy(v_new, v_out, sem.at[5]))
    copies[1].start()
    sender[...] = dot(mats_next[1], v_new[...]).astype(BF)
    select_rows(send, sender[...], rows, held, sem)
    for copy in copies:
        copy.wait()


def tail_last(
    meta, hid, hid_other, turned, turned_other, nodes, nodes_other, e_all, v_all, dst, local,
    e_out, v_out, e_new, sums, held, sem,
):
    new_edges(hid, hid_other, turned, turned_other, e_all, e_new)
    mine = pl.ds(pl.multiple_of(meta[4] * 64, 64), 64)
    copies = [pltpu.make_async_copy(e_new.at[mine, :], e_out, sem.at[0])]
    copies[0].start()

    def body(sl, first):
        msg = node_message(first, sl, turned, turned_other, nodes, nodes_other, e_new, dst, lambda i: local[i, :, sl])
        sums[...] = msg
        held[:, sl] = norm_add(msg, v_all[mine, sl], sums[mine, :])
        copies.append(pltpu.make_async_copy(held.at[:, sl], v_out.at[:, sl], sem.at[len(copies)]))
        copies[-1].start()

    chunks(v_out.shape[1], body)
    for copy in copies:
        copy.wait()


def edge_local(meta, v_all, e_all, mats, src, dst, part, sender, receiver):
    n = v_all.shape[1]
    sender[...] = dot(mats[1], v_all[...]).astype(BF)
    receiver[...] = dot(mats[2], v_all[...]).astype(BF)

    def body(sl, _):
        pre = dot(mats[0], e_all[:, sl])
        pre += dot(sender[...], hot(src[:, sl], 0, n))
        part[:, sl] = pre + dot(receiver[...], hot(dst[:, sl], 0, n))

    chunks(part.shape[1], body)


def edge_far(n, meta, part, rows, src, hidden, far):
    far[...] = rows[...].astype(F32).T.astype(BF)

    def body(sl, _):
        hidden[:, sl] = silu(part[:, sl] + dot(far[...], hot(src[:, sl], n, far.shape[1])))

    chunks(hidden.shape[1], body)


def shards(node_feats, edge_feats, send_rows, edge_src, edge_dst, w_edge_in, w_edge_out, w_node_in, w_node_out):
    d = lax.axis_index("dom")
    c = lax.axis_index("ch")
    k = c & 1
    y, x = (d >> 2) & 3, d & 3
    n = node_feats.shape[1]
    m = edge_feats.shape[1]
    first = jnp.where(k == 0, y, x)
    second = jnp.where(k == 0, x, y)
    meta = jnp.stack([c >> 1, first, second, k, c]).astype(jnp.int32)
    send, src, dst = (a.reshape(1, -1) for a in (send_rows, edge_src, edge_dst))

    shared = (jnp.swapaxes(w_edge_in, 2, 3), w_edge_out, jnp.swapaxes(w_node_in, 2, 3), w_node_out, node_feats, edge_feats)
    piece, both = call(
        prepare,
        [((7, 8, LATENT), BF), ((64, n + m), BF)],
        meta, *(pltpu.with_memory_space_constraint(a, pltpu.HBM) for a in shared),
        scratch=[pltpu.SemaphoreType.DMA((6,))], space=HBM,
    )
    pieces = [piece] + [lax.ppermute(piece, "ch", z_shift(s)) for s in (2, 1, 3)]
    both = lax.optimization_barrier((both, pieces[1]))[0]
    wz = jnp.stack(pieces)
    parts = ring_gather(both, "ch", z_shift)
    far, nxt, prev = (lax.ppermute(wz, ("dom", "ch"), ring(1, s)) for s in (2, 3, 1))
    quarters = [wz, nxt, far, prev]
    quarters[0] = lax.optimization_barrier((wz, parts[1], parts[4]))[0]
    one = jnp.stack(quarters)
    w_parts = ring_gather(one, ("dom", "ch"), lambda s: ring(2, s))

    v_half, rows = call(
        send_first, [((HALF, n), BF), pltpu.HBM((m, HALF), BF)], meta, *parts, send,
        scratch=[pltpu.VMEM((m, HALF), BF), pltpu.SemaphoreType.DMA((4,))], flops=2 * HALF * n * m,
    )

    def exchange(rows):
        return lax.all_to_all(rows.reshape(32, SLOTS, HALF), "dom", 0, 0, tiled=True).reshape(-1, HALF)

    halo = exchange(lax.optimization_barrier((rows, w_parts[1], w_parts[4]))[0])
    v_other = swap(v_half)
    (e_half,) = call(gather_edges, [((HALF, m), BF)], meta, *parts)
    e_other = swap(e_half)
    halo_other = swap(halo)

    turning = [pltpu.VMEM((2, HALF, LATENT), BF)]
    for_nodes = [((2, HALF, LATENT), BF), ((2, LATENT, HALF), BF)]
    for_edges = [((3, HALF, LATENT), BF)]
    w, nodes, turned = call(
        functools.partial(unpack, 0), for_edges + for_nodes, meta, *w_parts, scratch=turning, flops=8 * HALF * n * m
    )
    tails = [(turned, swap(turned), nodes, swap(nodes))]
    mats = [w, call(functools.partial(unpack_edges, 1), for_edges, meta, *w_parts)[0]]
    nodes, turned = call(
        functools.partial(unpack_tail, 1), for_nodes, meta, *w_parts, scratch=turning, flops=4 * HALF * n * m
    )
    tails.append((turned, swap(turned), nodes, swap(nodes)))

    big = lambda r, q: 2 * r * q * LATENT
    v_all, e_all, hid = call(
        edge_first,
        [((LATENT, n), BF), ((LATENT, m), BF), ((HALF, m), BF)],
        meta, v_half, v_other, e_half, e_other, halo, halo_other, mats[0], src, dst,
        scratch=[pltpu.VMEM((HALF, n + m), BF), pltpu.VMEM((HALF, n), BF), pltpu.VMEM((m, LATENT), BF)],
        flops=4 * big(HALF, n + m),
    )
    e_new, v_new, rows = call(
        tail_first,
        [pltpu.HBM((LATENT, m), BF), pltpu.HBM((LATENT, n), BF), pltpu.HBM((m, HALF), BF)],
        meta, hid, swap(hid), *tails[0], e_all, v_all, dst, mats[1], send,
        scratch=[
            pltpu.VMEM((LATENT, m), BF), pltpu.VMEM((LATENT, n), BF), pltpu.VMEM((HALF, n), BF),
            pltpu.VMEM((m, HALF), BF), pltpu.SemaphoreType.DMA((6,)),
        ],
        flops=6 * big(LATENT, m),
    )
    far = exchange(rows)
    (part,) = call(
        edge_local, [((HALF, m), F32)], meta, v_new, e_new, mats[1], src, dst,
        scratch=[pltpu.VMEM((HALF, n), BF)] * 2, flops=3 * big(HALF, m),
    )
    (local,) = call(node_local, [((2, HALF, n), F32)], meta, tails[1][2], tails[1][3], v_new, flops=2 * big(HALF, n))
    (hid,) = call(
        lambda *refs: edge_far(n, *refs), [((HALF, m), BF)], meta, part, far, src,
        scratch=[pltpu.VMEM((HALF, m), BF)], flops=2 * big(HALF, m),
    )
    e_out, v_out = call(
        tail_last,
        [pltpu.HBM((64, m), BF), pltpu.HBM((64, n), BF)],
        meta, hid, swap(hid), *tails[1], e_new, v_new, dst, local,
        scratch=[pltpu.VMEM((LATENT, m), BF), pltpu.VMEM((LATENT, n // 2), F32), pltpu.VMEM((64, n), BF), pltpu.SemaphoreType.DMA((3,))], flops=5 * big(LATENT, m),
    )
    return v_out, e_out


def solution(mesh):
    in_specs = (
        P("ch", "dom"),
        P("ch", "dom"),
        P("dom"),
        P("dom"),
        P("dom"),
        P(None, None, None, "ch"),
        P(None, "ch", None),
        P(None, None, None, "ch"),
        P(None, "ch", None),
    )
    out_specs = (P("ch", "dom"), P("ch", "dom"))
    return jax.shard_map(shards, mesh=mesh, in_specs=in_specs, out_specs=out_specs, check_vma=False)
```

```python
import functools

import jax
import jax.numpy as jnp
from jax import lax
from jax.experimental import pallas as pl
from jax.experimental.pallas import tpu as pltpu
from jax.sharding import PartitionSpec as P

LATENT = 512
HALF = 256
SLOTS = 32
CHUNK = 512
BF = jnp.bfloat16
F32 = jnp.float32

CORE = [(c, c ^ 1) for c in range(8)]
VMEM = pl.BlockSpec(memory_space=pltpu.VMEM)
SMEM = pl.BlockSpec(memory_space=pltpu.SMEM)
HBM = pl.BlockSpec(memory_space=pltpu.HBM)


def z_shift(s):
    return [(c, ((c // 2 + s) % 4) * 2 + c % 2) for c in range(8)]


def ring(stage, s):
    pairs = []
    for d in range(32):
        along_x = (d // 4) * 4 + (d + s) % 4
        along_y = (d // 16) * 16 + (d + 4 * s) % 16
        for c in range(8):
            to = along_y if (c % 2 == 0) == (stage == 1) else along_x
            pairs.append((d * 8 + c, to * 8 + c))
    return pairs


def swap(x):
    return lax.ppermute(x, "ch", CORE)


def ring_gather(x, axis, perm):
    half = x.shape[0] // 2
    prev = lax.ppermute(x, axis, perm(1))
    nxt = lax.ppermute(x, axis, perm(3))
    far_a = lax.ppermute(prev[:half], axis, perm(1))
    far_b = lax.ppermute(nxt[half:], axis, perm(3))
    return x, nxt, far_a, far_b, prev


def dot(a, b, ca=1, cb=0):
    return lax.dot_general(a, b, (((ca,), (cb,)), ((), ())), preferred_element_type=F32)


def norm_add(msg, residual, part=None):
    mean = jnp.sum(msg, axis=0, keepdims=True) / LATENT
    var = jnp.sum(msg * msg, axis=0, keepdims=True) / LATENT - mean * mean
    part = msg if part is None else part
    return (residual.astype(F32) + (part - mean) * lax.rsqrt(var + 1e-05)).astype(BF)


def silu(x):
    return (x * jax.nn.sigmoid(x)).astype(BF)


def hot(idx, first, rows):
    where = lax.broadcasted_iota(jnp.int32, (rows, idx.shape[1]), 0) + first == idx
    return where.astype(BF)


def chunks(n, body):
    size = CHUNK if n % CHUNK == 0 else n // 2
    for first in range(0, n, size):
        body(slice(first, first + size), first)


def call(kernel, outs, *args, scratch=(), flops=0, space=VMEM, after=()):
    specs = [SMEM] + [space] * (len(args) - 1) + [pl.BlockSpec(memory_space=pl.ANY)] * len(after)
    moved = sum(a.size * a.dtype.itemsize for a in args)
    inputs = len(args)

    def body(*refs):
        kernel(*refs[:inputs], *refs[inputs + len(after) :])

    return pl.pallas_call(
        body,
        out_shape=[o if isinstance(o, pl.MemoryRef) else jax.ShapeDtypeStruct(*o) for o in outs],
        in_specs=specs,
        out_specs=[HBM if isinstance(o, pl.MemoryRef) else VMEM for o in outs],
        scratch_shapes=list(scratch),
        compiler_params=pltpu.CompilerParams(vmem_limit_bytes=6 << 20),
        cost_estimate=pl.CostEstimate(flops=flops, bytes_accessed=moved, transcendentals=0),
    )(*args, *after)


def place_half(meta, parts, out, col):
    own, nxt, far_a, far_b, prev = parts
    zi = meta[0]
    at = lambda s: pl.multiple_of(((zi + s) & 3) * 64, 64)
    cols = slice(col, col + out.shape[1])
    out[pl.ds(at(0), 64), :] = own[:, cols]
    out[pl.ds(at(1), 64), :] = nxt[:, cols]
    out[pl.ds(at(2), 32), :] = far_a[:, cols]
    out[pl.ds(at(2) + 32, 32), :] = far_b[:, cols]
    out[pl.ds(at(3), 64), :] = prev[:, cols]


def select_rows(send, x, rows, held, sem):
    size = rows.shape[0] // 4
    copies = []
    for i in range(4):
        sl = slice(i * size, i * size + size)
        held[sl, :] = dot(x, hot(send[:, sl], 0, x.shape[1])).T.astype(BF)
        copies.append(pltpu.make_async_copy(held.at[sl], rows.at[sl], sem.at[i]))
        copies[-1].start()
    for copy in copies:
        copy.wait()


def send_first(meta, own, nxt, far_a, far_b, prev, send, half, rows, held, sem):
    place_half(meta, (own, nxt, far_a, far_b, prev), half, 0)
    select_rows(send, half[...], rows, held, sem)


def gather_edges(meta, own, nxt, far_a, far_b, prev, half):
    place_half(meta, (own, nxt, far_a, far_b, prev), half, own.shape[1] - half.shape[1])


def prepare(meta, w_e, w_eo, w_n, w_no, v, e, piece, both, sem):
    lay = meta[1] >> 1
    rows = pl.ds(pl.multiple_of(8 * ((meta[1] & 1) * 4 + meta[2]), 8), 8)
    n = v.shape[1]
    copies = [
        (w_e.at[lay, :, rows], piece.at[0:3]),
        (w_eo.at[lay, rows], piece.at[3]),
        (w_n.at[lay, :, rows], piece.at[4:6]),
        (w_no.at[lay, rows], piece.at[6]),
        (v, both.at[:, :n]),
        (e, both.at[:, n:]),
    ]
    copies = [pltpu.make_async_copy(a, b, sem.at[i]) for i, (a, b) in enumerate(copies)]
    for copy in copies:
        copy.start()
    for copy in copies:
        copy.wait()


def unpack(layer, meta, own, nxt, far_a, far_b, prev, mats, nodes, turned, outs):
    where = [mats.at[0], mats.at[1], mats.at[2], outs.at[0], nodes.at[0], nodes.at[1], outs.at[1]]
    for s in range(4):
        for r in range(4):
            a = (meta[1] + r) & 3
            at = pl.multiple_of((((meta[2] + s) & 3) * 2 + (a & 1)) * 32, 32)
            ref, row = ((own, r), (nxt, r), (far_a, r) if r < 2 else (far_b, r - 2), (prev, r))[s]

            @pl.when((a >> 1) == layer)
            def _():
                for m in range(7):
                    where[m][pl.ds(at, 32), :] = ref[row, :, m].astype(F32).reshape(32, LATENT).astype(BF)

    turned[0] = outs[0].astype(F32).T.astype(BF)
    turned[1] = outs[1].astype(F32).T.astype(BF)


def interleave(meta, own, other, out):
    for z in range(4):
        out[pl.ds(pl.multiple_of(z * 128 + meta[3] * 64, 64), 64), :] = own[z * 64 : z * 64 + 64]
        out[pl.ds(pl.multiple_of(z * 128 + 64 - meta[3] * 64, 64), 64), :] = other[z * 64 : z * 64 + 64]


def edge_first(meta, v_own, v_other, e_own, e_other, h_own, h_other, mats, src, dst, v_all, e_all, hidden, sender, receiver, halo):
    n = v_all.shape[1]
    interleave(meta, v_own, v_other, v_all)
    interleave(meta, e_own, e_other, e_all)
    swapped = meta[3] == 1
    low = lax.broadcasted_iota(jnp.int32, (halo.shape[0], 128), 1) < 64
    for b in range(2):
        blk = slice(128 * b, 128 * b + 128)
        own, other = h_own[:, blk].astype(F32), h_other[:, blk].astype(F32)
        even = jnp.where(swapped, other, own)
        odd = jnp.where(swapped, own, other)
        halo[:, 256 * b : 256 * b + 128] = jnp.where(low, even, pltpu.roll(odd, 64, 1)).astype(BF)
        halo[:, 256 * b + 128 : 256 * b + 256] = jnp.where(low, pltpu.roll(even, 64, 1), odd).astype(BF)
    sender[:, :n] = dot(mats[1], v_all[...]).astype(BF)
    sender[:, n:] = dot(mats[1], halo[...], 1, 1).astype(BF)
    receiver[...] = dot(mats[2], v_all[...]).astype(BF)

    def body(sl, _):
        pre = dot(mats[0], e_all[:, sl])
        pre += dot(sender[...], hot(src[:, sl], 0, sender.shape[1]))
        pre += dot(receiver[...], hot(dst[:, sl], 0, n))
        hidden[:, sl] = silu(pre)

    chunks(hidden.shape[1], body)


def new_edges(hid, hid_other, turned, turned_other, e_all, e_new):
    def edges(sl, _):
        msg = dot(turned[0], hid[:, sl]) + dot(turned_other[0], hid_other[:, sl])
        e_new[:, sl] = norm_add(msg, e_all[:, sl])

    chunks(e_new.shape[1], edges)


def node_message(first, sl, turned, turned_other, nodes, nodes_other, e_new, dst, local):
    agg = dot(e_new[...], hot(dst[...], first, sl.stop - sl.start), 1, 1).astype(BF)
    msg = dot(turned[1], silu(local(0) + dot(nodes[1], agg)))
    return msg + dot(turned_other[1], silu(local(1) + dot(nodes_other[1], agg)))


def node_local(meta, nodes, nodes_other, v_all, out):
    out[0] = dot(nodes[0], v_all[...])
    out[1] = dot(nodes_other[0], v_all[...])


def tail_first(
    meta, hid, hid_other, turned, turned_other, nodes, nodes_other, e_all, v_all, dst, mats_next, send,
    e_out, v_out, rows, e_new, v_new, sender, held, sem,
):
    new_edges(hid, hid_other, turned, turned_other, e_all, e_new)
    copies = [pltpu.make_async_copy(e_new, e_out, sem.at[4])]
    copies[0].start()

    def body(sl, first):
        local = lambda i: dot((nodes, nodes_other)[i][0], v_all[:, sl])
        msg = node_message(first, sl, turned, turned_other, nodes, nodes_other, e_new, dst, local)
        v_new[:, sl] = norm_add(msg, v_all[:, sl])

    chunks(v_new.shape[1], body)
    copies.append(pltpu.make_async_copy(v_new, v_out, sem.at[5]))
    copies[1].start()
    sender[...] = dot(mats_next[1], v_new[...]).astype(BF)
    select_rows(send, sender[...], rows, held, sem)
    for copy in copies:
        copy.wait()


def tail_last(
    meta, hid, hid_other, turned, turned_other, nodes, nodes_other, e_all, v_all, dst, local,
    e_out, v_out, e_new, sums, held, sem,
):
    new_edges(hid, hid_other, turned, turned_other, e_all, e_new)
    mine = pl.ds(pl.multiple_of(meta[4] * 64, 64), 64)
    copies = [pltpu.make_async_copy(e_new.at[mine, :], e_out, sem.at[0])]
    copies[0].start()

    def body(sl, first):
        msg = node_message(first, sl, turned, turned_other, nodes, nodes_other, e_new, dst, lambda i: local[i, :, sl])
        sums[...] = msg
        held[:, sl] = norm_add(msg, v_all[mine, sl], sums[mine, :])
        copies.append(pltpu.make_async_copy(held.at[:, sl], v_out.at[:, sl], sem.at[len(copies)]))
        copies[-1].start()

    chunks(v_out.shape[1], body)
    for copy in copies:
        copy.wait()


def edge_local(meta, v_all, e_all, mats, src, dst, part, sender, receiver):
    n = v_all.shape[1]
    sender[...] = dot(mats[1], v_all[...]).astype(BF)
    receiver[...] = dot(mats[2], v_all[...]).astype(BF)

    def body(sl, _):
        pre = dot(mats[0], e_all[:, sl])
        pre += dot(sender[...], hot(src[:, sl], 0, n))
        part[:, sl] = pre + dot(receiver[...], hot(dst[:, sl], 0, n))

    chunks(part.shape[1], body)


def edge_far(n, meta, part, rows, src, hidden, far):
    far[...] = rows[...].astype(F32).T.astype(BF)

    def body(sl, _):
        hidden[:, sl] = silu(part[:, sl] + dot(far[...], hot(src[:, sl], n, far.shape[1])))

    chunks(hidden.shape[1], body)


def shards(node_feats, edge_feats, send_rows, edge_src, edge_dst, w_edge_in, w_edge_out, w_node_in, w_node_out):
    d = lax.axis_index("dom")
    c = lax.axis_index("ch")
    k = c & 1
    y, x = (d >> 2) & 3, d & 3
    n = node_feats.shape[1]
    m = edge_feats.shape[1]
    first = jnp.where(k == 0, y, x)
    second = jnp.where(k == 0, x, y)
    meta = jnp.stack([c >> 1, first, second, k, c]).astype(jnp.int32)
    send, src, dst = (a.reshape(1, -1) for a in (send_rows, edge_src, edge_dst))

    shared = (jnp.swapaxes(w_edge_in, 2, 3), w_edge_out, jnp.swapaxes(w_node_in, 2, 3), w_node_out, node_feats, edge_feats)
    piece, both = call(
        prepare,
        [((7, 8, LATENT), BF), ((64, n + m), BF)],
        meta, *(pltpu.with_memory_space_constraint(a, pltpu.HBM) for a in shared),
        scratch=[pltpu.SemaphoreType.DMA((6,))], space=HBM,
    )
    pieces = [piece] + [lax.ppermute(piece, "ch", z_shift(s)) for s in (2, 1, 3)]
    both = lax.optimization_barrier((both, pieces[1]))[0]
    wz = jnp.stack(pieces)
    parts = ring_gather(both, "ch", z_shift)
    far, nxt, prev = (lax.ppermute(wz, ("dom", "ch"), ring(1, s)) for s in (2, 3, 1))
    quarters = [wz, nxt, far, prev]
    quarters[0] = lax.optimization_barrier((wz, parts[1], parts[4]))[0]
    one = jnp.stack(quarters)
    w_parts = ring_gather(one, ("dom", "ch"), lambda s: ring(2, s))

    v_half, rows = call(
        send_first, [((HALF, n), BF), pltpu.HBM((m, HALF), BF)], meta, *parts, send,
        scratch=[pltpu.VMEM((m, HALF), BF), pltpu.SemaphoreType.DMA((4,))], flops=2 * HALF * n * m,
    )

    def exchange(rows):
        return lax.all_to_all(rows.reshape(32, SLOTS, HALF), "dom", 0, 0, tiled=True).reshape(-1, HALF)

    halo = exchange(lax.optimization_barrier((rows, w_parts[1], w_parts[4]))[0])
    v_other = swap(v_half)
    (e_half,) = call(gather_edges, [((HALF, m), BF)], meta, *parts)
    e_other = swap(e_half)
    halo_other = swap(halo)

    mats, tails = [], []
    for layer in range(2):
        w, nodes, turned = call(
            functools.partial(unpack, layer),
            [((3, HALF, LATENT), BF), ((2, HALF, LATENT), BF), ((2, LATENT, HALF), BF)],
            meta, *w_parts, scratch=[pltpu.VMEM((2, HALF, LATENT), BF)], flops=8 * HALF * n * m * (1 - layer),
        )
        mats.append(w)
        tails.append((turned, swap(turned), nodes, swap(nodes)))

    big = lambda r, q: 2 * r * q * LATENT
    v_all, e_all, hid = call(
        edge_first,
        [((LATENT, n), BF), ((LATENT, m), BF), ((HALF, m), BF)],
        meta, v_half, v_other, e_half, e_other, halo, halo_other, mats[0], src, dst,
        scratch=[pltpu.VMEM((HALF, n + m), BF), pltpu.VMEM((HALF, n), BF), pltpu.VMEM((m, LATENT), BF)],
        flops=4 * big(HALF, n + m),
    )
    e_new, v_new, rows = call(
        tail_first,
        [pltpu.HBM((LATENT, m), BF), pltpu.HBM((LATENT, n), BF), pltpu.HBM((m, HALF), BF)],
        meta, hid, swap(hid), *tails[0], e_all, v_all, dst, mats[1], send,
        scratch=[
            pltpu.VMEM((LATENT, m), BF), pltpu.VMEM((LATENT, n), BF), pltpu.VMEM((HALF, n), BF),
            pltpu.VMEM((m, HALF), BF), pltpu.SemaphoreType.DMA((6,)),
        ],
        flops=6 * big(LATENT, m),
    )
    far = exchange(rows)
    (part,) = call(
        edge_local, [((HALF, m), F32)], meta, v_new, e_new, mats[1], src, dst,
        scratch=[pltpu.VMEM((HALF, n), BF)] * 2, flops=3 * big(HALF, m),
    )
    (local,) = call(node_local, [((2, HALF, n), F32)], meta, tails[1][2], tails[1][3], v_new, flops=2 * big(HALF, n))
    (hid,) = call(
        lambda *refs: edge_far(n, *refs), [((HALF, m), BF)], meta, part, far, src,
        scratch=[pltpu.VMEM((HALF, m), BF)], flops=2 * big(HALF, m),
    )
    e_out, v_out = call(
        tail_last,
        [pltpu.HBM((64, m), BF), pltpu.HBM((64, n), BF)],
        meta, hid, swap(hid), *tails[1], e_new, v_new, dst, local,
        scratch=[pltpu.VMEM((LATENT, m), BF), pltpu.VMEM((LATENT, n // 2), F32), pltpu.VMEM((64, n), BF), pltpu.SemaphoreType.DMA((3,))], flops=5 * big(LATENT, m),
    )
    return v_out, e_out


def solution(mesh):
    in_specs = (
        P("ch", "dom"),
        P("ch", "dom"),
        P("dom"),
        P("dom"),
        P("dom"),
        P(None, None, None, "ch"),
        P(None, "ch", None),
        P(None, None, None, "ch"),
        P(None, "ch", None),
    )
    out_specs = (P("ch", "dom"), P("ch", "dom"))
    return jax.shard_map(shards, mesh=mesh, in_specs=in_specs, out_specs=out_specs, check_vma=False)
```

```python
import functools

import jax
import jax.numpy as jnp
from jax import lax
from jax.experimental import pallas as pl
from jax.experimental.pallas import tpu as pltpu
from jax.sharding import PartitionSpec as P

LATENT = 512
HALF = 256
SLOTS = 32
CHUNK = 512
BF = jnp.bfloat16
F32 = jnp.float32

CORE = [(c, c ^ 1) for c in range(8)]
VMEM = pl.BlockSpec(memory_space=pltpu.VMEM)
SMEM = pl.BlockSpec(memory_space=pltpu.SMEM)
HBM = pl.BlockSpec(memory_space=pltpu.HBM)


def z_shift(s):
    return [(c, ((c // 2 + s) % 4) * 2 + c % 2) for c in range(8)]


def ring(stage, s):
    pairs = []
    for d in range(32):
        along_x = (d // 4) * 4 + (d + s) % 4
        along_y = (d // 16) * 16 + (d + 4 * s) % 16
        for c in range(8):
            to = along_y if (c % 2 == 0) == (stage == 1) else along_x
            pairs.append((d * 8 + c, to * 8 + c))
    return pairs


def swap(x):
    return lax.ppermute(x, "ch", CORE)


def ring_gather(x, axis, perm):
    half = x.shape[0] // 2
    prev = lax.ppermute(x, axis, perm(1))
    nxt = lax.ppermute(x, axis, perm(3))
    far_a = lax.ppermute(prev[:half], axis, perm(1))
    far_b = lax.ppermute(nxt[half:], axis, perm(3))
    return x, nxt, far_a, far_b, prev


def dot(a, b, ca=1, cb=0):
    return lax.dot_general(a, b, (((ca,), (cb,)), ((), ())), preferred_element_type=F32)


def norm_add(msg, residual, part=None):
    mean = jnp.sum(msg, axis=0, keepdims=True) / LATENT
    var = jnp.sum(msg * msg, axis=0, keepdims=True) / LATENT - mean * mean
    part = msg if part is None else part
    return (residual.astype(F32) + (part - mean) * lax.rsqrt(var + 1e-05)).astype(BF)


def silu(x):
    return (x * jax.nn.sigmoid(x)).astype(BF)


def hot(idx, first, rows):
    where = lax.broadcasted_iota(jnp.int32, (rows, idx.shape[1]), 0) + first == idx
    return where.astype(BF)


def chunks(n, body):
    size = CHUNK if n % CHUNK == 0 else n // 2
    for first in range(0, n, size):
        body(slice(first, first + size), first)


def call(kernel, outs, *args, scratch=(), flops=0, space=VMEM, after=()):
    specs = [SMEM] + [space] * (len(args) - 1) + [pl.BlockSpec(memory_space=pl.ANY)] * len(after)
    moved = sum(a.size * a.dtype.itemsize for a in args)
    inputs = len(args)

    def body(*refs):
        kernel(*refs[:inputs], *refs[inputs + len(after) :])

    return pl.pallas_call(
        body,
        out_shape=[o if isinstance(o, pl.MemoryRef) else jax.ShapeDtypeStruct(*o) for o in outs],
        in_specs=specs,
        out_specs=[HBM if isinstance(o, pl.MemoryRef) else VMEM for o in outs],
        scratch_shapes=list(scratch),
        compiler_params=pltpu.CompilerParams(vmem_limit_bytes=6 << 20),
        cost_estimate=pl.CostEstimate(flops=flops, bytes_accessed=moved, transcendentals=0),
    )(*args, *after)


def place_half(meta, parts, out, col):
    own, nxt, far_a, far_b, prev = parts
    zi = meta[0]
    at = lambda s: pl.multiple_of(((zi + s) & 3) * 64, 64)
    cols = slice(col, col + out.shape[1])
    out[pl.ds(at(0), 64), :] = own[:, cols]
    out[pl.ds(at(1), 64), :] = nxt[:, cols]
    out[pl.ds(at(2), 32), :] = far_a[:, cols]
    out[pl.ds(at(2) + 32, 32), :] = far_b[:, cols]
    out[pl.ds(at(3), 64), :] = prev[:, cols]


def select_rows(send, x, rows, held, sem):
    size = rows.shape[0] // 4
    copies = []
    for i in range(4):
        sl = slice(i * size, i * size + size)
        held[sl, :] = dot(x, hot(send[:, sl], 0, x.shape[1])).T.astype(BF)
        copies.append(pltpu.make_async_copy(held.at[sl], rows.at[sl], sem.at[i]))
        copies[-1].start()
    for copy in copies:
        copy.wait()


def send_first(meta, own, nxt, far_a, far_b, prev, send, half, rows, held, sem):
    place_half(meta, (own, nxt, far_a, far_b, prev), half, 0)
    select_rows(send, half[...], rows, held, sem)


def gather_edges(meta, own, nxt, far_a, far_b, prev, half):
    place_half(meta, (own, nxt, far_a, far_b, prev), half, own.shape[1] - half.shape[1])


def prepare(meta, w_e, w_eo, w_n, w_no, v, e, piece, both, sem):
    lay = meta[1] >> 1
    rows = pl.ds(pl.multiple_of(8 * ((meta[1] & 1) * 4 + meta[2]), 8), 8)
    n = v.shape[1]
    copies = [
        (w_e.at[lay, :, rows], piece.at[0:3]),
        (w_eo.at[lay, rows], piece.at[3]),
        (w_n.at[lay, :, rows], piece.at[4:6]),
        (w_no.at[lay, rows], piece.at[6]),
        (v, both.at[:, :n]),
        (e, both.at[:, n:]),
    ]
    copies = [pltpu.make_async_copy(a, b, sem.at[i]) for i, (a, b) in enumerate(copies)]
    for copy in copies:
        copy.start()
    for copy in copies:
        copy.wait()


def unpack(layer, meta, own, nxt, far_a, far_b, prev, mats, nodes, turned, outs):
    where = [mats.at[0], mats.at[1], mats.at[2], outs.at[0], nodes.at[0], nodes.at[1], outs.at[1]]
    for s in range(4):
        for r in range(4):
            a = (meta[1] + r) & 3
            at = pl.multiple_of((((meta[2] + s) & 3) * 2 + (a & 1)) * 32, 32)
            ref, row = ((own, r), (nxt, r), (far_a, r) if r < 2 else (far_b, r - 2), (prev, r))[s]

            @pl.when((a >> 1) == layer)
            def _():
                for m in range(7):
                    where[m][pl.ds(at, 32), :] = ref[row, :, m].astype(F32).reshape(32, LATENT).astype(BF)

    turned[0] = outs[0].astype(F32).T.astype(BF)
    turned[1] = outs[1].astype(F32).T.astype(BF)


def interleave(meta, own, other, out):
    for z in range(4):
        out[pl.ds(pl.multiple_of(z * 128 + meta[3] * 64, 64), 64), :] = own[z * 64 : z * 64 + 64]
        out[pl.ds(pl.multiple_of(z * 128 + 64 - meta[3] * 64, 64), 64), :] = other[z * 64 : z * 64 + 64]


def edge_first(meta, v_own, v_other, e_own, e_other, h_own, h_other, mats, src, dst, v_all, e_all, hidden, sender, receiver, halo):
    n = v_all.shape[1]
    interleave(meta, v_own, v_other, v_all)
    interleave(meta, e_own, e_other, e_all)
    swapped = meta[3] == 1
    low = lax.broadcasted_iota(jnp.int32, (halo.shape[0], 128), 1) < 64
    for b in range(2):
        blk = slice(128 * b, 128 * b + 128)
        own, other = h_own[:, blk].astype(F32), h_other[:, blk].astype(F32)
        even = jnp.where(swapped, other, own)
        odd = jnp.where(swapped, own, other)
        halo[:, 256 * b : 256 * b + 128] = jnp.where(low, even, pltpu.roll(odd, 64, 1)).astype(BF)
        halo[:, 256 * b + 128 : 256 * b + 256] = jnp.where(low, pltpu.roll(even, 64, 1), odd).astype(BF)
    sender[:, :n] = dot(mats[1], v_all[...]).astype(BF)
    sender[:, n:] = dot(mats[1], halo[...], 1, 1).astype(BF)
    receiver[...] = dot(mats[2], v_all[...]).astype(BF)

    def body(sl, _):
        pre = dot(mats[0], e_all[:, sl])
        pre += dot(sender[...], hot(src[:, sl], 0, sender.shape[1]))
        pre += dot(receiver[...], hot(dst[:, sl], 0, n))
        hidden[:, sl] = silu(pre)

    chunks(hidden.shape[1], body)


def new_edges(hid, hid_other, turned, turned_other, e_all, e_new):
    def edges(sl, _):
        msg = dot(turned[0], hid[:, sl]) + dot(turned_other[0], hid_other[:, sl])
        e_new[:, sl] = norm_add(msg, e_all[:, sl])

    chunks(e_new.shape[1], edges)


def node_message(first, sl, turned, turned_other, nodes, nodes_other, e_new, dst, local):
    agg = dot(e_new[...], hot(dst[...], first, sl.stop - sl.start), 1, 1).astype(BF)
    msg = dot(turned[1], silu(local(0) + dot(nodes[1], agg)))
    return msg + dot(turned_other[1], silu(local(1) + dot(nodes_other[1], agg)))


def node_local(meta, nodes, nodes_other, v_all, out):
    out[0] = dot(nodes[0], v_all[...])
    out[1] = dot(nodes_other[0], v_all[...])


def tail_first(
    meta, hid, hid_other, turned, turned_other, nodes, nodes_other, e_all, v_all, dst, mats_next, send,
    e_new, v_new, rows, sender, held, sem,
):
    new_edges(hid, hid_other, turned, turned_other, e_all, e_new)

    def body(sl, first):
        local = lambda i: dot((nodes, nodes_other)[i][0], v_all[:, sl])
        msg = node_message(first, sl, turned, turned_other, nodes, nodes_other, e_new, dst, local)
        v_new[:, sl] = norm_add(msg, v_all[:, sl])

    chunks(v_new.shape[1], body)
    sender[...] = dot(mats_next[1], v_new[...]).astype(BF)
    select_rows(send, sender[...], rows, held, sem)


def tail_last(
    meta, hid, hid_other, turned, turned_other, nodes, nodes_other, e_all, v_all, dst, local,
    e_out, v_out, e_new, sums,
):
    new_edges(hid, hid_other, turned, turned_other, e_all, e_new)
    mine = pl.ds(pl.multiple_of(meta[4] * 64, 64), 64)
    e_out[...] = e_new[mine, :]

    def body(sl, first):
        msg = node_message(first, sl, turned, turned_other, nodes, nodes_other, e_new, dst, lambda i: local[i, :, sl])
        sums[...] = msg
        v_out[:, sl] = norm_add(msg, v_all[mine, sl], sums[mine, :])

    chunks(v_out.shape[1], body)


def edge_local(meta, v_all, e_all, mats, src, dst, part, sender, receiver):
    n = v_all.shape[1]
    sender[...] = dot(mats[1], v_all[...]).astype(BF)
    receiver[...] = dot(mats[2], v_all[...]).astype(BF)

    def body(sl, _):
        pre = dot(mats[0], e_all[:, sl])
        pre += dot(sender[...], hot(src[:, sl], 0, n))
        part[:, sl] = pre + dot(receiver[...], hot(dst[:, sl], 0, n))

    chunks(part.shape[1], body)


def edge_far(n, meta, part, rows, src, hidden, far):
    far[...] = rows[...].astype(F32).T.astype(BF)

    def body(sl, _):
        hidden[:, sl] = silu(part[:, sl] + dot(far[...], hot(src[:, sl], n, far.shape[1])))

    chunks(hidden.shape[1], body)


def shards(node_feats, edge_feats, send_rows, edge_src, edge_dst, w_edge_in, w_edge_out, w_node_in, w_node_out):
    d = lax.axis_index("dom")
    c = lax.axis_index("ch")
    k = c & 1
    y, x = (d >> 2) & 3, d & 3
    n = node_feats.shape[1]
    m = edge_feats.shape[1]
    first = jnp.where(k == 0, y, x)
    second = jnp.where(k == 0, x, y)
    meta = jnp.stack([c >> 1, first, second, k, c]).astype(jnp.int32)
    send, src, dst = (a.reshape(1, -1) for a in (send_rows, edge_src, edge_dst))

    shared = (jnp.swapaxes(w_edge_in, 2, 3), w_edge_out, jnp.swapaxes(w_node_in, 2, 3), w_node_out, node_feats, edge_feats)
    piece, both = call(
        prepare,
        [((7, 8, LATENT), BF), ((64, n + m), BF)],
        meta, *(pltpu.with_memory_space_constraint(a, pltpu.HBM) for a in shared),
        scratch=[pltpu.SemaphoreType.DMA((6,))], space=HBM,
    )
    pieces = [piece] + [lax.ppermute(piece, "ch", z_shift(s)) for s in (2, 1, 3)]
    both = lax.optimization_barrier((both, pieces[1]))[0]
    wz = jnp.stack(pieces)
    parts = ring_gather(both, "ch", z_shift)
    far, nxt, prev = (lax.ppermute(wz, ("dom", "ch"), ring(1, s)) for s in (2, 3, 1))
    quarters = [wz, nxt, far, prev]
    quarters[0] = lax.optimization_barrier((wz, parts[1], parts[4]))[0]
    one = jnp.stack(quarters)
    w_prev = lax.ppermute(one, ("dom", "ch"), ring(2, 1))
    w_next = lax.ppermute(one, ("dom", "ch"), ring(2, 3))

    v_half, rows = call(
        send_first, [((HALF, n), BF), pltpu.HBM((m, HALF), BF)], meta, *parts, send,
        scratch=[pltpu.VMEM((m, HALF), BF), pltpu.SemaphoreType.DMA((4,))], flops=2 * HALF * n * m,
    )

    def exchange(rows):
        return lax.all_to_all(rows.reshape(32, SLOTS, HALF), "dom", 0, 0, tiled=True).reshape(-1, HALF)

    rows, half_a, half_b = lax.optimization_barrier((rows, w_prev[:2], w_next[2:]))
    halo = exchange(rows)
    far_a = lax.ppermute(half_a, ("dom", "ch"), ring(2, 1))
    far_b = lax.ppermute(half_b, ("dom", "ch"), ring(2, 3))
    w_parts = (one, w_next, far_a, far_b, w_prev)
    v_other = swap(v_half)
    (e_half,) = call(gather_edges, [((HALF, m), BF)], meta, *parts)
    e_other = swap(e_half)
    halo_other = swap(halo)

    mats, tails = [], []
    for layer in range(2):
        w, nodes, turned = call(
            functools.partial(unpack, layer),
            [((3, HALF, LATENT), BF), ((2, HALF, LATENT), BF), ((2, LATENT, HALF), BF)],
            meta, *w_parts, scratch=[pltpu.VMEM((2, HALF, LATENT), BF)], flops=8 * HALF * n * m * (1 - layer),
        )
        mats.append(w)
        tails.append((turned, swap(turned), nodes, swap(nodes)))

    big = lambda r, q: 2 * r * q * LATENT
    v_all, e_all, hid = call(
        edge_first,
        [((LATENT, n), BF), ((LATENT, m), BF), ((HALF, m), BF)],
        meta, v_half, v_other, e_half, e_other, halo, halo_other, mats[0], src, dst,
        scratch=[pltpu.VMEM((HALF, n + m), BF), pltpu.VMEM((HALF, n), BF), pltpu.VMEM((m, LATENT), BF)],
        flops=4 * big(HALF, n + m),
    )
    e_new, v_new, rows = call(
        tail_first,
        [((LATENT, m), BF), ((LATENT, n), BF), pltpu.HBM((m, HALF), BF)],
        meta, hid, swap(hid), *tails[0], e_all, v_all, dst, mats[1], send,
        scratch=[pltpu.VMEM((HALF, n), BF), pltpu.VMEM((m, HALF), BF), pltpu.SemaphoreType.DMA((4,))], flops=6 * big(LATENT, m),
    )
    far = exchange(rows)
    (part,) = call(
        edge_local, [((HALF, m), F32)], meta, v_new, e_new, mats[1], src, dst,
        scratch=[pltpu.VMEM((HALF, n), BF)] * 2, flops=3 * big(HALF, m),
    )
    (local,) = call(node_local, [((2, HALF, n), F32)], meta, tails[1][2], tails[1][3], v_new, flops=2 * big(HALF, n))
    (hid,) = call(
        lambda *refs: edge_far(n, *refs), [((HALF, m), BF)], meta, part, far, src,
        scratch=[pltpu.VMEM((HALF, m), BF)], flops=2 * big(HALF, m),
    )
    e_out, v_out = call(
        tail_last,
        [((64, m), BF), ((64, n), BF)],
        meta, hid, swap(hid), *tails[1], e_new, v_new, dst, local,
        scratch=[pltpu.VMEM((LATENT, m), BF), pltpu.VMEM((LATENT, n // 2), F32)], flops=5 * big(LATENT, m),
    )
    return v_out, e_out


def solution(mesh):
    in_specs = (
        P("ch", "dom"),
        P("ch", "dom"),
        P("dom"),
        P("dom"),
        P("dom"),
        P(None, None, None, "ch"),
        P(None, "ch", None),
        P(None, None, None, "ch"),
        P(None, "ch", None),
    )
    out_specs = (P("ch", "dom"), P("ch", "dom"))
    return jax.shard_map(shards, mesh=mesh, in_specs=in_specs, out_specs=out_specs, check_vma=False)
```

```python
import functools

import jax
import jax.numpy as jnp
from jax import lax
from jax.experimental import pallas as pl
from jax.experimental.pallas import tpu as pltpu
from jax.sharding import PartitionSpec as P

LATENT = 512
HALF = 256
SLOTS = 32
CHUNK = 512
BF = jnp.bfloat16
F32 = jnp.float32

CORE = [(c, c ^ 1) for c in range(8)]
VMEM = pl.BlockSpec(memory_space=pltpu.VMEM)
SMEM = pl.BlockSpec(memory_space=pltpu.SMEM)
HBM = pl.BlockSpec(memory_space=pltpu.HBM)


def z_shift(s):
    return [(c, ((c // 2 + s) % 4) * 2 + c % 2) for c in range(8)]


def ring(stage, s):
    pairs = []
    for d in range(32):
        along_x = (d // 4) * 4 + (d + s) % 4
        along_y = (d // 16) * 16 + (d + 4 * s) % 16
        for c in range(8):
            to = along_y if (c % 2 == 0) == (stage == 1) else along_x
            pairs.append((d * 8 + c, to * 8 + c))
    return pairs


def swap(x):
    return lax.ppermute(x, "ch", CORE)


def ring_gather(x, axis, perm):
    half = x.shape[0] // 2
    prev = lax.ppermute(x, axis, perm(1))
    nxt = lax.ppermute(x, axis, perm(3))
    far_a = lax.ppermute(prev[:half], axis, perm(1))
    far_b = lax.ppermute(nxt[half:], axis, perm(3))
    return x, nxt, far_a, far_b, prev


def dot(a, b, ca=1, cb=0):
    return lax.dot_general(a, b, (((ca,), (cb,)), ((), ())), preferred_element_type=F32)


def norm_add(msg, residual, part=None):
    mean = jnp.sum(msg, axis=0, keepdims=True) / LATENT
    var = jnp.sum(msg * msg, axis=0, keepdims=True) / LATENT - mean * mean
    part = msg if part is None else part
    return (residual.astype(F32) + (part - mean) * lax.rsqrt(var + 1e-05)).astype(BF)


def silu(x):
    return (x * jax.nn.sigmoid(x)).astype(BF)


def hot(idx, first, rows):
    where = lax.broadcasted_iota(jnp.int32, (rows, idx.shape[1]), 0) + first == idx
    return where.astype(BF)


def chunks(n, body):
    size = CHUNK if n % CHUNK == 0 else n // 2
    for first in range(0, n, size):
        body(slice(first, first + size), first)


def call(kernel, outs, *args, scratch=(), flops=0, space=VMEM, after=()):
    specs = [SMEM] + [space] * (len(args) - 1) + [pl.BlockSpec(memory_space=pl.ANY)] * len(after)
    moved = sum(a.size * a.dtype.itemsize for a in args)
    inputs = len(args)

    def body(*refs):
        kernel(*refs[:inputs], *refs[inputs + len(after) :])

    return pl.pallas_call(
        body,
        out_shape=[o if isinstance(o, pl.MemoryRef) else jax.ShapeDtypeStruct(*o) for o in outs],
        in_specs=specs,
        out_specs=[HBM if isinstance(o, pl.MemoryRef) else VMEM for o in outs],
        scratch_shapes=list(scratch),
        compiler_params=pltpu.CompilerParams(vmem_limit_bytes=6 << 20),
        cost_estimate=pl.CostEstimate(flops=flops, bytes_accessed=moved, transcendentals=0),
    )(*args, *after)


def place_half(meta, parts, out, col):
    own, nxt, far_a, far_b, prev = parts
    zi = meta[0]
    at = lambda s: pl.multiple_of(((zi + s) & 3) * 64, 64)
    cols = slice(col, col + out.shape[1])
    out[pl.ds(at(0), 64), :] = own[:, cols]
    out[pl.ds(at(1), 64), :] = nxt[:, cols]
    out[pl.ds(at(2), 32), :] = far_a[:, cols]
    out[pl.ds(at(2) + 32, 32), :] = far_b[:, cols]
    out[pl.ds(at(3), 64), :] = prev[:, cols]


def select_rows(send, x, rows, held, sem):
    size = rows.shape[0] // 4
    copies = []
    for i in range(4):
        sl = slice(i * size, i * size + size)
        held[sl, :] = dot(x, hot(send[:, sl], 0, x.shape[1])).T.astype(BF)
        copies.append(pltpu.make_async_copy(held.at[sl], rows.at[sl], sem.at[i]))
        copies[-1].start()
    for copy in copies:
        copy.wait()


def send_first(meta, own, nxt, far_a, far_b, prev, send, half, rows, held, sem):
    place_half(meta, (own, nxt, far_a, far_b, prev), half, 0)
    select_rows(send, half[...], rows, held, sem)


def gather_edges(meta, own, nxt, far_a, far_b, prev, half):
    place_half(meta, (own, nxt, far_a, far_b, prev), half, own.shape[1] - half.shape[1])


def prepare(meta, w_e, w_eo, w_n, w_no, v, e, piece, both, sem):
    lay = meta[1] >> 1
    rows = pl.ds(pl.multiple_of(8 * ((meta[1] & 1) * 4 + meta[2]), 8), 8)
    n = v.shape[1]
    copies = [
        (w_e.at[lay, :, rows], piece.at[0:3]),
        (w_eo.at[lay, rows], piece.at[3]),
        (w_n.at[lay, :, rows], piece.at[4:6]),
        (w_no.at[lay, rows], piece.at[6]),
        (v, both.at[:, :n]),
        (e, both.at[:, n:]),
    ]
    copies = [pltpu.make_async_copy(a, b, sem.at[i]) for i, (a, b) in enumerate(copies)]
    for copy in copies:
        copy.start()
    for copy in copies:
        copy.wait()


def unpack(layer, meta, own, nxt, far_a, far_b, prev, mats, nodes, turned, outs):
    where = [mats.at[0], mats.at[1], mats.at[2], outs.at[0], nodes.at[0], nodes.at[1], outs.at[1]]
    for s in range(4):
        for r in range(4):
            a = (meta[1] + r) & 3
            at = pl.multiple_of((((meta[2] + s) & 3) * 2 + (a & 1)) * 32, 32)
            ref, row = ((own, r), (nxt, r), (far_a, r) if r < 2 else (far_b, r - 2), (prev, r))[s]

            @pl.when((a >> 1) == layer)
            def _():
                for m in range(7):
                    where[m][pl.ds(at, 32), :] = ref[row, :, m].astype(F32).reshape(32, LATENT).astype(BF)

    turned[0] = outs[0].astype(F32).T.astype(BF)
    turned[1] = outs[1].astype(F32).T.astype(BF)


def interleave(meta, own, other, out):
    for z in range(4):
        out[pl.ds(pl.multiple_of(z * 128 + meta[3] * 64, 64), 64), :] = own[z * 64 : z * 64 + 64]
        out[pl.ds(pl.multiple_of(z * 128 + 64 - meta[3] * 64, 64), 64), :] = other[z * 64 : z * 64 + 64]


def edge_first(meta, v_own, v_other, e_own, e_other, h_own, h_other, mats, src, dst, v_all, e_all, hidden, sender, receiver, halo):
    n = v_all.shape[1]
    interleave(meta, v_own, v_other, v_all)
    interleave(meta, e_own, e_other, e_all)
    swapped = meta[3] == 1
    low = lax.broadcasted_iota(jnp.int32, (halo.shape[0], 128), 1) < 64
    for b in range(2):
        blk = slice(128 * b, 128 * b + 128)
        own, other = h_own[:, blk].astype(F32), h_other[:, blk].astype(F32)
        even = jnp.where(swapped, other, own)
        odd = jnp.where(swapped, own, other)
        halo[:, 256 * b : 256 * b + 128] = jnp.where(low, even, pltpu.roll(odd, 64, 1)).astype(BF)
        halo[:, 256 * b + 128 : 256 * b + 256] = jnp.where(low, pltpu.roll(even, 64, 1), odd).astype(BF)
    sender[:, :n] = dot(mats[1], v_all[...]).astype(BF)
    sender[:, n:] = dot(mats[1], halo[...], 1, 1).astype(BF)
    receiver[...] = dot(mats[2], v_all[...]).astype(BF)

    def body(sl, _):
        pre = dot(mats[0], e_all[:, sl])
        pre += dot(sender[...], hot(src[:, sl], 0, sender.shape[1]))
        pre += dot(receiver[...], hot(dst[:, sl], 0, n))
        hidden[:, sl] = silu(pre)

    chunks(hidden.shape[1], body)


def new_edges(hid, hid_other, turned, turned_other, e_all, e_new):
    def edges(sl, _):
        msg = dot(turned[0], hid[:, sl]) + dot(turned_other[0], hid_other[:, sl])
        e_new[:, sl] = norm_add(msg, e_all[:, sl])

    chunks(e_new.shape[1], edges)


def node_message(first, sl, turned, turned_other, nodes, nodes_other, e_new, dst, local):
    agg = dot(e_new[...], hot(dst[...], first, sl.stop - sl.start), 1, 1).astype(BF)
    msg = dot(turned[1], silu(local(0) + dot(nodes[1], agg)))
    return msg + dot(turned_other[1], silu(local(1) + dot(nodes_other[1], agg)))


def node_local(meta, nodes, nodes_other, v_all, out):
    out[0] = dot(nodes[0], v_all[...])
    out[1] = dot(nodes_other[0], v_all[...])


def tail_first(
    meta, hid, hid_other, turned, turned_other, nodes, nodes_other, e_all, v_all, dst, mats_next, send,
    e_out, v_out, rows, e_new, v_new, sender, held, sem,
):
    new_edges(hid, hid_other, turned, turned_other, e_all, e_new)
    copies = [pltpu.make_async_copy(e_new, e_out, sem.at[4])]
    copies[0].start()

    def body(sl, first):
        local = lambda i: dot((nodes, nodes_other)[i][0], v_all[:, sl])
        msg = node_message(first, sl, turned, turned_other, nodes, nodes_other, e_new, dst, local)
        v_new[:, sl] = norm_add(msg, v_all[:, sl])

    chunks(v_new.shape[1], body)
    copies.append(pltpu.make_async_copy(v_new, v_out, sem.at[5]))
    copies[1].start()
    sender[...] = dot(mats_next[1], v_new[...]).astype(BF)
    select_rows(send, sender[...], rows, held, sem)
    for copy in copies:
        copy.wait()


def tail_last(
    meta, hid, hid_other, turned, turned_other, nodes, nodes_other, e_all, v_all, dst, local,
    e_out, v_out, e_new, sums, held, sem,
):
    new_edges(hid, hid_other, turned, turned_other, e_all, e_new)
    mine = pl.ds(pl.multiple_of(meta[4] * 64, 64), 64)
    copies = [pltpu.make_async_copy(e_new.at[mine, :], e_out, sem.at[0])]
    copies[0].start()

    def body(sl, first):
        msg = node_message(first, sl, turned, turned_other, nodes, nodes_other, e_new, dst, lambda i: local[i, :, sl])
        sums[...] = msg
        held[:, sl] = norm_add(msg, v_all[mine, sl], sums[mine, :])
        copies.append(pltpu.make_async_copy(held.at[:, sl], v_out.at[:, sl], sem.at[len(copies)]))
        copies[-1].start()

    chunks(v_out.shape[1], body)
    for copy in copies:
        copy.wait()


def edge_local(meta, v_all, e_all, mats, src, dst, part, sender, receiver):
    n = v_all.shape[1]
    sender[...] = dot(mats[1], v_all[...]).astype(BF)
    receiver[...] = dot(mats[2], v_all[...]).astype(BF)

    def body(sl, _):
        pre = dot(mats[0], e_all[:, sl])
        pre += dot(sender[...], hot(src[:, sl], 0, n))
        part[:, sl] = pre + dot(receiver[...], hot(dst[:, sl], 0, n))

    chunks(part.shape[1], body)


def edge_far(n, meta, part, rows, src, hidden, far):
    far[...] = rows[...].astype(F32).T.astype(BF)

    def body(sl, _):
        hidden[:, sl] = silu(part[:, sl] + dot(far[...], hot(src[:, sl], n, far.shape[1])))

    chunks(hidden.shape[1], body)


def shards(node_feats, edge_feats, send_rows, edge_src, edge_dst, w_edge_in, w_edge_out, w_node_in, w_node_out):
    d = lax.axis_index("dom")
    c = lax.axis_index("ch")
    k = c & 1
    y, x = (d >> 2) & 3, d & 3
    n = node_feats.shape[1]
    m = edge_feats.shape[1]
    first = jnp.where(k == 0, y, x)
    second = jnp.where(k == 0, x, y)
    meta = jnp.stack([c >> 1, first, second, k, c]).astype(jnp.int32)
    send, src, dst = (a.reshape(1, -1) for a in (send_rows, edge_src, edge_dst))

    shared = (jnp.swapaxes(w_edge_in, 2, 3), w_edge_out, jnp.swapaxes(w_node_in, 2, 3), w_node_out, node_feats, edge_feats)
    piece, both = call(
        prepare,
        [((7, 8, LATENT), BF), ((64, n + m), BF)],
        meta, *(pltpu.with_memory_space_constraint(a, pltpu.HBM) for a in shared),
        scratch=[pltpu.SemaphoreType.DMA((6,))], space=HBM,
    )
    pieces = [piece] + [lax.ppermute(piece, "ch", z_shift(s)) for s in (2, 1, 3)]
    both = lax.optimization_barrier((both, pieces[1]))[0]
    wz = jnp.stack(pieces)
    parts = ring_gather(both, "ch", z_shift)
    far, nxt, prev = (lax.ppermute(wz, ("dom", "ch"), ring(1, s)) for s in (2, 3, 1))
    quarters = [wz, nxt, far, prev]
    quarters[0] = lax.optimization_barrier((wz, parts[1], parts[4]))[0]
    one = jnp.stack(quarters)
    w_prev = lax.ppermute(one, ("dom", "ch"), ring(2, 1))
    w_next = lax.ppermute(one, ("dom", "ch"), ring(2, 3))

    v_half, rows = call(
        send_first, [((HALF, n), BF), pltpu.HBM((m, HALF), BF)], meta, *parts, send,
        scratch=[pltpu.VMEM((m, HALF), BF), pltpu.SemaphoreType.DMA((4,))], flops=2 * HALF * n * m,
    )

    def exchange(rows):
        return lax.all_to_all(rows.reshape(32, SLOTS, HALF), "dom", 0, 0, tiled=True).reshape(-1, HALF)

    rows, half_a, half_b = lax.optimization_barrier((rows, w_prev[:2], w_next[2:]))
    halo = exchange(rows)
    far_a = lax.ppermute(half_a, ("dom", "ch"), ring(2, 1))
    far_b = lax.ppermute(half_b, ("dom", "ch"), ring(2, 3))
    w_parts = (one, w_next, far_a, far_b, w_prev)
    v_other = swap(v_half)
    (e_half,) = call(gather_edges, [((HALF, m), BF)], meta, *parts)
    e_other = swap(e_half)
    halo_other = swap(halo)

    mats, tails = [], []
    for layer in range(2):
        w, nodes, turned = call(
            functools.partial(unpack, layer),
            [((3, HALF, LATENT), BF), ((2, HALF, LATENT), BF), ((2, LATENT, HALF), BF)],
            meta, *w_parts, scratch=[pltpu.VMEM((2, HALF, LATENT), BF)], flops=8 * HALF * n * m * (1 - layer),
        )
        mats.append(w)
        tails.append((turned, swap(turned), nodes, swap(nodes)))

    big = lambda r, q: 2 * r * q * LATENT
    v_all, e_all, hid = call(
        edge_first,
        [((LATENT, n), BF), ((LATENT, m), BF), ((HALF, m), BF)],
        meta, v_half, v_other, e_half, e_other, halo, halo_other, mats[0], src, dst,
        scratch=[pltpu.VMEM((HALF, n + m), BF), pltpu.VMEM((HALF, n), BF), pltpu.VMEM((m, LATENT), BF)],
        flops=4 * big(HALF, n + m),
    )
    e_new, v_new, rows = call(
        tail_first,
        [pltpu.HBM((LATENT, m), BF), pltpu.HBM((LATENT, n), BF), pltpu.HBM((m, HALF), BF)],
        meta, hid, swap(hid), *tails[0], e_all, v_all, dst, mats[1], send,
        scratch=[
            pltpu.VMEM((LATENT, m), BF), pltpu.VMEM((LATENT, n), BF), pltpu.VMEM((HALF, n), BF),
            pltpu.VMEM((m, HALF), BF), pltpu.SemaphoreType.DMA((6,)),
        ],
        flops=6 * big(LATENT, m),
    )
    far = exchange(rows)
    (part,) = call(
        edge_local, [((HALF, m), F32)], meta, v_new, e_new, mats[1], src, dst,
        scratch=[pltpu.VMEM((HALF, n), BF)] * 2, flops=3 * big(HALF, m),
    )
    (local,) = call(node_local, [((2, HALF, n), F32)], meta, tails[1][2], tails[1][3], v_new, flops=2 * big(HALF, n))
    (hid,) = call(
        lambda *refs: edge_far(n, *refs), [((HALF, m), BF)], meta, part, far, src,
        scratch=[pltpu.VMEM((HALF, m), BF)], flops=2 * big(HALF, m),
    )
    e_out, v_out = call(
        tail_last,
        [pltpu.HBM((64, m), BF), pltpu.HBM((64, n), BF)],
        meta, hid, swap(hid), *tails[1], e_new, v_new, dst, local,
        scratch=[pltpu.VMEM((LATENT, m), BF), pltpu.VMEM((LATENT, n // 2), F32), pltpu.VMEM((64, n), BF), pltpu.SemaphoreType.DMA((3,))], flops=5 * big(LATENT, m),
    )
    return v_out, e_out


def solution(mesh):
    in_specs = (
        P("ch", "dom"),
        P("ch", "dom"),
        P("dom"),
        P("dom"),
        P("dom"),
        P(None, None, None, "ch"),
        P(None, "ch", None),
        P(None, None, None, "ch"),
        P(None, "ch", None),
    )
    out_specs = (P("ch", "dom"), P("ch", "dom"))
    return jax.shard_map(shards, mesh=mesh, in_specs=in_specs, out_specs=out_specs, check_vma=False)
```
